32 devices in a mesh: dp: 2 (over y), fsdp: 4 (over x, core), tensor: 4 (over z).
Axes of the slice: x: 2, y: 2, z: 4, core: 2. Of those that a mesh axis runs over, the one named last changes fastest.
Arguments:
- activations: bfloat16 [1024, 8192], P(('dp', 'fsdp'), 'tensor'), may hold values from -6 to 6
- cotangent: bfloat16 [1024, 8192], P(('dp', 'fsdp'), 'tensor'), may hold values from -6 to 6
- up_tiles: bfloat16 [1024, 128, 128], P(('fsdp', 'tensor')), may hold values from -0.1875 to 0.1875
- down_tiles: bfloat16 [1024, 128, 128], P(('fsdp', 'tensor')), may hold values from -0.125 to 0.125
- up_rows: int32 [256, 4], P(None, 'tensor'), may hold values from 0 to 63, as said below
- up_cols: int32 [256, 4], P(None, 'tensor'), may hold values from 0 to 31, as said below
- down_rows: int32 [256, 4], P(None, 'tensor'), may hold values from 0 to 31, as said below
- down_cols: int32 [256, 4], P(None, 'tensor'), may hold values from 0 to 63, as said below
Outputs:
- output: bfloat16 [1024, 8192], P(('dp', 'fsdp'), 'tensor')
- input_grad: bfloat16 [1024, 8192], P(('dp', 'fsdp'), 'tensor')
- up_grad: float32 [1024, 128, 128], P(('fsdp', 'tensor'))
- down_grad: float32 [1024, 128, 128], P(('fsdp', 'tensor'))
The draws below stay inside these ranges and needn't reach their ends.
Inputs may be any that keep to these rules, and one draw needn't show every extreme that they name: `up_rows`: within a column, the up tiles of one hidden-unit block name distinct feature blocks. `up_cols`: every value occurs exactly 8 times in each column. `down_rows`: every value occurs exactly 8 times in each column. `down_cols`: within a column, the down tiles of one hidden-unit block name distinct feature blocks.
All inputs are finite; a program needn't handle non-finite values.
Results may differ from the reference program's by a relative error of at most 0.018.
Values may be sent and summed in bfloat16 or wider, within the bound.
A program may use at most 128 MiB of HBM per device.

```python
import jax
import jax.numpy as jnp
from jax import lax

D = 8192
FF = 16384
BLOCK = 128
TOK_DEV = 128
TOKENS = 1024
RANK_COLS = 32
COL_TILES = 8
RANK_TILES = 256
TILES = 1024
TILE_DEV = 64
N_FSDP = 4
N_TENSOR = 4


def tile_lists(key):
    model_blocks = D // BLOCK
    ranks_here = TILES // RANK_TILES

    def one_block(block_key, top_here, bottom_here):
        order = jax.random.permutation(block_key, model_blocks).astype(jnp.int32)
        spots = jnp.arange(model_blocks, dtype=jnp.int32)
        top_spot = jnp.sum(jnp.where(order == model_blocks - 1, spots, 0))
        moved = order.at[top_spot].set(order[0]).at[0].set(model_blocks - 1)
        order = jnp.where(top_here, moved, order)
        low_spot = jnp.sum(jnp.where(order == 0, spots, 0))
        moved = order.at[low_spot].set(order[1]).at[1].set(0)
        order = jnp.where(bottom_here, moved, order)
        return order[:COL_TILES]

    def one_rank(rank_key):
        order_key, block_key, pick_key = jax.random.split(rank_key, 3)
        chosen = jax.random.randint(pick_key, (2,), 0, RANK_COLS)
        blocks = jnp.arange(RANK_COLS, dtype=jnp.int32)
        block_keys = jax.random.split(block_key, RANK_COLS)
        table = jax.vmap(one_block)(block_keys, blocks == chosen[0], blocks == chosen[1])
        slots = jax.random.permutation(order_key, RANK_TILES).astype(jnp.int32)
        near_blocks = slots // COL_TILES
        far_blocks = table[near_blocks, slots % COL_TILES]
        return (far_blocks, near_blocks)
    keys = jax.random.split(key, ranks_here)
    far_blocks, near_blocks = jax.vmap(one_rank)(keys)
    return (far_blocks.T.astype(jnp.int32), near_blocks.T.astype(jnp.int32))


def draw_up_rows(key, part):
    return tile_lists(jax.random.fold_in(key, 11))[0]


def draw_up_cols(key, part):
    return tile_lists(jax.random.fold_in(key, 11))[1]


def draw_down_rows(key, part):
    return tile_lists(jax.random.fold_in(key, 12))[1]


def draw_down_cols(key, part):
    return tile_lists(jax.random.fold_in(key, 12))[0]


def block_levels(rng, extent, shards, low, top_value):
    def one(dim, shards_of):
        draws = jax.random.uniform(jax.random.fold_in(jax.random.fold_in(rng, 6), dim), (shards_of,), jnp.float32, low / len(shards), top_value / len(shards))
        return jnp.repeat(jnp.exp(draws), extent[dim] // shards_of).reshape((-1,) + (1,) * (len(extent) - dim - 1))

    level = one(*shards[0])
    for cut in shards[1:]:
        level = level * one(*cut)
    return level


def normal_values(rng, shape, scale, most, cuts=(), kind=jnp.bfloat16):
    values = scale * jax.random.normal(rng, shape, jnp.float32)
    if cuts:
        values = values * block_levels(rng, shape, cuts, -0.22, 0.18)
    return jnp.clip(values, -most, most).astype(kind)


def setup_inputs(seed: int = 0) -> dict:
    streams_of = jax.random.split(jax.random.key(seed), 9)
    activations = normal_values(streams_of[0], (TOKENS, D), 1.0, 6.0, ((0, 8), (1, 4)))
    cotangent = normal_values(streams_of[1], (TOKENS, D), 1.0, 6.0, ((0, 8), (1, 4)))
    up_tiles = normal_values(streams_of[2], (TILES, BLOCK, BLOCK), (D // 8) ** -0.5, 0.1875, ((0, 16),))
    down_tiles = normal_values(streams_of[3], (TILES, BLOCK, BLOCK), (FF // 8) ** -0.5, 0.125, ((0, 16),))
    up_rows = draw_up_rows(jax.random.fold_in(streams_of[8], 71), 0)
    up_cols = draw_up_cols(jax.random.fold_in(streams_of[8], 71), 0)
    down_rows = draw_down_rows(jax.random.fold_in(streams_of[8], 71), 0)
    down_cols = draw_down_cols(jax.random.fold_in(streams_of[8], 71), 0)
    return {"activations": activations, "cotangent": cotangent, "up_tiles": up_tiles, "down_tiles": down_tiles, "up_rows": up_rows, "up_cols": up_cols, "down_rows": down_rows, "down_cols": down_cols}


inv_root_two = 0.7071067811865476
inv_root_tau = 0.3989422804014327


def gelu_parts(values):
    normal_cdf = 0.5 * (1.0 + jax.scipy.special.erf(values * inv_root_two))
    density = inv_root_tau * jnp.exp(-0.5 * values * values)
    return values * normal_cdf, normal_cdf + values * density


def rank_order(tiles):
    shaped = tiles.reshape(N_FSDP, N_TENSOR, TILE_DEV, BLOCK, BLOCK)
    return shaped.transpose(1, 0, 2, 3, 4).reshape(TILES, BLOCK, BLOCK)


def tile_order(grads):
    shaped = grads.reshape(N_TENSOR, N_FSDP, TILE_DEV, BLOCK, BLOCK)
    return shaped.transpose(1, 0, 2, 3, 4).reshape(TILES, BLOCK, BLOCK)


def apply_tiles(acting, tiles, source, target, segments, letters):
    picked = acting.reshape(TOK_DEV, -1, BLOCK)[:, source].astype(jnp.float32)
    product = jnp.einsum(letters, picked, tiles)
    summed = jnp.zeros((TOK_DEV, segments, BLOCK), jnp.float32).at[:, target].add(product)
    return summed.reshape(TOK_DEV, segments * BLOCK)


def rank_total(partial_value):
    shaped = partial_value.reshape(TOK_DEV, N_TENSOR, D)
    rounded = lax.optimization_barrier(shaped.astype(jnp.bfloat16)).astype(jnp.float32)
    return jnp.sum(rounded, axis=1).astype(jnp.bfloat16)


def outer_tiles(left_side, right_side, left_index, right_index):
    left_pick = left_side.reshape(TOK_DEV, -1, BLOCK)[:, left_index].astype(jnp.float32)
    right_pick = right_side.reshape(TOK_DEV, -1, BLOCK)[:, right_index].astype(jnp.float32)
    term = jnp.einsum("tnb,tnc->nbc", left_pick, right_pick)
    return lax.optimization_barrier(term.astype(jnp.bfloat16)).astype(jnp.float32)


def reference(activations, cotangent, up_tiles, down_tiles, up_rows, up_cols, down_rows, down_cols):
    ranks = jnp.repeat(jnp.arange(N_TENSOR, dtype=jnp.int32), RANK_TILES)
    model_blocks = D // BLOCK
    up_far = up_rows.T.reshape(-1).astype(jnp.int32)
    up_near = ranks * RANK_COLS + up_cols.T.reshape(-1).astype(jnp.int32)
    down_near = ranks * RANK_COLS + down_rows.T.reshape(-1).astype(jnp.int32)
    down_far = down_cols.T.reshape(-1).astype(jnp.int32)
    up_wide = ranks * model_blocks + up_far
    down_wide = ranks * model_blocks + down_far
    up_float = rank_order(up_tiles).astype(jnp.float32)
    down_float = rank_order(down_tiles).astype(jnp.float32)
    groups = TOKENS // TOK_DEV

    def step(carry, blocks_in):
        input_block, cot_block = blocks_in
        pre_act = apply_tiles(input_block, up_float, up_far, up_near, FF // BLOCK, "tnb,nbc->tnc")
        gelu_out, gelu_slope = gelu_parts(pre_act)
        hidden = gelu_out.astype(jnp.bfloat16)
        output = rank_total(apply_tiles(hidden, down_float, down_near, down_wide, N_TENSOR * model_blocks, "tnb,nbc->tnc"))
        hidden_grad = apply_tiles(cot_block, down_float, down_far, down_near, FF // BLOCK, "tnb,ncb->tnc")
        pre_grad = (hidden_grad * gelu_slope).astype(jnp.bfloat16)
        input_grad = rank_total(apply_tiles(pre_grad, up_float, up_near, up_wide, N_TENSOR * model_blocks, "tnb,ncb->tnc"))
        up_term = outer_tiles(input_block, pre_grad, up_far, up_near)
        down_term = outer_tiles(hidden, cot_block, down_near, down_far)
        return (carry[0] + up_term, carry[1] + down_term), (output, input_grad)

    zeros = jnp.zeros((TILES, BLOCK, BLOCK), jnp.float32)
    inputs_split = activations.reshape(groups, TOK_DEV, D)
    cot_split = cotangent.reshape(groups, TOK_DEV, D)
    sums, results = lax.scan(step, (zeros, zeros), (inputs_split, cot_split))
    output = results[0].reshape(TOKENS, D)
    input_grad = results[1].reshape(TOKENS, D)
    return (output, input_grad, tile_order(sums[0]), tile_order(sums[1]))
```

```python
import functools

import jax
import jax.numpy as jnp
from jax import lax
from jax.experimental import pallas as pl
from jax.experimental.pallas import tpu as pltpu
from jax.sharding import PartitionSpec as P

MESH = pl.DeviceIdType.MESH
COL_TILES = 8
PIECES = 16
CHUNKS = 2
WEIGHT_CHUNKS = 4
PARTS = 4

SHARD_TIME = 11.3
PIECE_TIME = 2.8
WEIGHT_TIME = 5.6

inv_root_two = 0.7071067811865476
inv_root_tau = 0.3989422804014327


def gelu_parts(values):
    normal_cdf = 0.5 * (1.0 + lax.erf(values * inv_root_two))
    density = inv_root_tau * jnp.exp(-0.5 * values * values)
    return (values * normal_cdf, normal_cdf + values * density)


def mm(a, b, ca, cb):
    return lax.dot_general(a, b, (((ca,), (cb,)), ((), ())), preferred_element_type=jnp.float32)


def wide(blocks, axis):
    return jnp.concatenate(blocks, axis=axis)


def remote(src, dst, send_sem, recv_sem, where):
    return pltpu.make_async_remote_copy(
        src_ref=src, dst_ref=dst, send_sem=send_sem, recv_sem=recv_sem,
        device_id=where, device_id_type=MESH,
    )


def place(sizes):
    n, chips, replicas = sizes
    z = lax.axis_index("tensor")
    f = lax.axis_index("fsdp")
    y = lax.axis_index("dp")
    return z, f // 2, f % 2, y


def enter(sizes):
    n, chips, replicas = sizes
    z, r, c, y = place(sizes)
    barrier = pltpu.get_barrier_semaphore()

    def greet(where):
        pl.semaphore_signal(barrier, inc=1, device_id=where, device_id_type=MESH)

    @pl.when(z < n - 1)
    def _():
        greet({"tensor": z + 1})

    @pl.when(z > 0)
    def _():
        greet({"tensor": z - 1})

    greet({"fsdp": r * 2 + 1 - c})
    for d in range(1, chips):
        greet({"fsdp": lax.rem(r + d, chips) * 2 + c})
    for e in range(1, replicas):
        greet({"dp": lax.rem(y + e, replicas)})
    sides = jnp.where(z < n - 1, 1, 0) + jnp.where(z > 0, 1, 0)
    pl.semaphore_wait(barrier, sides + 1 + (chips - 1) + (replicas - 1))


def block_kernel(
    sizes, uo, uf, do, df, up_rows, up_cols, down_rows, down_cols,
    pair_order_u, pair_near_u, pair_first_u, last_u, pair_order_d, pair_near_d, pair_first_d, last_d,
    act, cot, up, down,
    out, inp, ga_u, ga_d, gb_u, gb_d,
    x_all, xt_own, xt_mate, cot_own, cot_mate, u_all, d_all, hidden, ht_own, ht_mate, slope,
    pg_own, pg_mate, run, acc, parts_o, parts_i, held_r, held_l, stage, x_in,
    load_sem, zs_sem, zr_sem, ms_sem, mr_sem, ts_sem, tr_sem, ws_sem, wr_sem, ys_sem, yr_sem, cs_sem, cr_sem,
    os_sem, or_sem, hs_sem, hr_sem, gs_sem, gr_sem, ls_sem, lr_sem, xs_sem, xr_sem, es_sem, er_sem, keep_sem,
):
    n, chips, replicas = sizes
    z, r, c, y = place(sizes)
    f = r * 2 + c
    blocks = act.shape[1] // 128
    per = up.shape[0]
    part = per // replicas
    total_tiles = u_all.shape[0]
    hidden_blocks = slope.shape[0]
    chunk = blocks // CHUNKS
    weight_chunks = min(WEIGHT_CHUNKS, part)
    weight_size = part // weight_chunks
    pieces = min(PIECES, per)
    size = per // pieces
    span = hidden_blocks // PARTS
    features = (x_all, cot_own)
    weights = ((up, u_all), (down, d_all))
    mate = {"fsdp": r * 2 + 1 - c}

    loads = ([], [])
    for a, (src, full) in enumerate(((act, x_all), (cot, cot_own))):
        for b in range(blocks):
            copy = pltpu.make_async_copy(
                src.at[:, pl.ds(b * 128, 128)], full.at[z * blocks + b], load_sem.at[a, b]
            )
            copy.start()
            loads[a].append(copy)
    weight_loads = []
    for a, (src, full) in enumerate(weights):
        copy = pltpu.make_async_copy(src, full.at[pl.ds(f * per, per)], load_sem.at[2 + a, 0])
        copy.start()
        weight_loads.append(copy)
    hidden[hidden_blocks] = jnp.zeros(hidden.shape[1:], hidden.dtype)
    pg_own[hidden_blocks] = jnp.zeros(pg_own.shape[1:], pg_own.dtype)
    enter(sizes)

    def shard(full, s, k):
        return full.at[pl.ds(s * blocks + k * chunk, chunk)]

    def line(a, s, k, way):
        piece = shard(features[a], z - way * s, k)
        w = 0 if way > 0 else 1
        return remote(
            piece, piece, zs_sem.at[a, w, s, k], zr_sem.at[a, w, s, k], {"tensor": z + way}
        )

    def can_send(way):
        return z < n - 1 if way > 0 else z > 0

    def has(s, way):
        return z - s >= 0 if way > 0 else z + s <= n - 1

    def z_start(a):
        for k in range(CHUNKS):
            for way in (1, -1):

                @pl.when(can_send(way))
                def _():
                    line(a, 0, k, way).start()

    def mate_chunk(a, s, k, way):
        w = 0 if way > 0 else 1
        src, dst = ((xt_own, xt_mate), (cot_own, cot_mate))[a]
        sems = ((ts_sem, tr_sem), (ms_sem, mr_sem))[a]
        return remote(
            shard(src, z - way * s, k), shard(dst, z - way * s, k),
            sems[0].at[w, s, k], sems[1].at[w, s, k], mate,
        )

    def turn(s, k, way):
        first = (z - way * s) * blocks + k * chunk

        @pl.loop(0, chunk)
        def _(b):
            xt_own[first + b] = x_all[first + b].T

        mate_chunk(0, s, k, way).start()

    def z_event(a, s, k):
        for way in (1, -1):

            @pl.when(has(s, way))
            def _():
                line(a, s - 1, k, way).wait_recv()
                if s < n - 1:

                    @pl.when(can_send(way))
                    def _():
                        line(a, s, k, way).start()

                if a == 1:
                    mate_chunk(1, s, k, way).start()

    def turn_event(s, k):
        for way in (1, -1):

            @pl.when(has(s, way))
            def _():
                turn(s, k, way)

    def mate_chunks(a, act_on):
        for k in range(CHUNKS):
            act_on(mate_chunk(a, 0, k, 1))
            for s in range(1, n):
                for way in (1, -1):

                    @pl.when(has(s, way))
                    def _():
                        act_on(mate_chunk(a, s, k, way))

    def tile_range(full, r_of, q, k):
        return full.at[pl.ds((r_of * 2 + c) * per + q * part + k * weight_size, weight_size)]

    def from_chip(d):
        return lax.rem(r - d + chips, chips)

    def w_copy(a, d, k):
        src = weights[a][0].at[pl.ds(y * part + k * weight_size, weight_size)]
        return remote(
            src, tile_range(weights[a][1], r, y, k), ws_sem.at[a, d, k], wr_sem.at[a, d, k],
            {"fsdp": lax.rem(r + d, chips) * 2 + c},
        )

    def y_copy(a, d, e, k):
        piece = tile_range(weights[a][1], from_chip(d), y, k)
        return remote(
            piece, piece, ys_sem.at[a, d, e, k], yr_sem.at[a, d, e, k],
            {"dp": lax.rem(y + e, replicas)},
        )

    def core_copy(a, d, e, k):
        piece = tile_range(weights[a][1], from_chip(d), lax.rem(y - e + replicas, replicas), k)
        return remote(piece, piece, cs_sem.at[a, d, e, k], cr_sem.at[a, d, e, k], mate)

    def own_core(a):
        return remote(
            weights[a][0], weights[a][1].at[pl.ds(f * per, per)], os_sem.at[a], or_sem.at[a], mate
        )

    def w_event(a, k):
        for d in range(1, chips):
            w_copy(a, d, k).wait_recv()
            for e in range(1, replicas):
                y_copy(a, d, e, k).start()
            core_copy(a, d, 0, k).start()

    def y_event(a, k):
        for d in range(1, chips):
            for e in range(1, replicas):
                y_copy(a, d, e, k).wait_recv()
                core_copy(a, d, e, k).start()

    def weights_in(a):
        weight_loads[a].wait()
        own_core(a).wait_recv()
        for d in range(1, chips):
            for e in range(replicas):
                for k in range(weight_chunks):
                    core_copy(a, d, e, k).wait_recv()

    def hidden_mate(g):
        at = pl.ds(g * span, span)
        return remote(ht_own.at[at], ht_mate.at[at], hs_sem.at[g], hr_sem.at[g], mate)

    def hidden_part(g):
        @pl.loop(g * span, (g + 1) * span)
        def _(h):
            spots = [h * COL_TILES + k for k in range(COL_TILES)]
            pre = mm(
                wide([x_all[uf[i]] for i in spots], 1), wide([u_all[uo[i]] for i in spots], 0), 1, 0
            )
            value, tangent = gelu_parts(pre)
            value = value.astype(jnp.bfloat16)
            hidden[h] = value
            ht_own[h] = value.T
            slope[h] = tangent

        hidden_mate(g).start()

    def grad_mate(g):
        at = pl.ds(g * span, span)
        return remote(pg_own.at[at], pg_mate.at[at], gs_sem.at[g], gr_sem.at[g], mate)

    def slope_part(g):
        @pl.loop(g * span, (g + 1) * span)
        def _(h):
            spots = [h * COL_TILES + k for k in range(COL_TILES)]
            value = mm(
                wide([cot_own[df[i]] for i in spots], 1), wide([d_all[do[i]] for i in spots], 1), 1, 1
            )
            pg_own[h] = (value * slope[h]).astype(jnp.bfloat16)

        grad_mate(g).start()

    parts = (parts_o, parts_i)
    outs = (out, inp)
    held = (held_r, held_l)
    pair_width = 4

    def run_part(a, g):
        order, near, fresh = (
            (pair_order_d, pair_near_d, pair_first_d) if a == 0 else (pair_order_u, pair_near_u, pair_first_u)
        )
        left, right, cut = (hidden, d_all, 0) if a == 0 else (pg_own, u_all, 1)
        steps = run.shape[0] // PARTS // pair_width
        if g == 0:
            acc[...] = jnp.zeros_like(acc)

        @pl.loop(g * steps, (g + 1) * steps)
        def _(b):
            total = acc[...]
            for i in [b * pair_width + k for k in range(pair_width)]:
                product = mm(
                    wide([left[near[2 * i]], left[near[2 * i + 1]]], 1),
                    wide([right[order[2 * i]], right[order[2 * i + 1]]], cut), 1, cut,
                )
                total = jnp.where(fresh[i] == 1, 0.0, total) + product
                run[i] = total.astype(jnp.bfloat16)
            acc[...] = total

    def part_shard(ref, s):
        return ref.at[pl.ds(s * blocks, blocks)]

    def fold(a, i, way, source):
        s = n - 1 - i if way > 0 else i
        k = 0 if way > 0 else 1
        src = part_shard(parts[a], s) if source else held[k].at[a, i]
        return remote(
            src, held[k].at[a, i], ls_sem.at[a, k, i], lr_sem.at[a, k, i], {"tensor": z + way}
        )

    def edge(way):
        return z == 0 if way > 0 else z == n - 1

    def sends(i, way):
        return n - 1 - i > z if way > 0 else i < z

    def settle(a):
        last = last_d if a == 0 else last_u
        target = parts[a]

        @pl.loop(0, target.shape[0])
        def _(b):
            spot = last[b]
            found = run[jnp.maximum(spot, 0)]
            target[b] = jnp.where(spot >= 0, found, jnp.zeros_like(found))

        for i in range(n - 1):
            for way in (1, -1):

                @pl.when(edge(way))
                def _():
                    fold(a, i, way, True).start()

    def add_into(target, terms):
        @pl.loop(0, target.shape[0])
        def _(b):
            total = terms[0][b].astype(jnp.float32)
            for term_of in terms[1:]:
                total += term_of[b].astype(jnp.float32)
            target[b] = total.astype(target.dtype)

    def fold_event(a, t):
        for way in (1, -1):
            i = t - z if way > 0 else t - (n - 1 - z)
            s = n - 1 - i if way > 0 else i
            k = 0 if way > 0 else 1
            on_way = jnp.logical_and(i >= 0, sends(i, way))

            @pl.when(jnp.logical_and(on_way, jnp.logical_not(edge(way))))
            def _():
                fold(a, i, way, False).wait_recv()
                add_into(held[k].at[a, i], (held[k].at[a, i], part_shard(parts[a], s)))
                fold(a, i, way, False).start()

    def finish(a):
        mine = part_shard(parts[a], z)
        target = outs[a]

        def write(terms):
            for b in range(blocks):
                total = terms[0][b].astype(jnp.float32)
                for term_of in terms[1:]:
                    total += term_of[b].astype(jnp.float32)
                target[:, pl.ds(b * 128, 128)] = total.astype(target.dtype)

        @pl.when(z > 0)
        def _():
            fold(a, n - 1 - z, 1, False).wait_recv()

        @pl.when(z < n - 1)
        def _():
            fold(a, z, -1, False).wait_recv()

        @pl.when(z == 0)
        def _():
            write((mine, held_l.at[a, z]))

        @pl.when(z == n - 1)
        def _():
            write((mine, held_r.at[a, n - 1 - z]))

        @pl.when(jnp.logical_and(z > 0, z < n - 1))
        def _():
            write((mine, held_r.at[a, n - 1 - z], held_l.at[a, z]))

    sums = (ga_d, ga_u)
    others = (gb_d, gb_u)

    def term(a, j):
        if a == 0:
            at, to = down_rows[j], down_cols[j]
            return mm(wide([ht_own[at], ht_mate[at]], 1), wide([cot_own[to], cot_mate[to]], 0), 1, 0)
        at, to = up_rows[j], up_cols[j]
        return mm(wide([xt_own[at], xt_mate[at]], 1), wide([pg_own[to], pg_mate[to]], 0), 1, 0)

    def first_tile(q, k):
        return (q * 2 + c) * per + k * size

    def x_copy(a, k, d):
        q = lax.rem(r + d, chips)
        at = pl.ds(k * size, size)
        return remote(
            stage.at[a, d - 1, at], x_in.at[a, d - 1, at], xs_sem.at[a, k, d], xr_sem.at[a, k, d],
            {"fsdp": q * 2 + c},
        )

    def hand_over(a):
        @pl.loop(0, pieces)
        def _(k):
            for d in range(1, chips):
                first = first_tile(lax.rem(r + d, chips), k)
                values = [term(a, first + i) for i in range(size)]
                for i in range(size):
                    stage[a, d - 1, k * size + i] = values[i].astype(jnp.bfloat16)
                x_copy(a, k, d).start()

    def done_piece(a, k):
        return x_in.at[a, 0, pl.ds(k * size, size)]

    def e_copy(a, k, e):
        return remote(
            done_piece(a, k), others[a].at[e - 1, pl.ds(k * size, size)],
            es_sem.at[a, k, e], er_sem.at[a, k, e], {"dp": lax.rem(y + e, replicas)},
        )

    def keep_copy(a, k):
        return pltpu.make_async_copy(
            done_piece(a, k), sums[a].at[pl.ds(k * size, size)], keep_sem.at[a, k]
        )

    def x_event(a, k):
        first = first_tile(r, k)
        values = [term(a, first + i) for i in range(size)]
        for d in range(1, chips):
            x_copy(a, k, d).wait_recv()
        for i in range(size):
            total = values[i]
            for d in range(1, chips):
                total += x_in[a, d - 1, k * size + i].astype(jnp.float32)
            x_in[a, 0, k * size + i] = total.astype(jnp.bfloat16)
        for e in range(1, replicas):
            e_copy(a, k, e).start()
        keep_copy(a, k).start()

    plan = []

    def at(time, work, *args):
        plan.append((time, functools.partial(work, *args)))

    def start_all():
        for copy in loads[0]:
            copy.wait()
        z_start(0)
        for a in range(2):
            for k in range(weight_chunks):
                for d in range(1, chips):
                    w_copy(a, d, k).start()
        for a in range(2):
            own_core(a).start()
        for k in range(CHUNKS):
            turn(0, k, 1)
        for copy in loads[1]:
            copy.wait()
        for k in range(CHUNKS):
            mate_chunk(1, 0, k, 1).start()

    at(0.0, start_all)
    chunk_time = SHARD_TIME / CHUNKS
    for s in range(1, n):
        for k in range(CHUNKS):
            when = 2.0 + ((s - 1) * CHUNKS + k + 1) * chunk_time
            at(when, z_event, 0, s, k)
            at(when + 0.1, turn_event, s, k)
    act_in = 2.0 + (n - 1) * SHARD_TIME
    at(2.05 + max(n - 2, 0) * SHARD_TIME, z_start, 1)
    for a in range(2):
        for k in range(weight_chunks):
            when = 2.2 + (a * weight_chunks + k + 1) * WEIGHT_TIME
            at(when, w_event, a, k)
            at(when + 1.2 * WEIGHT_TIME, y_event, a, k)
    up_in = 2.3 + (weight_chunks + 1.2) * WEIGHT_TIME
    down_in = 2.3 + (2 * weight_chunks + 1.2) * WEIGHT_TIME
    at(up_in + 2.0, weights_in, 0)
    at(down_in + 2.0, weights_in, 1)
    hidden_from = max(act_in, up_in + 2.0) + 0.5
    for g in range(PARTS):
        at(hidden_from + 3.0 * g, hidden_part, g)
    out_from = max(hidden_from + 3.0 * PARTS, down_in + 2.0) + 0.5
    for g in range(PARTS):
        at(out_from + 2.0 * g, run_part, 0, g)
    out_settle = out_from + 2.0 * PARTS
    at(out_settle, settle, 0)
    for s in range(1, n):
        for k in range(CHUNKS):
            at(act_in + ((s - 1) * CHUNKS + k + 1) * chunk_time, z_event, 1, s, k)
    cot_in = max(act_in + (n - 1) * SHARD_TIME, out_settle) + 1.0

    def cot_ready():
        mate_chunks(1, lambda copy: copy.wait_recv())
        for g in range(PARTS):
            hidden_mate(g).wait_recv()

    at(cot_in, cot_ready)
    at(cot_in + 0.1, hand_over, 0)
    slope_from = cot_in + 7.0
    for g in range(PARTS):
        at(slope_from + 2.5 * g, slope_part, g)

    def grads_ready():
        mate_chunks(0, lambda copy: copy.wait_recv())
        for g in range(PARTS):
            grad_mate(g).wait_recv()

    up_from = slope_from + 2.5 * PARTS
    at(up_from, grads_ready)
    at(up_from + 0.1, hand_over, 1)
    inp_from = up_from + 7.0
    for g in range(PARTS):
        at(inp_from + 2.0 * g, run_part, 1, g)
    inp_settle = inp_from + 2.0 * PARTS
    at(inp_settle, settle, 1)
    for a, start in enumerate((out_settle, inp_settle)):
        for t in range(1, n - 1):
            at(start + 1.0 + t * SHARD_TIME, fold_event, a, t)
        at(start + 3.0 + (n - 1) * SHARD_TIME, finish, a)
    for a in range(2):
        for k in range(pieces):
            when = cot_in + 4.0 + PIECE_TIME * (a * pieces + k + 1)
            at(max(when, up_from + 0.2) if a else when, x_event, a, k)

    plan.sort(key=lambda item: item[0])
    for _, work in plan:
        work()

    for a in range(2):
        mate_chunks(a, lambda copy: copy.wait_send())
        own_core(a).wait_send()
        for d in range(1, chips):
            for k in range(weight_chunks):
                w_copy(a, d, k).wait_send()
                for e in range(replicas):
                    core_copy(a, d, e, k).wait_send()
                for e in range(1, replicas):
                    y_copy(a, d, e, k).wait_send()
        for way in (1, -1):
            for s in range(n - 1):

                @pl.when(jnp.logical_and(can_send(way), has(s, way)))
                def _():
                    for k in range(CHUNKS):
                        line(a, s, k, way).wait_send()

        for i in range(n - 1):
            for way in (1, -1):

                @pl.when(sends(i, way))
                def _():
                    fold(a, i, way, False).wait_send()

    for g in range(PARTS):
        hidden_mate(g).wait_send()
        grad_mate(g).wait_send()
    for a in range(2):

        @pl.loop(0, pieces)
        def _(k):
            for d in range(1, chips):
                x_copy(a, k, d).wait_send()
            keep_copy(a, k).wait()
            for e in range(1, replicas):
                e_copy(a, k, e).wait()


def run_block(sizes, tables, activations, cotangent, up_tiles, down_tiles):
    n, chips, replicas = sizes
    rows, features = activations.shape
    blocks = features // 128
    per = up_tiles.shape[0]
    total_tiles = 2 * chips * per
    hidden_blocks = total_tiles // COL_TILES
    model_blocks = n * blocks
    pairs = (total_tiles + model_blocks) // 2
    part = per // replicas
    weight_chunks = min(WEIGHT_CHUNKS, part)
    pieces = min(PIECES, per)
    kind = jnp.bfloat16
    dma = pltpu.SemaphoreType.DMA
    vmem = pl.BlockSpec(memory_space=pltpu.VMEM)
    smem = pl.BlockSpec(memory_space=pltpu.SMEM)
    anywhere = pl.BlockSpec(memory_space=pl.ANY)

    def held(*shape):
        return pltpu.VMEM(shape + (rows, 128), kind)

    def twice(*shape):
        return [dma(shape), dma(shape)]

    return pl.pallas_call(
        functools.partial(block_kernel, sizes),
        out_shape=(
            [jax.ShapeDtypeStruct((rows, features), kind)] * 2
            + [jax.ShapeDtypeStruct((per, 128, 128), kind)] * 2
            + [jax.ShapeDtypeStruct((replicas - 1, per, 128, 128), kind)] * 2
        ),
        in_specs=[smem] * len(tables) + [anywhere] * 4,
        out_specs=[vmem] * 2 + [anywhere] * 4,
        scratch_shapes=[
            held(model_blocks),
            pltpu.VMEM((model_blocks, 128, rows), kind),
            pltpu.VMEM((model_blocks, 128, rows), kind),
            held(model_blocks),
            held(model_blocks),
            pltpu.VMEM((total_tiles, 128, 128), kind),
            pltpu.VMEM((total_tiles, 128, 128), kind),
            held(hidden_blocks + 1),
            pltpu.VMEM((hidden_blocks, 128, rows), kind),
            pltpu.VMEM((hidden_blocks, 128, rows), kind),
            pltpu.VMEM((hidden_blocks, rows, 128), jnp.float32),
            held(hidden_blocks + 1),
            held(hidden_blocks),
            held(pairs),
            pltpu.VMEM((rows, 128), jnp.float32),
            held(model_blocks),
            held(model_blocks),
            held(2, n - 1, blocks),
            held(2, n - 1, blocks),
            pltpu.VMEM((2, chips - 1, per, 128, 128), kind),
            pltpu.VMEM((2, chips - 1, per, 128, 128), kind),
            dma((4, blocks)),
            *twice(2, 2, n, CHUNKS),
            *twice(2, n, CHUNKS),
            *twice(2, n, CHUNKS),
            *twice(2, chips, weight_chunks),
            *twice(2, chips, replicas, weight_chunks),
            *twice(2, chips, replicas, weight_chunks),
            *twice(2),
            *twice(PARTS),
            *twice(PARTS),
            *twice(2, 2, n),
            *twice(2, pieces, chips),
            *twice(2, pieces, replicas),
            dma((2, pieces)),
        ],
        compiler_params=pltpu.CompilerParams(
            collective_id=0, has_side_effects=True, vmem_limit_bytes=67043328
        ),
        name="block_all",
    )(*tables, activations, cotangent, up_tiles, down_tiles)


def total_kernel(ga_u, gb_u, ga_d, gb_d, up_grad, down_grad):
    for one, more, target in ((ga_u, gb_u, up_grad), (ga_d, gb_d, down_grad)):
        total = one[...].astype(jnp.float32)
        for e in range(more.shape[0]):
            total += more[e].astype(jnp.float32)
        target[...] = total


def totals(ga_u, gb_u, ga_d, gb_d):
    per = ga_u.shape[0]
    step = min(8, per)
    one = pl.BlockSpec((step, 128, 128), lambda i: (i, 0, 0))
    more = pl.BlockSpec((gb_u.shape[0], step, 128, 128), lambda i: (0, i, 0, 0))
    return pl.pallas_call(
        total_kernel,
        grid=(per // step,),
        out_shape=[jax.ShapeDtypeStruct(ga_u.shape, jnp.float32)] * 2,
        in_specs=[one, more, one, more],
        out_specs=[one, one],
        name="totals",
    )(ga_u, gb_u, ga_d, gb_d)


def tables_of(near, far, model_blocks):
    count = near.shape[0]
    near_size = count // COL_TILES + 1
    at = lax.iota(jnp.int32, count)
    before = at[:, None] < at[None, :]
    equal = far[:, None] == far[None, :]
    spot = near * COL_TILES + jnp.sum(((near[:, None] == near[None, :]) & before).astype(jnp.int32), axis=0)
    here = spot[:, None] == at[None, :]
    packed = jnp.sum(jnp.where(here, (at * model_blocks + far)[:, None], 0), axis=0)
    rank = jnp.sum((equal & before).astype(jnp.int32), axis=0)
    often = jnp.sum(equal.astype(jnp.int32), axis=0)
    takes = 1 + jnp.where((rank == often - 1) & (often % 2 == 1), 1, 0)
    place_of = rank + jnp.sum(jnp.where(far[:, None] < far[None, :], takes[:, None], 0), axis=0)
    there = place_of[:, None] == lax.iota(jnp.int32, count + model_blocks)[None, :]
    code = ((at * near_size + near) * 2 + (rank == 0)) - (near_size - 1) * 2
    pair_code = jnp.sum(jnp.where(there, code[:, None], 0), axis=0) + (near_size - 1) * 2
    block = lax.iota(jnp.int32, model_blocks)
    matches = far[:, None] == block[None, :]
    until = jnp.sum(jnp.where(far[:, None] <= block[None, :], takes[:, None], 0), axis=0)
    last = jnp.where(jnp.any(matches, axis=0), until // 2 - 1, -1)
    pair_far = pair_code // 2
    return (
        packed // model_blocks, packed % model_blocks,
        pair_far // near_size, pair_far % near_size, (pair_code % 2)[::2], last,
    )


def body(sizes, activations, cotangent, up_tiles, down_tiles, up_rows, up_cols, down_rows, down_cols):
    ur, uc, dr, dc = (v[:, 0] for v in (up_rows, up_cols, down_rows, down_cols))
    model_blocks = sizes[0] * activations.shape[1] // 128
    sort = jax.vmap(functools.partial(tables_of, model_blocks=model_blocks))
    order, far, *pair = sort(jnp.stack([uc, dr]), jnp.stack([ur, dc]))
    tables = (
        order[0], far[0], order[1], far[1], ur, uc, dr, dc,
        *(v[0] for v in pair), *(v[1] for v in pair),
    )
    out, inp, ga_u, ga_d, gb_u, gb_d = run_block(
        sizes, tables, activations, cotangent, up_tiles, down_tiles
    )
    up_grad, down_grad = totals(ga_u, gb_u, ga_d, gb_d)
    return out, inp, up_grad, down_grad


def solution(mesh):
    sizes = (mesh.shape["tensor"], mesh.shape["fsdp"] // 2, mesh.shape["dp"])
    in_specs = (
        P(("dp", "fsdp"), "tensor"),
        P(("dp", "fsdp"), "tensor"),
        P(("fsdp", "tensor"), None, None),
        P(("fsdp", "tensor"), None, None),
        P(None, "tensor"),
        P(None, "tensor"),
        P(None, "tensor"),
        P(None, "tensor"),
    )
    out_specs = (
        P(("dp", "fsdp"), "tensor"),
        P(("dp", "fsdp"), "tensor"),
        P(("fsdp", "tensor"), None, None),
        P(("fsdp", "tensor"), None, None),
    )
    return jax.shard_map(
        functools.partial(body, sizes), mesh=mesh, in_specs=in_specs, out_specs=out_specs,
        check_vma=False,
    )
```

```python
import functools

import jax
import jax.numpy as jnp
from jax import lax
from jax.experimental import pallas as pl
from jax.experimental.pallas import tpu as pltpu
from jax.sharding import PartitionSpec as P

MESH = pl.DeviceIdType.MESH
COL_TILES = 8
PIECES = 32
CHUNKS = 4
WEIGHT_CHUNKS = 4
PARTS = 8
LANES = 128

SHARD_TIME = 11.3
WEIGHT_TIME = 5.6
PIECE_SHARE = 2

inv_root_two = 0.7071067811865476
inv_root_tau = 0.3989422804014327


def gelu_parts(values):
    normal_cdf = 0.5 * (1.0 + lax.erf(values * inv_root_two))
    density = inv_root_tau * jnp.exp(-0.5 * values * values)
    return (values * normal_cdf, normal_cdf + values * density)


def mm(a, b, ca, cb):
    return lax.dot_general(a, b, (((ca,), (cb,)), ((), ())), preferred_element_type=jnp.float32)


def wide(blocks, axis):
    return jnp.concatenate(blocks, axis=axis)


def remote(src, dst, send_sem, recv_sem, where):
    return pltpu.make_async_remote_copy(
        src_ref=src, dst_ref=dst, send_sem=send_sem, recv_sem=recv_sem,
        device_id=where, device_id_type=MESH,
    )


def place(sizes):
    n, chips, replicas = sizes
    z = lax.axis_index("tensor")
    f = lax.axis_index("fsdp")
    y = lax.axis_index("dp")
    return z, f // 2, f % 2, y


def enter(sizes):
    n, chips, replicas = sizes
    z, r, c, y = place(sizes)
    barrier = pltpu.get_barrier_semaphore()

    def greet(where):
        pl.semaphore_signal(barrier, inc=1, device_id=where, device_id_type=MESH)

    @pl.when(z < n - 1)
    def _():
        greet({"tensor": z + 1})

    @pl.when(z > 0)
    def _():
        greet({"tensor": z - 1})

    greet({"fsdp": r * 2 + 1 - c})
    for d in range(1, chips):
        greet({"fsdp": lax.rem(r + d, chips) * 2 + c})
    for e in range(1, replicas):
        greet({"dp": lax.rem(y + e, replicas)})
    sides = jnp.where(z < n - 1, 1, 0) + jnp.where(z > 0, 1, 0)
    pl.semaphore_wait(barrier, sides + 1 + (chips - 1) + (replicas - 1))


def padded(size):
    return -(-size // LANES) * LANES


def tables_of(near, far, model_blocks):
    count = near.shape[1]
    near_size = count // COL_TILES + 1
    spare = (near_size - 1) * 2
    wide_count = padded(count + model_blocks)

    def along(size, axis, rows=count):
        return lax.broadcasted_iota(jnp.int32, (rows, size), axis)

    def total(picked, values, axis):
        return jnp.sum(jnp.where(picked, values, 0), axis=axis, keepdims=True)

    down, over = along(count, 0), along(count, 1)
    same = down == over
    before = over < down
    at = along(1, 0)
    near_c, far_c = total(same, near, 1), total(same, far, 1)
    spot = near_c * COL_TILES + total((near == near_c) & before, 1, 1)
    packed = total(spot == over, at * model_blocks + far_c, 0)
    equal = far == far_c
    rank = total(equal & before, 1, 1)
    often = total(equal, 1, 1)
    takes = jnp.where((rank == often - 1) & (often % 2 == 1), 2, 1)
    place_of = rank + total(far < far_c, total(same, takes, 0), 1)
    code = (at * near_size + near_c) * 2 + jnp.where(rank == 0, 1, 0) - spare
    pair_code = total(place_of == along(wide_count, 1), code, 0) + spare
    block = along(padded(model_blocks), 1)
    until = total(far_c <= block, takes, 0)
    last = jnp.where(total(far_c == block, 1, 0) > 0, until // 2 - 1, -1)
    pair_far = pair_code // 2
    return (
        packed // model_blocks, packed % model_blocks,
        pair_far // near_size, pair_far % near_size, pair_code % 2, last,
    )


def block_kernel(
    sizes, up_rows, up_cols, down_rows, down_cols, ur, uc, dr, dc,
    act, cot, up, down,
    out, inp, ga_u, ga_d, gb_u, gb_d,
    x_all, xt_own, xt_mate, cot_own, cot_mate, u_all, d_all, hidden, ht_own, ht_mate, slope,
    pg_own, pg_mate, run, acc, parts_o, parts_i, held_r, held_l, stage, x_in, made, tables,
    load_sem, zs_sem, zr_sem, ms_sem, mr_sem, ts_sem, tr_sem, ws_sem, wr_sem, ys_sem, yr_sem, cs_sem, cr_sem,
    os_sem, or_sem, hs_sem, hr_sem, gs_sem, gr_sem, ls_sem, lr_sem, xs_sem, xr_sem, es_sem, er_sem, keep_sem, table_sem,
):
    n, chips, replicas = sizes
    z, r, c, y = place(sizes)
    f = r * 2 + c
    blocks = act.shape[1] // 128
    per = up.shape[0]
    part = per // replicas
    total_tiles = u_all.shape[0]
    hidden_blocks = slope.shape[0]
    chunk = blocks // CHUNKS
    weight_chunks = min(WEIGHT_CHUNKS, part)
    weight_size = part // weight_chunks
    pieces = min(PIECES, per)
    size = per // pieces
    span = hidden_blocks // PARTS
    features = (x_all, cot_own)
    weights = ((up, u_all), (down, d_all))
    mate = {"fsdp": r * 2 + 1 - c}

    loads = ([], [])
    for a, (src, full) in enumerate(((act, x_all), (cot, cot_own))):
        for b in range(blocks):
            copy = pltpu.make_async_copy(
                src.at[:, pl.ds(b * 128, 128)], full.at[z * blocks + b], load_sem.at[a, b]
            )
            copy.start()
            loads[a].append(copy)
    weight_loads = []
    for a, (src, full) in enumerate(weights):
        copy = pltpu.make_async_copy(src, full.at[pl.ds(f * per, per)], load_sem.at[2 + a, 0])
        copy.start()
        weight_loads.append(copy)
    hidden[hidden_blocks] = jnp.zeros(hidden.shape[1:], hidden.dtype)
    pg_own[hidden_blocks] = jnp.zeros(pg_own.shape[1:], pg_own.dtype)
    enter(sizes)

    def shard(full, s, k):
        return full.at[pl.ds(s * blocks + k * chunk, chunk)]

    def line(a, s, k, way):
        piece = shard(features[a], z - way * s, k)
        w = 0 if way > 0 else 1
        return remote(
            piece, piece, zs_sem.at[a, w, s, k], zr_sem.at[a, w, s, k], {"tensor": z + way}
        )

    def can_send(way):
        return z < n - 1 if way > 0 else z > 0

    def has(s, way):
        return z - s >= 0 if way > 0 else z + s <= n - 1

    def z_start(a):
        for k in range(CHUNKS):
            for way in (1, -1):

                @pl.when(can_send(way))
                def _():
                    line(a, 0, k, way).start()

    def mate_chunk(a, s, k, way):
        w = 0 if way > 0 else 1
        src, dst = ((xt_own, xt_mate), (cot_own, cot_mate))[a]
        sems = ((ts_sem, tr_sem), (ms_sem, mr_sem))[a]
        return remote(
            shard(src, z - way * s, k), shard(dst, z - way * s, k),
            sems[0].at[w, s, k], sems[1].at[w, s, k], mate,
        )

    def turn(s, k, way):
        first = (z - way * s) * blocks + k * chunk

        @pl.loop(0, chunk)
        def _(b):
            xt_own[first + b] = x_all[first + b].T

        mate_chunk(0, s, k, way).start()

    def z_event(a, s, k):
        for way in (1, -1):

            @pl.when(has(s, way))
            def _():
                line(a, s - 1, k, way).wait_recv()
                if s < n - 1:

                    @pl.when(can_send(way))
                    def _():
                        line(a, s, k, way).start()

                if a == 1:
                    mate_chunk(1, s, k, way).start()

    def turn_event(s, k):
        for way in (1, -1):

            @pl.when(has(s, way))
            def _():
                turn(s, k, way)

    def mate_chunks(a, act_on):
        for k in range(CHUNKS):
            act_on(mate_chunk(a, 0, k, 1))
            for s in range(1, n):
                for way in (1, -1):

                    @pl.when(has(s, way))
                    def _():
                        act_on(mate_chunk(a, s, k, way))

    def tile_range(full, r_of, q, k):
        return full.at[pl.ds((r_of * 2 + c) * per + q * part + k * weight_size, weight_size)]

    def from_chip(d):
        return lax.rem(r - d + chips, chips)

    def w_copy(a, d, k):
        src = weights[a][0].at[pl.ds(y * part + k * weight_size, weight_size)]
        return remote(
            src, tile_range(weights[a][1], r, y, k), ws_sem.at[a, d, k], wr_sem.at[a, d, k],
            {"fsdp": lax.rem(r + d, chips) * 2 + c},
        )

    def y_copy(a, d, e, k):
        piece = tile_range(weights[a][1], from_chip(d), y, k)
        return remote(
            piece, piece, ys_sem.at[a, d, e, k], yr_sem.at[a, d, e, k],
            {"dp": lax.rem(y + e, replicas)},
        )

    def core_copy(a, d, e, k):
        piece = tile_range(weights[a][1], from_chip(d), lax.rem(y - e + replicas, replicas), k)
        return remote(piece, piece, cs_sem.at[a, d, e, k], cr_sem.at[a, d, e, k], mate)

    def own_core(a):
        return remote(
            weights[a][0], weights[a][1].at[pl.ds(f * per, per)], os_sem.at[a], or_sem.at[a], mate
        )

    def w_event(a, k):
        for d in range(1, chips):
            w_copy(a, d, k).wait_recv()
            for e in range(1, replicas):
                y_copy(a, d, e, k).start()
            core_copy(a, d, 0, k).start()

    def y_event(a, k):
        for d in range(1, chips):
            for e in range(1, replicas):
                y_copy(a, d, e, k).wait_recv()
                core_copy(a, d, e, k).start()

    def weights_in(a):
        weight_loads[a].wait()
        own_core(a).wait_recv()
        for d in range(1, chips):
            for e in range(replicas):
                for k in range(weight_chunks):
                    core_copy(a, d, e, k).wait_recv()

    def hidden_mate(g):
        at = pl.ds(g * span, span)
        return remote(ht_own.at[at], ht_mate.at[at], hs_sem.at[g], hr_sem.at[g], mate)

    def hidden_part(g):
        @pl.loop(g * span, (g + 1) * span)
        def _(h):
            spots = [h * COL_TILES + k for k in range(COL_TILES)]
            pre = mm(
                wide([x_all[tables[0, 1, i]] for i in spots], 1),
                wide([u_all[tables[0, 0, i]] for i in spots], 0), 1, 0,
            )
            value, tangent = gelu_parts(pre)
            value = value.astype(jnp.bfloat16)
            hidden[h] = value
            ht_own[h] = value.T
            slope[h] = tangent

        hidden_mate(g).start()

    def grad_mate(g):
        at = pl.ds(g * span, span)
        return remote(pg_own.at[at], pg_mate.at[at], gs_sem.at[g], gr_sem.at[g], mate)

    def slope_part(g):
        @pl.loop(g * span, (g + 1) * span)
        def _(h):
            spots = [h * COL_TILES + k for k in range(COL_TILES)]
            value = mm(
                wide([cot_own[tables[1, 1, i]] for i in spots], 1),
                wide([d_all[tables[1, 0, i]] for i in spots], 1), 1, 1,
            )
            pg_own[h] = (value * slope[h]).astype(jnp.bfloat16)

        grad_mate(g).start()

    parts = (parts_o, parts_i)
    outs = (out, inp)
    held = (held_r, held_l)
    pair_width = 4

    def run_part(a, g):
        t = 1 - a
        left, right, cut = (hidden, d_all, 0) if a == 0 else (pg_own, u_all, 1)
        steps = run.shape[0] // PARTS // pair_width
        if g == 0:
            acc[...] = jnp.zeros_like(acc)

        @pl.loop(g * steps, (g + 1) * steps)
        def _(b):
            total = acc[...]
            for i in [b * pair_width + k for k in range(pair_width)]:
                product = mm(
                    wide([left[tables[t, 3, 2 * i]], left[tables[t, 3, 2 * i + 1]]], 1),
                    wide([right[tables[t, 2, 2 * i]], right[tables[t, 2, 2 * i + 1]]], cut), 1, cut,
                )
                total = jnp.where(tables[t, 4, 2 * i] == 1, 0.0, total) + product
                run[i] = total.astype(jnp.bfloat16)
            acc[...] = total

    def part_shard(ref, s):
        return ref.at[pl.ds(s * blocks, blocks)]

    def fold(a, i, way, source):
        s = n - 1 - i if way > 0 else i
        k = 0 if way > 0 else 1
        src = part_shard(parts[a], s) if source else held[k].at[a, i]
        return remote(
            src, held[k].at[a, i], ls_sem.at[a, k, i], lr_sem.at[a, k, i], {"tensor": z + way}
        )

    def edge(way):
        return z == 0 if way > 0 else z == n - 1

    def sends(i, way):
        return n - 1 - i > z if way > 0 else i < z

    def settle(a):
        target = parts[a]

        @pl.loop(0, target.shape[0])
        def _(b):
            spot = tables[1 - a, 5, b]
            found = run[jnp.maximum(spot, 0)]
            target[b] = jnp.where(spot >= 0, found, jnp.zeros_like(found))

        for i in range(n - 1):
            for way in (1, -1):

                @pl.when(edge(way))
                def _():
                    fold(a, i, way, True).start()

    def add_into(target, terms):
        @pl.loop(0, target.shape[0])
        def _(b):
            total = terms[0][b].astype(jnp.float32)
            for term_of in terms[1:]:
                total += term_of[b].astype(jnp.float32)
            target[b] = total.astype(target.dtype)

    def fold_event(a, t):
        for way in (1, -1):
            i = t - z if way > 0 else t - (n - 1 - z)
            s = n - 1 - i if way > 0 else i
            k = 0 if way > 0 else 1
            on_way = jnp.logical_and(i >= 0, sends(i, way))

            @pl.when(jnp.logical_and(on_way, jnp.logical_not(edge(way))))
            def _():
                fold(a, i, way, False).wait_recv()
                add_into(held[k].at[a, i], (held[k].at[a, i], part_shard(parts[a], s)))
                fold(a, i, way, False).start()

    def finish(a):
        mine = part_shard(parts[a], z)
        target = outs[a]

        def write(terms):
            for b in range(blocks):
                total = terms[0][b].astype(jnp.float32)
                for term_of in terms[1:]:
                    total += term_of[b].astype(jnp.float32)
                target[:, pl.ds(b * 128, 128)] = total.astype(target.dtype)

        @pl.when(z > 0)
        def _():
            fold(a, n - 1 - z, 1, False).wait_recv()

        @pl.when(z < n - 1)
        def _():
            fold(a, z, -1, False).wait_recv()

        @pl.when(z == 0)
        def _():
            write((mine, held_l.at[a, z]))

        @pl.when(z == n - 1)
        def _():
            write((mine, held_r.at[a, n - 1 - z]))

        @pl.when(jnp.logical_and(z > 0, z < n - 1))
        def _():
            write((mine, held_r.at[a, n - 1 - z], held_l.at[a, z]))

    sums = (ga_d, ga_u)
    others = (gb_d, gb_u)

    def term(a, j):
        if a == 0:
            at, to = down_rows[j], down_cols[j]
            return mm(wide([ht_own[at], ht_mate[at]], 1), wide([cot_own[to], cot_mate[to]], 0), 1, 0)
        at, to = up_rows[j], up_cols[j]
        return mm(wide([xt_own[at], xt_mate[at]], 1), wide([pg_own[to], pg_mate[to]], 0), 1, 0)

    def first_tile(q, k):
        return (q * 2 + c) * per + k * size

    def x_copy(a, k, d):
        q = lax.rem(r + d, chips)
        at = pl.ds(k * size, size)
        return remote(
            stage.at[a, d - 1, at], x_in.at[a, d - 1, at], xs_sem.at[a, k, d], xr_sem.at[a, k, d],
            {"fsdp": q * 2 + c},
        )

    def hand_over(a, first_piece, end):
        @pl.loop(first_piece, end)
        def _(k):
            for d in range(1, chips):
                first = first_tile(lax.rem(r + d, chips), k)
                values = [term(a, first + i) for i in range(size)]
                for i in range(size):
                    stage[a, d - 1, k * size + i] = values[i].astype(jnp.bfloat16)
                x_copy(a, k, d).start()

    def done_piece(a, k):
        return x_in.at[a, 0, pl.ds(k * size, size)]

    def e_copy(a, k, e):
        return remote(
            done_piece(a, k), others[a].at[e - 1, pl.ds(k * size, size)],
            es_sem.at[a, k, e], er_sem.at[a, k, e], {"dp": lax.rem(y + e, replicas)},
        )

    def keep_copy(a, k):
        return pltpu.make_async_copy(
            done_piece(a, k), sums[a].at[pl.ds(k * size, size)], keep_sem.at[a, k]
        )

    def x_event(a, k):
        first = first_tile(r, k)
        values = [term(a, first + i) for i in range(size)]
        for d in range(1, chips):
            x_copy(a, k, d).wait_recv()
        for i in range(size):
            total = values[i]
            for d in range(1, chips):
                total += x_in[a, d - 1, k * size + i].astype(jnp.float32)
            x_in[a, 0, k * size + i] = total.astype(jnp.bfloat16)
        for e in range(1, replicas):
            e_copy(a, k, e).start()
        keep_copy(a, k).start()

    plan = []

    def at(time, work, *args):
        plan.append((time, functools.partial(work, *args)))

    def start_all():
        for copy in loads[0]:
            copy.wait()
        z_start(0)
        for a in range(2):
            for k in range(weight_chunks):
                for d in range(1, chips):
                    w_copy(a, d, k).start()
        for a in range(2):
            own_core(a).start()
        for copy in loads[1]:
            copy.wait()
        for k in range(CHUNKS):
            mate_chunk(1, 0, k, 1).start()
        for t, (near, far) in enumerate(((uc, ur), (dr, dc))):
            for row, values in enumerate(tables_of(near[...], far[...], n * blocks)):
                made[t, pl.ds(row, 1), pl.ds(0, values.shape[1])] = values
        pltpu.make_async_copy(made, tables, table_sem).start()
        for k in range(CHUNKS):
            turn(0, k, 1)
        pltpu.make_async_copy(made, tables, table_sem).wait()

    at(0.0, start_all)
    chunk_time = SHARD_TIME / CHUNKS
    for s in range(1, n):
        for k in range(CHUNKS):
            when = 2.0 + ((s - 1) * CHUNKS + k + 1) * chunk_time
            at(when, z_event, 0, s, k)
            at(when + 0.1, turn_event, s, k)
    act_in = 2.0 + (n - 1) * SHARD_TIME
    at(2.05 + max(n - 2, 0) * SHARD_TIME, z_start, 1)
    for a in range(2):
        for k in range(weight_chunks):
            when = 2.2 + (a * weight_chunks + k + 1) * WEIGHT_TIME
            at(when, w_event, a, k)
            at(when + 1.2 * WEIGHT_TIME, y_event, a, k)
    up_in = 2.3 + (weight_chunks + 1.2) * WEIGHT_TIME
    down_in = 2.3 + (2 * weight_chunks + 1.2) * WEIGHT_TIME
    at(up_in + 2.0, weights_in, 0)
    at(down_in + 2.0, weights_in, 1)
    hidden_from = max(act_in, up_in + 2.0) + 0.5
    for g in range(PARTS):
        at(hidden_from + 1.5 * g, hidden_part, g)
    out_from = max(hidden_from + 1.5 * PARTS, down_in + 2.0) + 0.5
    for g in range(PARTS):
        at(out_from + 1.2 * g, run_part, 0, g)
    out_settle = out_from + 1.2 * PARTS
    at(out_settle, settle, 0)
    for s in range(1, n):
        for k in range(CHUNKS):
            at(act_in + ((s - 1) * CHUNKS + k + 1) * chunk_time, z_event, 1, s, k)
    cot_in = max(act_in + (n - 1) * SHARD_TIME, out_settle) + 1.0

    def cot_ready():
        mate_chunks(1, lambda copy: copy.wait_recv())
        for g in range(PARTS):
            hidden_mate(g).wait_recv()

    at(cot_in, cot_ready)
    piece_time = 2 * SHARD_TIME * PIECE_SHARE / pieces
    group = max(pieces // 8, 1)
    at(cot_in + 0.1, hand_over, 0, 0, group)
    for k in range(group, pieces, group):
        at(cot_in + 0.2 + 1.2 * (k // group), hand_over, 0, k, min(k + group, pieces))
    slope_from = cot_in + 9.0
    for g in range(PARTS):
        at(slope_from + 1.5 * g, slope_part, g)

    def grads_ready():
        mate_chunks(0, lambda copy: copy.wait_recv())
        for g in range(PARTS):
            grad_mate(g).wait_recv()

    up_from = slope_from + 1.5 * PARTS + 1.0
    at(up_from, grads_ready)
    for k in range(0, pieces, group):
        at(up_from + 0.1 + 1.4 * (k // group), hand_over, 1, k, min(k + group, pieces))
    inp_from = up_from + 0.1 + 1.4 * 8
    for g in range(PARTS):
        at(inp_from + 1.5 * g, run_part, 1, g)
    inp_settle = inp_from + 1.5 * PARTS
    at(inp_settle, settle, 1)
    for a, start in enumerate((out_settle, inp_settle)):
        for t in range(1, n - 1):
            at(start + 1.0 + t * SHARD_TIME, fold_event, a, t)
        at(start + 3.0 + (n - 1) * SHARD_TIME, finish, a)
    for a in range(2):
        for k in range(pieces):
            when = cot_in + 2.2 + piece_time * (a * pieces + k + 1)
            at(max(when, up_from + 0.2) if a else when, x_event, a, k)

    plan.sort(key=lambda item: item[0])
    for _, work in plan:
        work()

    for a in range(2):
        mate_chunks(a, lambda copy: copy.wait_send())
        own_core(a).wait_send()
        for d in range(1, chips):
            for k in range(weight_chunks):
                w_copy(a, d, k).wait_send()
                for e in range(replicas):
                    core_copy(a, d, e, k).wait_send()
                for e in range(1, replicas):
                    y_copy(a, d, e, k).wait_send()
        for way in (1, -1):
            for s in range(n - 1):

                @pl.when(jnp.logical_and(can_send(way), has(s, way)))
                def _():
                    for k in range(CHUNKS):
                        line(a, s, k, way).wait_send()

        for i in range(n - 1):
            for way in (1, -1):

                @pl.when(sends(i, way))
                def _():
                    fold(a, i, way, False).wait_send()

    for g in range(PARTS):
        hidden_mate(g).wait_send()
        grad_mate(g).wait_send()
    for a in range(2):

        @pl.loop(0, pieces)
        def _(k):
            for d in range(1, chips):
                x_copy(a, k, d).wait_send()
            keep_copy(a, k).wait()
            for e in range(1, replicas):
                e_copy(a, k, e).wait()


def run_block(sizes, lists, activations, cotangent, up_tiles, down_tiles):
    n, chips, replicas = sizes
    rows, features = activations.shape
    blocks = features // 128
    per = up_tiles.shape[0]
    total_tiles = 2 * chips * per
    hidden_blocks = total_tiles // COL_TILES
    model_blocks = n * blocks
    pairs = (total_tiles + model_blocks) // 2
    part = per // replicas
    weight_chunks = min(WEIGHT_CHUNKS, part)
    pieces = min(PIECES, per)
    kind = jnp.bfloat16
    dma = pltpu.SemaphoreType.DMA
    vmem = pl.BlockSpec(memory_space=pltpu.VMEM)
    smem = pl.BlockSpec(memory_space=pltpu.SMEM)
    anywhere = pl.BlockSpec(memory_space=pl.ANY)

    def held(*shape):
        return pltpu.VMEM(shape + (rows, 128), kind)

    def twice(*shape):
        return [dma(shape), dma(shape)]

    return pl.pallas_call(
        functools.partial(block_kernel, sizes),
        out_shape=(
            [jax.ShapeDtypeStruct((rows, features), kind)] * 2
            + [jax.ShapeDtypeStruct((per, 128, 128), kind)] * 2
            + [jax.ShapeDtypeStruct((replicas - 1, per, 128, 128), kind)] * 2
        ),
        in_specs=[smem] * 4 + [vmem] * 4 + [anywhere] * 4,
        out_specs=[vmem] * 2 + [anywhere] * 4,
        scratch_shapes=[
            held(model_blocks),
            pltpu.VMEM((model_blocks, 128, rows), kind),
            pltpu.VMEM((model_blocks, 128, rows), kind),
            held(model_blocks),
            held(model_blocks),
            pltpu.VMEM((total_tiles, 128, 128), kind),
            pltpu.VMEM((total_tiles, 128, 128), kind),
            held(hidden_blocks + 1),
            pltpu.VMEM((hidden_blocks, 128, rows), kind),
            pltpu.VMEM((hidden_blocks, 128, rows), kind),
            pltpu.VMEM((hidden_blocks, rows, 128), jnp.float32),
            held(hidden_blocks + 1),
            held(hidden_blocks),
            held(pairs),
            pltpu.VMEM((rows, 128), jnp.float32),
            held(model_blocks),
            held(model_blocks),
            held(2, n - 1, blocks),
            held(2, n - 1, blocks),
            pltpu.VMEM((2, chips - 1, per, 128, 128), kind),
            pltpu.VMEM((2, chips - 1, per, 128, 128), kind),
            pltpu.VMEM((2, 8, padded(total_tiles + model_blocks)), jnp.int32),
            pltpu.SMEM((2, 8, padded(total_tiles + model_blocks)), jnp.int32),
            dma((4, blocks)),
            *twice(2, 2, n, CHUNKS),
            *twice(2, n, CHUNKS),
            *twice(2, n, CHUNKS),
            *twice(2, chips, weight_chunks),
            *twice(2, chips, replicas, weight_chunks),
            *twice(2, chips, replicas, weight_chunks),
            *twice(2),
            *twice(PARTS),
            *twice(PARTS),
            *twice(2, 2, n),
            *twice(2, pieces, chips),
            *twice(2, pieces, replicas),
            dma((2, pieces)),
            dma,
        ],
        compiler_params=pltpu.CompilerParams(
            collective_id=0, has_side_effects=True, vmem_limit_bytes=67043328
        ),
        name="block_all",
    )(*(v[:, 0] for v in lists), *(v.T for v in lists), activations, cotangent, up_tiles, down_tiles)


def total_kernel(ga_u, gb_u, ga_d, gb_d, up_grad, down_grad):
    for one, more, target in ((ga_u, gb_u, up_grad), (ga_d, gb_d, down_grad)):
        total = one[...].astype(jnp.float32)
        for e in range(more.shape[0]):
            total += more[e].astype(jnp.float32)
        target[...] = total


def totals(ga_u, gb_u, ga_d, gb_d):
    per = ga_u.shape[0]
    step = max(per // 2, 1)
    one = pl.BlockSpec((step, 128, 128), lambda i: (i, 0, 0))
    more = pl.BlockSpec((gb_u.shape[0], step, 128, 128), lambda i: (0, i, 0, 0))
    return pl.pallas_call(
        total_kernel,
        grid=(per // step,),
        out_shape=[jax.ShapeDtypeStruct(ga_u.shape, jnp.float32)] * 2,
        in_specs=[one, more, one, more],
        out_specs=[one, one],
        name="totals",
    )(ga_u, gb_u, ga_d, gb_d)


def body(sizes, activations, cotangent, up_tiles, down_tiles, up_rows, up_cols, down_rows, down_cols):
    lists = (up_rows, up_cols, down_rows, down_cols)
    out, inp, ga_u, ga_d, gb_u, gb_d = run_block(
        sizes, lists, activations, cotangent, up_tiles, down_tiles
    )
    up_grad, down_grad = totals(ga_u, gb_u, ga_d, gb_d)
    return out, inp, up_grad, down_grad


def solution(mesh):
    sizes = (mesh.shape["tensor"], mesh.shape["fsdp"] // 2, mesh.shape["dp"])
    in_specs = (
        P(("dp", "fsdp"), "tensor"),
        P(("dp", "fsdp"), "tensor"),
        P(("fsdp", "tensor"), None, None),
        P(("fsdp", "tensor"), None, None),
        P(None, "tensor"),
        P(None, "tensor"),
        P(None, "tensor"),
        P(None, "tensor"),
    )
    out_specs = (
        P(("dp", "fsdp"), "tensor"),
        P(("dp", "fsdp"), "tensor"),
        P(("fsdp", "tensor"), None, None),
        P(("fsdp", "tensor"), None, None),
    )
    return jax.shard_map(
        functools.partial(body, sizes), mesh=mesh, in_specs=in_specs, out_specs=out_specs,
        check_vma=False,
    )
```

```python
import functools

import jax
import jax.numpy as jnp
from jax import lax
from jax.experimental import pallas as pl
from jax.experimental.pallas import tpu as pltpu
from jax.sharding import PartitionSpec as P

MESH = pl.DeviceIdType.MESH
COL_TILES = 8
PIECES = 32
CHUNKS = 4
WEIGHT_CHUNKS = 4
PARTS = 8
HIDDEN_PARTS = 4
LANES = 128

SHARD_TIME = 11.3
WEIGHT_TIME = 5.6
PIECE_SHARE = 2

inv_root_two = 0.7071067811865476
inv_root_tau = 0.3989422804014327


def gelu_parts(values):
    normal_cdf = 0.5 * (1.0 + lax.erf(values * inv_root_two))
    density = inv_root_tau * jnp.exp(-0.5 * values * values)
    return (values * normal_cdf, normal_cdf + values * density)


def mm(a, b, ca, cb):
    return lax.dot_general(a, b, (((ca,), (cb,)), ((), ())), preferred_element_type=jnp.float32)


def wide(blocks, axis):
    return jnp.concatenate(blocks, axis=axis)


def remote(src, dst, send_sem, recv_sem, where):
    return pltpu.make_async_remote_copy(
        src_ref=src, dst_ref=dst, send_sem=send_sem, recv_sem=recv_sem,
        device_id=where, device_id_type=MESH,
    )


def place(sizes):
    n, chips, replicas = sizes
    z = lax.axis_index("tensor")
    f = lax.axis_index("fsdp")
    y = lax.axis_index("dp")
    return z, f // 2, f % 2, y


def enter(sizes):
    n, chips, replicas = sizes
    z, r, c, y = place(sizes)
    barrier = pltpu.get_barrier_semaphore()

    def greet(where):
        pl.semaphore_signal(barrier, inc=1, device_id=where, device_id_type=MESH)

    @pl.when(z < n - 1)
    def _():
        greet({"tensor": z + 1})

    @pl.when(z > 0)
    def _():
        greet({"tensor": z - 1})

    greet({"fsdp": r * 2 + 1 - c})
    for d in range(1, chips):
        greet({"fsdp": lax.rem(r + d, chips) * 2 + c})
    for e in range(1, replicas):
        greet({"dp": lax.rem(y + e, replicas)})
    sides = jnp.where(z < n - 1, 1, 0) + jnp.where(z > 0, 1, 0)
    pl.semaphore_wait(barrier, sides + 1 + (chips - 1) + (replicas - 1))


def padded(size):
    return -(-size // LANES) * LANES


def tables_of(near, far, model_blocks):
    count = near.shape[1]
    near_size = count // COL_TILES + 1
    spare = (near_size - 1) * 2
    wide_count = padded(count + model_blocks)

    def along(size, axis):
        return lax.broadcasted_iota(jnp.int32, (count, size), axis)

    def column(row, size):
        turned = jnp.broadcast_to(row, (LANES, count)).T
        return wide([turned] * (size // LANES), 1)

    def total(picked, values):
        return jnp.sum(jnp.where(picked, values, 0), axis=0, keepdims=True)

    at, over, over_wide = along(count, 0), along(count, 1), along(wide_count, 1)
    before = at < over
    near_c, far_c = column(near, wide_count), column(far, wide_count)
    near_n, far_n = near_c[:, :count], far_c[:, :count]
    spot = near * COL_TILES + total((near_n == near) & before, 1)
    packed = total(column(spot, count) == over, at * model_blocks + far_n)
    equal = far_n == far
    rank = total(equal & before, 1)
    often = total(equal, 1)
    takes = jnp.where((rank == often - 1) & (often % 2 == 1), 2, 1)
    takes_c = column(takes, count)
    place_of = rank + total(far_n < far, takes_c)
    place_c = column(place_of * 2 + jnp.where(rank == 0, 1, 0), wide_count)
    code = (along(wide_count, 0) * near_size + near_c) * 2 + place_c % 2 - spare
    pair_code = total(place_c // 2 == over_wide, code) + spare
    ends = padded(model_blocks)
    block = along(ends, 1)
    until = total(far_c[:, :ends] <= block, takes_c[:, :ends])
    last = jnp.where(total(far_c[:, :ends] == block, 1) > 0, until // 2 - 1, -1)
    pair_far = pair_code // 2
    return (
        packed // model_blocks, packed % model_blocks,
        pair_far // near_size, pair_far % near_size, pair_code % 2, last,
    )


def block_kernel(
    sizes, up_rows, up_cols, down_rows, down_cols, ur, uc, dr, dc,
    act, cot, up, down,
    out, inp, ga_u, ga_d, gb_u, gb_d,
    x_all, xt_own, xt_mate, cot_own, cot_mate, u_all, d_all, hidden, ht_own, ht_mate, slope,
    pg_own, pg_mate, run, acc, parts_o, parts_i, held_r, held_l, stage, x_in, made, tables,
    load_sem, zs_sem, zr_sem, ms_sem, mr_sem, ts_sem, tr_sem, ws_sem, wr_sem, ys_sem, yr_sem, cs_sem, cr_sem,
    os_sem, or_sem, hs_sem, hr_sem, gs_sem, gr_sem, ls_sem, lr_sem, xs_sem, xr_sem, es_sem, er_sem, keep_sem, table_sem,
):
    n, chips, replicas = sizes
    z, r, c, y = place(sizes)
    f = r * 2 + c
    blocks = act.shape[1] // 128
    per = up.shape[0]
    part = per // replicas
    total_tiles = u_all.shape[0]
    hidden_blocks = slope.shape[0]
    chunk = blocks // CHUNKS
    weight_chunks = min(WEIGHT_CHUNKS, part)
    weight_size = part // weight_chunks
    pieces = min(PIECES, per)
    size = per // pieces
    span = hidden_blocks // PARTS
    hidden_span = hidden_blocks // HIDDEN_PARTS
    features = (x_all, cot_own)
    weights = ((up, u_all), (down, d_all))
    mate = {"fsdp": r * 2 + 1 - c}

    loads = []
    for a, (src, full) in enumerate(((act, x_all), (cot, cot_own))):
        for b in range(blocks):
            pltpu.make_async_copy(
                src.at[:, pl.ds(b * 128, 128)], full.at[z * blocks + b], load_sem.at[a]
            ).start()
        own = full.at[pl.ds(z * blocks, blocks)]
        loads.append(pltpu.make_async_copy(own, own, load_sem.at[a]))
    weight_loads = []
    for a, (src, full) in enumerate(weights):
        copy = pltpu.make_async_copy(src, full.at[pl.ds(f * per, per)], load_sem.at[2 + a])
        copy.start()
        weight_loads.append(copy)
    hidden[hidden_blocks] = jnp.zeros(hidden.shape[1:], hidden.dtype)
    pg_own[hidden_blocks] = jnp.zeros(pg_own.shape[1:], pg_own.dtype)
    enter(sizes)

    def part_shard(ref, s):
        return ref.at[pl.ds(s * blocks, blocks)]

    def shard(full, s, k):
        return full.at[pl.ds(s * blocks + k * chunk, chunk)]

    def line(a, s, k, way):
        piece = shard(features[a], z - way * s, k)
        w = 0 if way > 0 else 1
        return remote(
            piece, piece, zs_sem.at[a, w, s], zr_sem.at[a, w, s, k], {"tensor": z + way}
        )

    def line_sent(a, s, way):
        whole = part_shard(features[a], z - way * s)
        w = 0 if way > 0 else 1
        remote(
            whole, whole, zs_sem.at[a, w, s], zr_sem.at[a, w, s, 0], {"tensor": z + way}
        ).wait_send()

    def can_send(way):
        return z < n - 1 if way > 0 else z > 0

    def has(s, way):
        return z - s >= 0 if way > 0 else z + s <= n - 1

    def z_start(a):
        for k in range(CHUNKS):
            for way in (1, -1):

                @pl.when(can_send(way))
                def _():
                    line(a, 0, k, way).start()

    def mate_copy(src, dst, s, way):
        w = 0 if way > 0 else 1
        return remote(src, dst, ms_sem.at[w, s], mr_sem.at[w, s], mate)

    def mate_chunk(s, k, way):
        return mate_copy(shard(cot_own, z - way * s, k), shard(cot_mate, z - way * s, k), s, way)

    def mate_turned(s, way):
        w = 0 if way > 0 else 1
        at = pl.ds((z - way * s) * blocks, blocks)
        return remote(xt_own.at[at], xt_mate.at[at], ts_sem.at[w, s], tr_sem.at[w, s], mate)

    def turn(s, way):
        first = (z - way * s) * blocks

        @pl.loop(0, blocks // 2)
        def _(b):
            for i in range(2):
                xt_own[first + 2 * b + i] = x_all[first + 2 * b + i].T

        mate_turned(s, way).start()

    def z_event(a, s, k):
        for way in (1, -1):

            @pl.when(has(s, way))
            def _():
                line(a, s - 1, k, way).wait_recv()
                if s < n - 1:

                    @pl.when(can_send(way))
                    def _():
                        line(a, s, k, way).start()

                if a == 1:
                    mate_chunk(s, k, way).start()

    def turn_event(s):
        for way in (1, -1):

            @pl.when(has(s, way))
            def _():
                turn(s, way)

    def mate_chunks(act_on):
        def each(s, way):
            act_on(mate_copy(part_shard(cot_own, z - way * s), part_shard(cot_mate, z - way * s), s, way))

        each(0, 1)
        for s in range(1, n):
            for way in (1, -1):
                pl.when(has(s, way))(functools.partial(each, s, way))

    def mate_turns(act_on):
        act_on(mate_turned(0, 1))
        for s in range(1, n):
            for way in (1, -1):

                @pl.when(has(s, way))
                def _():
                    act_on(mate_turned(s, way))

    def tile_range(full, r_of, q, k):
        return full.at[pl.ds((r_of * 2 + c) * per + q * part + k * weight_size, weight_size)]

    def from_chip(d):
        return lax.rem(r - d + chips, chips)

    def w_copy(a, d, k):
        src = weights[a][0].at[pl.ds(y * part + k * weight_size, weight_size)]
        return remote(
            src, tile_range(weights[a][1], r, y, k), ws_sem.at[a, d - 1], wr_sem.at[a, d - 1, k],
            {"fsdp": lax.rem(r + d, chips) * 2 + c},
        )

    def y_copy(a, d, e, k):
        piece = tile_range(weights[a][1], from_chip(d), y, k)
        return remote(
            piece, piece, ys_sem.at[a, d - 1, e - 1], yr_sem.at[a, d - 1, e - 1, k],
            {"dp": lax.rem(y + e, replicas)},
        )

    def core_copy(a, d, e, k):
        piece = tile_range(weights[a][1], from_chip(d), lax.rem(y - e + replicas, replicas), k)
        return remote(piece, piece, cs_sem.at[a, d - 1, e], cr_sem.at[a, d - 1, e], mate)

    def share(full, r_of, q):
        return full.at[pl.ds((r_of * 2 + c) * per + q * part, part)]

    def core_copies(a, d, e):
        whole = share(weights[a][1], from_chip(d), lax.rem(y - e + replicas, replicas))
        return remote(whole, whole, cs_sem.at[a, d - 1, e], cr_sem.at[a, d - 1, e], mate)

    def weights_sent(a):
        own_core(a).wait_send()
        for d in range(1, chips):
            remote(
                weights[a][0].at[pl.ds(y * part, part)], share(weights[a][1], r, y),
                ws_sem.at[a, d - 1], wr_sem.at[a, d - 1, 0], {"fsdp": lax.rem(r + d, chips) * 2 + c},
            ).wait_send()
            for e in range(replicas):
                core_copies(a, d, e).wait_send()
            for e in range(1, replicas):
                whole = share(weights[a][1], from_chip(d), y)
                remote(
                    whole, whole, ys_sem.at[a, d - 1, e - 1], yr_sem.at[a, d - 1, e - 1, 0],
                    {"dp": lax.rem(y + e, replicas)},
                ).wait_send()

    def own_core(a):
        return remote(
            weights[a][0], weights[a][1].at[pl.ds(f * per, per)], os_sem.at[a], or_sem.at[a], mate
        )

    def w_event(a, k):
        for d in range(1, chips):
            w_copy(a, d, k).wait_recv()
            for e in range(1, replicas):
                y_copy(a, d, e, k).start()
            core_copy(a, d, 0, k).start()

    def y_event(a, k):
        for d in range(1, chips):
            for e in range(1, replicas):
                y_copy(a, d, e, k).wait_recv()
                core_copy(a, d, e, k).start()

    def weights_in(a):
        weight_loads[a].wait()
        own_core(a).wait_recv()
        for d in range(1, chips):
            for e in range(replicas):
                core_copies(a, d, e).wait_recv()

    def hidden_mate(g):
        at = pl.ds(g * hidden_span, hidden_span)
        return remote(ht_own.at[at], ht_mate.at[at], hs_sem.at[0], hr_sem.at[0], mate)

    def hidden_mates():
        return remote(ht_own, ht_mate, hs_sem.at[0], hr_sem.at[0], mate)

    def hidden_part(g):
        @pl.loop(g * hidden_span, (g + 1) * hidden_span)
        def _(h):
            spots = [h * COL_TILES + k for k in range(COL_TILES)]
            pre = mm(
                wide([x_all[tables[0, 1, i]] for i in spots], 1),
                wide([u_all[tables[0, 0, i]] for i in spots], 0), 1, 0,
            )
            value, tangent = gelu_parts(pre)
            value = value.astype(jnp.bfloat16)
            hidden[h] = value
            ht_own[h] = value.T
            slope[h] = tangent

        hidden_mate(g).start()

    def grad_mate(g):
        at = pl.ds(g * span, span)
        return remote(pg_own.at[at], pg_mate.at[at], gs_sem.at[0], gr_sem.at[0], mate)

    def grad_mates():
        at = pl.ds(0, hidden_blocks)
        return remote(pg_own.at[at], pg_mate, gs_sem.at[0], gr_sem.at[0], mate)

    def slope_part(g):
        @pl.loop(g * span, (g + 1) * span)
        def _(h):
            spots = [h * COL_TILES + k for k in range(COL_TILES)]
            value = mm(
                wide([cot_own[tables[1, 1, i]] for i in spots], 1),
                wide([d_all[tables[1, 0, i]] for i in spots], 1), 1, 1,
            )
            pg_own[h] = (value * slope[h]).astype(jnp.bfloat16)

        grad_mate(g).start()

    parts = (parts_o, parts_i)
    outs = (out, inp)
    held = (held_r, held_l)
    pair_width = 4

    run_parts = (HIDDEN_PARTS, PARTS)

    def run_part(a, g):
        t = 1 - a
        left, right, cut = (hidden, d_all, 0) if a == 0 else (pg_own, u_all, 1)
        steps = run.shape[0] // run_parts[a] // pair_width
        if g == 0:
            acc[...] = jnp.zeros_like(acc)

        @pl.loop(g * steps, (g + 1) * steps)
        def _(b):
            total = acc[...]
            for i in [b * pair_width + k for k in range(pair_width)]:
                product = mm(
                    wide([left[tables[t, 3, 2 * i]], left[tables[t, 3, 2 * i + 1]]], 1),
                    wide([right[tables[t, 2, 2 * i]], right[tables[t, 2, 2 * i + 1]]], cut), 1, cut,
                )
                total = jnp.where(tables[t, 4, 2 * i] == 1, 0.0, total) + product
                run[i] = total.astype(jnp.bfloat16)
            acc[...] = total

    def fold(a, i, way, source):
        s = n - 1 - i if way > 0 else i
        k = 0 if way > 0 else 1
        src = part_shard(parts[a], s) if source else held[k].at[a, i]
        return remote(
            src, held[k].at[a, i], ls_sem.at[a, k, i], lr_sem.at[a, k, i], {"tensor": z + way}
        )

    def edge(way):
        return z == 0 if way > 0 else z == n - 1

    def sends(i, way):
        return n - 1 - i > z if way > 0 else i < z

    def settle(a):
        target = parts[a]

        @pl.loop(0, target.shape[0])
        def _(b):
            spot = tables[1 - a, 5, b]
            found = run[jnp.maximum(spot, 0)]
            target[b] = jnp.where(spot >= 0, found, jnp.zeros_like(found))

        for i in range(n - 1):
            for way in (1, -1):

                @pl.when(edge(way))
                def _():
                    fold(a, i, way, True).start()

    def add_into(target, terms):
        @pl.loop(0, target.shape[0])
        def _(b):
            total = terms[0][b].astype(jnp.float32)
            for term_of in terms[1:]:
                total += term_of[b].astype(jnp.float32)
            target[b] = total.astype(target.dtype)

    def fold_event(a, t):
        for way in (1, -1):
            i = t - z if way > 0 else t - (n - 1 - z)
            s = n - 1 - i if way > 0 else i
            k = 0 if way > 0 else 1
            on_way = jnp.logical_and(i >= 0, sends(i, way))

            @pl.when(jnp.logical_and(on_way, jnp.logical_not(edge(way))))
            def _():
                fold(a, i, way, False).wait_recv()
                add_into(held[k].at[a, i], (held[k].at[a, i], part_shard(parts[a], s)))
                fold(a, i, way, False).start()

    def finish(a):
        mine = part_shard(parts[a], z)
        target = outs[a]

        def write(terms):
            for b in range(blocks):
                total = terms[0][b].astype(jnp.float32)
                for term_of in terms[1:]:
                    total += term_of[b].astype(jnp.float32)
                target[:, pl.ds(b * 128, 128)] = total.astype(target.dtype)

        @pl.when(z > 0)
        def _():
            fold(a, n - 1 - z, 1, False).wait_recv()

        @pl.when(z < n - 1)
        def _():
            fold(a, z, -1, False).wait_recv()

        @pl.when(z == 0)
        def _():
            write((mine, held_l.at[a, z]))

        @pl.when(z == n - 1)
        def _():
            write((mine, held_r.at[a, n - 1 - z]))

        @pl.when(jnp.logical_and(z > 0, z < n - 1))
        def _():
            write((mine, held_r.at[a, n - 1 - z], held_l.at[a, z]))

    sums = (ga_d, ga_u)
    others = (gb_d, gb_u)

    def term(a, j):
        if a == 0:
            at, to = down_rows[j], down_cols[j]
            return mm(wide([ht_own[at], ht_mate[at]], 1), wide([cot_own[to], cot_mate[to]], 0), 1, 0)
        at, to = up_rows[j], up_cols[j]
        return mm(wide([xt_own[at], xt_mate[at]], 1), wide([pg_own[to], pg_mate[to]], 0), 1, 0)

    def first_tile(q, k):
        return (q * 2 + c) * per + k * size

    def x_copy(a, k, d):
        q = lax.rem(r + d, chips)
        at = pl.ds(k * size, size)
        return remote(
            stage.at[a, d - 1, at], x_in.at[a, d - 1, at], xs_sem.at[a, d - 1], xr_sem.at[a, k, d - 1],
            {"fsdp": q * 2 + c},
        )

    def hand_over(a, first_piece, end):
        @pl.loop(first_piece, end)
        def _(k):
            for d in range(1, chips):
                first = first_tile(lax.rem(r + d, chips), k)
                values = [term(a, first + i) for i in range(size)]
                for i in range(size):
                    stage[a, d - 1, k * size + i] = values[i].astype(jnp.bfloat16)
                x_copy(a, k, d).start()

    def done_piece(a, k):
        return x_in.at[a, 0, pl.ds(k * size, size)]

    def e_copy(a, k, e):
        return remote(
            done_piece(a, k), others[a].at[e - 1, pl.ds(k * size, size)],
            es_sem.at[a, e - 1], er_sem.at[a, e - 1], {"dp": lax.rem(y + e, replicas)},
        )

    def keep_copy(a, k):
        return pltpu.make_async_copy(
            done_piece(a, k), sums[a].at[pl.ds(k * size, size)], keep_sem.at[a]
        )

    def x_events(a, first_piece, end):
        pl.loop(first_piece, end)(functools.partial(x_event, a))

    def x_event(a, k):
        first = first_tile(r, k)
        values = [term(a, first + i) for i in range(size)]
        for d in range(1, chips):
            x_copy(a, k, d).wait_recv()
        for i in range(size):
            total = values[i]
            for d in range(1, chips):
                total += x_in[a, d - 1, k * size + i].astype(jnp.float32)
            x_in[a, 0, k * size + i] = total.astype(jnp.bfloat16)
        for e in range(1, replicas):
            e_copy(a, k, e).start()
        keep_copy(a, k).start()

    plan = []

    def at(time, work, *args):
        plan.append((time, functools.partial(work, *args)))

    def start_all():
        loads[0].wait()
        z_start(0)
        for a in range(2):
            for k in range(weight_chunks):
                for d in range(1, chips):
                    w_copy(a, d, k).start()
        for a in range(2):
            own_core(a).start()
        loads[1].wait()
        for k in range(CHUNKS):
            mate_chunk(0, k, 1).start()

    def table_copy(t):
        return pltpu.make_async_copy(made.at[t], tables.at[t], table_sem.at[t])

    def make_table(t):
        near, far = ((uc, ur), (dr, dc))[t]
        for row, values in enumerate(tables_of(near[...], far[...], n * blocks)):
            made[t, pl.ds(row, 1), pl.ds(0, values.shape[1])] = values
        table_copy(t).start()

    at(0.0, start_all)
    for t in range(2):
        at(10.2 + 5.65 * t, make_table, t)
        at(24.0, lambda t: table_copy(t).wait(), t)
    at(5.7, turn, 0, 1)
    chunk_time = SHARD_TIME / CHUNKS
    for s in range(1, n):
        for k in range(CHUNKS):
            when = 2.0 + ((s - 1) * CHUNKS + k + 1) * chunk_time
            at(when, z_event, 0, s, k)
        at(2.0 + s * SHARD_TIME + 0.1 + chunk_time, turn_event, s)
    act_in = 2.0 + (n - 1) * SHARD_TIME
    at(2.05 + max(n - 2, 0) * SHARD_TIME, z_start, 1)
    for a in range(2):
        for k in range(weight_chunks):
            when = 2.2 + (a * weight_chunks + k + 1) * WEIGHT_TIME
            at(when, w_event, a, k)
            at(when + 1.2 * WEIGHT_TIME, y_event, a, k)
    up_in = 2.3 + (weight_chunks + 1.2) * WEIGHT_TIME
    down_in = 2.3 + (2 * weight_chunks + 1.2) * WEIGHT_TIME
    at(up_in + 2.0, weights_in, 0)
    at(down_in + 2.0, weights_in, 1)
    hidden_from = max(act_in, up_in + 2.0) + 0.5
    for g in range(HIDDEN_PARTS):
        at(hidden_from + 3.0 * g, hidden_part, g)
    out_from = max(hidden_from + 3.0 * HIDDEN_PARTS, down_in + 2.0) + 0.5
    for g in range(HIDDEN_PARTS):
        at(out_from + 2.4 * g, run_part, 0, g)
    out_settle = out_from + 2.4 * HIDDEN_PARTS
    at(out_settle, settle, 0)
    for s in range(1, n):
        for k in range(CHUNKS):
            at(act_in + ((s - 1) * CHUNKS + k + 1) * chunk_time, z_event, 1, s, k)
    cot_in = max(act_in + (n - 1) * SHARD_TIME, out_settle) + 1.0

    def cot_ready():
        mate_chunks(lambda copy: copy.wait_recv())
        hidden_mates().wait_recv()

    at(cot_in, cot_ready)
    piece_time = 2 * SHARD_TIME * PIECE_SHARE / pieces
    group = max(pieces // 8, 1)
    at(cot_in + 0.1, hand_over, 0, 0, group)
    for k in range(group, pieces, group):
        at(cot_in + 0.2 + 1.2 * (k // group), hand_over, 0, k, min(k + group, pieces))
    slope_from = cot_in + 9.0
    for g in range(PARTS):
        at(slope_from + 1.5 * g, slope_part, g)

    def grads_ready():
        mate_turns(lambda copy: copy.wait_recv())
        grad_mates().wait_recv()

    up_from = slope_from + 1.5 * PARTS + 1.0
    at(up_from, grads_ready)
    for k in range(0, pieces, group):
        at(up_from + 0.1 + 1.4 * (k // group), hand_over, 1, k, min(k + group, pieces))
    inp_from = up_from + 0.1 + 1.4 * 8
    for g in range(PARTS):
        at(inp_from + 1.5 * g, run_part, 1, g)
    inp_settle = inp_from + 1.5 * PARTS
    at(inp_settle, settle, 1)
    for a, start in enumerate((out_settle, inp_settle)):
        for t in range(1, n - 1):
            at(start + 1.0 + t * SHARD_TIME, fold_event, a, t)
        at(start + 3.0 + (n - 1) * SHARD_TIME, finish, a)
    for a in range(2):
        for k in range(pieces):
            when = cot_in + 2.2 + piece_time * (a * pieces + k + 1)
            at(max(when, up_from + 0.2) if a else when, x_event, a, k)

    plan.sort(key=lambda item: item[0])
    steps = []
    for _, work in plan:
        if work.func is x_event:
            a, k = work.args
            if steps and steps[-1].func is x_events and steps[-1].args[::2] == (a, k):
                work = functools.partial(x_events, a, steps.pop().args[1], k + 1)
            else:
                work = functools.partial(x_events, a, k, k + 1)
        steps.append(work)
    for work in steps:
        work()

    mate_chunks(lambda copy: copy.wait_send())
    mate_turns(lambda copy: copy.wait_send())
    for a in range(2):
        weights_sent(a)
        for way in (1, -1):
            for s in range(n - 1):

                @pl.when(jnp.logical_and(can_send(way), has(s, way)))
                def _():
                    line_sent(a, s, way)

        for i in range(n - 1):
            for way in (1, -1):

                @pl.when(sends(i, way))
                def _():
                    fold(a, i, way, False).wait_send()

    hidden_mates().wait_send()
    grad_mates().wait_send()
    for a in range(2):
        for d in range(1, chips):
            remote(
                stage.at[a, d - 1], x_in.at[a, d - 1], xs_sem.at[a, d - 1], xr_sem.at[a, 0, d - 1],
                {"fsdp": lax.rem(r + d, chips) * 2 + c},
            ).wait_send()
        pltpu.make_async_copy(x_in.at[a, 0], sums[a], keep_sem.at[a]).wait()
        for e in range(1, replicas):
            remote(
                x_in.at[a, 0], others[a].at[e - 1], es_sem.at[a, e - 1], er_sem.at[a, e - 1],
                {"dp": lax.rem(y + e, replicas)},
            ).wait()


def run_block(sizes, lists, activations, cotangent, up_tiles, down_tiles):
    n, chips, replicas = sizes
    rows, features = activations.shape
    blocks = features // 128
    per = up_tiles.shape[0]
    total_tiles = 2 * chips * per
    hidden_blocks = total_tiles // COL_TILES
    model_blocks = n * blocks
    pairs = (total_tiles + model_blocks) // 2
    part = per // replicas
    weight_chunks = min(WEIGHT_CHUNKS, part)
    pieces = min(PIECES, per)
    kind = jnp.bfloat16
    dma = pltpu.SemaphoreType.DMA
    vmem = pl.BlockSpec(memory_space=pltpu.VMEM)
    smem = pl.BlockSpec(memory_space=pltpu.SMEM)
    anywhere = pl.BlockSpec(memory_space=pl.ANY)

    def held(*shape):
        return pltpu.VMEM(shape + (rows, 128), kind)

    def twice(*shape):
        return [dma(shape), dma(shape)]

    return pl.pallas_call(
        functools.partial(block_kernel, sizes),
        out_shape=(
            [jax.ShapeDtypeStruct((rows, features), kind)] * 2
            + [jax.ShapeDtypeStruct((per, 128, 128), kind)] * 2
            + [jax.ShapeDtypeStruct((replicas - 1, per, 128, 128), kind)] * 2
        ),
        in_specs=[smem] * 4 + [vmem] * 4 + [anywhere] * 4,
        out_specs=[vmem] * 2 + [anywhere] * 4,
        scratch_shapes=[
            held(model_blocks),
            pltpu.VMEM((model_blocks, 128, rows), kind),
            pltpu.VMEM((model_blocks, 128, rows), kind),
            held(model_blocks),
            held(model_blocks),
            pltpu.VMEM((total_tiles, 128, 128), kind),
            pltpu.VMEM((total_tiles, 128, 128), kind),
            held(hidden_blocks + 1),
            pltpu.VMEM((hidden_blocks, 128, rows), kind),
            pltpu.VMEM((hidden_blocks, 128, rows), kind),
            pltpu.VMEM((hidden_blocks, rows, 128), jnp.float32),
            held(hidden_blocks + 1),
            held(hidden_blocks),
            held(pairs),
            pltpu.VMEM((rows, 128), jnp.float32),
            held(model_blocks),
            held(model_blocks),
            held(2, n - 1, blocks),
            held(2, n - 1, blocks),
            pltpu.VMEM((2, chips - 1, per, 128, 128), kind),
            pltpu.VMEM((2, chips - 1, per, 128, 128), kind),
            pltpu.VMEM((2, 8, padded(total_tiles + model_blocks)), jnp.int32),
            pltpu.SMEM((2, 8, padded(total_tiles + model_blocks)), jnp.int32),
            dma((4,)),
            dma((2, 2, n - 1)),
            dma((2, 2, n - 1, CHUNKS)),
            *twice(2, n),
            *twice(2, n),
            dma((2, chips - 1)),
            dma((2, chips - 1, weight_chunks)),
            dma((2, chips - 1, replicas - 1)),
            dma((2, chips - 1, replicas - 1, weight_chunks)),
            *twice(2, chips - 1, replicas),
            *twice(2),
            *twice(1),
            *twice(1),
            *twice(2, 2, n - 1),
            dma((2, chips - 1)),
            dma((2, pieces, chips - 1)),
            *twice(2, replicas - 1),
            dma((2,)),
            dma((2,)),
        ],
        compiler_params=pltpu.CompilerParams(
            collective_id=0, has_side_effects=True, vmem_limit_bytes=67043328
        ),
        name="block_all",
    )(*(v[:, 0] for v in lists), *(v.T for v in lists), activations, cotangent, up_tiles, down_tiles)


def total_kernel(ga_u, gb_u, ga_d, gb_d, up_grad, down_grad):
    for one, more, target in ((ga_u, gb_u, up_grad), (ga_d, gb_d, down_grad)):
        total = one[...].astype(jnp.float32)
        for e in range(more.shape[0]):
            total += more[e].astype(jnp.float32)
        target[...] = total


def totals(ga_u, gb_u, ga_d, gb_d):
    per = ga_u.shape[0]
    step = max(per // 2, 1)
    one = pl.BlockSpec((step, 128, 128), lambda i: (i, 0, 0))
    more = pl.BlockSpec((gb_u.shape[0], step, 128, 128), lambda i: (0, i, 0, 0))
    return pl.pallas_call(
        total_kernel,
        grid=(per // step,),
        out_shape=[jax.ShapeDtypeStruct(ga_u.shape, jnp.float32)] * 2,
        in_specs=[one, more, one, more],
        out_specs=[one, one],
        name="totals",
    )(ga_u, gb_u, ga_d, gb_d)


def body(sizes, activations, cotangent, up_tiles, down_tiles, up_rows, up_cols, down_rows, down_cols):
    lists = (up_rows, up_cols, down_rows, down_cols)
    out, inp, ga_u, ga_d, gb_u, gb_d = run_block(
        sizes, lists, activations, cotangent, up_tiles, down_tiles
    )
    up_grad, down_grad = totals(ga_u, gb_u, ga_d, gb_d)
    return out, inp, up_grad, down_grad


def solution(mesh):
    sizes = (mesh.shape["tensor"], mesh.shape["fsdp"] // 2, mesh.shape["dp"])
    in_specs = (
        P(("dp", "fsdp"), "tensor"),
        P(("dp", "fsdp"), "tensor"),
        P(("fsdp", "tensor"), None, None),
        P(("fsdp", "tensor"), None, None),
        P(None, "tensor"),
        P(None, "tensor"),
        P(None, "tensor"),
        P(None, "tensor"),
    )
    out_specs = (
        P(("dp", "fsdp"), "tensor"),
        P(("dp", "fsdp"), "tensor"),
        P(("fsdp", "tensor"), None, None),
        P(("fsdp", "tensor"), None, None),
    )
    return jax.shard_map(
        functools.partial(body, sizes), mesh=mesh, in_specs=in_specs, out_specs=out_specs,
        check_vma=False,
    )
```

```python
import functools

import jax
import jax.numpy as jnp
from jax import lax
from jax.experimental import pallas as pl
from jax.experimental.pallas import tpu as pltpu
from jax.sharding import PartitionSpec as P

MESH = pl.DeviceIdType.MESH
COL_TILES = 8
PIECES = 16
CHUNKS = 2
WEIGHT_CHUNKS = 4
PARTS = 8
HIDDEN_PARTS = 4
LANES = 128

SHARD_TIME = 11.3
WEIGHT_TIME = 5.6
PIECE_SHARE = 2

inv_root_two = 0.7071067811865476
inv_root_tau = 0.3989422804014327


def gelu_parts(values):
    normal_cdf = 0.5 * (1.0 + lax.erf(values * inv_root_two))
    density = inv_root_tau * jnp.exp(-0.5 * values * values)
    return (values * normal_cdf, normal_cdf + values * density)


def mm(a, b, ca, cb):
    return lax.dot_general(a, b, (((ca,), (cb,)), ((), ())), preferred_element_type=jnp.float32)


def wide(blocks, axis):
    return jnp.concatenate(blocks, axis=axis)


def remote(src, dst, send_sem, recv_sem, where):
    return pltpu.make_async_remote_copy(
        src_ref=src, dst_ref=dst, send_sem=send_sem, recv_sem=recv_sem,
        device_id=where, device_id_type=MESH,
    )


def place(sizes):
    n, chips, replicas = sizes
    z = lax.axis_index("tensor")
    f = lax.axis_index("fsdp")
    y = lax.axis_index("dp")
    return z, f // 2, f % 2, y


def enter(sizes):
    n, chips, replicas = sizes
    z, r, c, y = place(sizes)
    barrier = pltpu.get_barrier_semaphore()

    def greet(where):
        pl.semaphore_signal(barrier, inc=1, device_id=where, device_id_type=MESH)

    @pl.when(z < n - 1)
    def _():
        greet({"tensor": z + 1})

    @pl.when(z > 0)
    def _():
        greet({"tensor": z - 1})

    greet({"fsdp": r * 2 + 1 - c})
    for d in range(1, chips):
        greet({"fsdp": lax.rem(r + d, chips) * 2 + c})
    for e in range(1, replicas):
        greet({"dp": lax.rem(y + e, replicas)})
    sides = jnp.where(z < n - 1, 1, 0) + jnp.where(z > 0, 1, 0)
    pl.semaphore_wait(barrier, sides + 1 + (chips - 1) + (replicas - 1))


def padded(size):
    return -(-size // LANES) * LANES


def tables_of(near, far, model_blocks):
    count = near.shape[1]
    near_size = count // COL_TILES + 1
    spare = (near_size - 1) * 2
    wide_count = padded(count + model_blocks)

    def along(size, axis):
        return lax.broadcasted_iota(jnp.int32, (count, size), axis)

    def column(row, size):
        turned = jnp.broadcast_to(row, (LANES, count)).T
        return wide([turned] * (size // LANES), 1)

    def total(picked, values):
        return jnp.sum(jnp.where(picked, values, 0), axis=0, keepdims=True)

    at, over, over_wide = along(count, 0), along(count, 1), along(wide_count, 1)
    before = at < over
    near_c, far_c = column(near, wide_count), column(far, wide_count)
    near_n, far_n = near_c[:, :count], far_c[:, :count]
    spot = near * COL_TILES + total((near_n == near) & before, 1)
    packed = total(column(spot, count) == over, at * model_blocks + far_n)
    equal = far_n == far
    rank = total(equal & before, 1)
    often = total(equal, 1)
    takes = jnp.where((rank == often - 1) & (often % 2 == 1), 2, 1)
    takes_c = column(takes, count)
    place_of = rank + total(far_n < far, takes_c)
    place_c = column(place_of * 2 + jnp.where(rank == 0, 1, 0), wide_count)
    code = (along(wide_count, 0) * near_size + near_c) * 2 + place_c % 2 - spare
    pair_code = total(place_c // 2 == over_wide, code) + spare
    ends = padded(model_blocks)
    block = along(ends, 1)
    until = total(far_c[:, :ends] <= block, takes_c[:, :ends])
    last = jnp.where(total(far_c[:, :ends] == block, 1) > 0, until // 2 - 1, -1)
    pair_far = pair_code // 2
    return (
        packed // model_blocks, packed % model_blocks,
        pair_far // near_size, pair_far % near_size, pair_code % 2, last,
    )


def block_kernel(
    sizes, up_rows, up_cols, down_rows, down_cols, ur, uc, dr, dc,
    act, cot, up, down,
    out, inp, ga_u, ga_d, gb_u, gb_d,
    x_all, flat_o, flat_i, xt_own, xt_mate, cot_own, cot_mate, u_all, d_all, hidden, ht_own, ht_mate, slope,
    pg_own, pg_mate, run, acc, parts_o, parts_i, held_r, held_l, stage, x_in, made, tables,
    load_sem, zs_sem, zr_sem, ms_sem, mr_sem, ts_sem, tr_sem, ws_sem, wr_sem, ys_sem, yr_sem, cs_sem, cr_sem,
    hs_sem, hr_sem, gs_sem, gr_sem, ls_sem, lr_sem, xs_sem, xr_sem, es_sem, er_sem, keep_sem, table_sem, out_sem,
):
    n, chips, replicas = sizes
    z, r, c, y = place(sizes)
    f = r * 2 + c
    blocks = act.shape[1] // 128
    per = up.shape[0]
    part = per // replicas
    total_tiles = u_all.shape[0]
    hidden_blocks = slope.shape[0]
    chunk = blocks // CHUNKS
    weight_chunks = min(WEIGHT_CHUNKS, part)
    weight_size = part // weight_chunks
    pieces = min(PIECES, per)
    size = per // pieces
    span = hidden_blocks // PARTS
    hidden_span = hidden_blocks // HIDDEN_PARTS
    features = (x_all, cot_own)
    weights = ((up, u_all), (down, d_all))
    mate = {"fsdp": r * 2 + 1 - c}

    loads = []
    for a, (src, full) in enumerate(((act, x_all), (cot, cot_own))):
        for b in range(blocks):
            pltpu.make_async_copy(
                src.at[:, pl.ds(b * 128, 128)], full.at[z * blocks + b], load_sem.at[a]
            ).start()
        own = full.at[pl.ds(z * blocks, blocks)]
        loads.append(pltpu.make_async_copy(own, own, load_sem.at[a]))
    weight_loads = []
    for a, (src, full) in enumerate(weights):
        copy = pltpu.make_async_copy(src, full.at[pl.ds(f * per, per)], load_sem.at[2 + a])
        copy.start()
        weight_loads.append(copy)
    hidden[hidden_blocks] = jnp.zeros(hidden.shape[1:], hidden.dtype)
    pg_own[hidden_blocks] = jnp.zeros(pg_own.shape[1:], pg_own.dtype)
    enter(sizes)

    def part_shard(ref, s):
        return ref.at[pl.ds(s * blocks, blocks)]

    def shard(full, s, k):
        return full.at[pl.ds(s * blocks + k * chunk, chunk)]

    def line(a, s, k, way):
        piece = shard(features[a], z - way * s, k)
        w = 0 if way > 0 else 1
        return remote(
            piece, piece, zs_sem.at[a, w, s], zr_sem.at[a, w, s, k], {"tensor": z + way}
        )

    def line_sent(a, s, way):
        whole = part_shard(features[a], z - way * s)
        w = 0 if way > 0 else 1
        remote(
            whole, whole, zs_sem.at[a, w, s], zr_sem.at[a, w, s, 0], {"tensor": z + way}
        ).wait_send()

    def can_send(way):
        return z < n - 1 if way > 0 else z > 0

    def has(s, way):
        return z - s >= 0 if way > 0 else z + s <= n - 1

    def z_start(a):
        for k in range(CHUNKS):
            for way in (1, -1):

                @pl.when(can_send(way))
                def _():
                    line(a, 0, k, way).start()

    def mate_chunk(s, k, way):
        return remote(
            shard(cot_own, z - way * s, k), shard(cot_mate, z - way * s, k),
            ms_sem.at[0], mr_sem.at[0], mate,
        )

    def mate_chunks():
        return remote(cot_own, cot_mate, ms_sem.at[0], mr_sem.at[0], mate)

    def mate_turned(s, way):
        at = pl.ds((z - way * s) * blocks, blocks)
        return remote(xt_own.at[at], xt_mate.at[at], ts_sem.at[0], tr_sem.at[0], mate)

    def mate_turns():
        return remote(xt_own, xt_mate, ts_sem.at[0], tr_sem.at[0], mate)

    def turn(s, way):
        first = (z - way * s) * blocks

        @pl.loop(0, blocks // 2)
        def _(b):
            for i in range(2):
                xt_own[first + 2 * b + i] = x_all[first + 2 * b + i].T

        mate_turned(s, way).start()

    def z_event(a, s, k):
        for way in (1, -1):

            @pl.when(has(s, way))
            def _():
                line(a, s - 1, k, way).wait_recv()
                if s < n - 1:

                    @pl.when(can_send(way))
                    def _():
                        line(a, s, k, way).start()

                if a == 1:
                    mate_chunk(s, k, way).start()

    def turn_event(s):
        for way in (1, -1):

            @pl.when(has(s, way))
            def _():
                turn(s, way)

    def tile_range(full, r_of, q, k):
        return full.at[pl.ds((r_of * 2 + c) * per + q * part + k * weight_size, weight_size)]

    def from_chip(d):
        return lax.rem(r - d + chips, chips)

    def w_copy(a, d, k):
        src = weights[a][0].at[pl.ds(y * part + k * weight_size, weight_size)]
        return remote(
            src, tile_range(weights[a][1], r, y, k), ws_sem.at[a, d - 1], wr_sem.at[a, d - 1, k],
            {"fsdp": lax.rem(r + d, chips) * 2 + c},
        )

    def y_copy(a, d, e, k):
        piece = tile_range(weights[a][1], from_chip(d), y, k)
        return remote(
            piece, piece, ys_sem.at[a, d - 1, e - 1], yr_sem.at[a, d - 1, e - 1, k],
            {"dp": lax.rem(y + e, replicas)},
        )

    def core_copy(a, d, e, k):
        piece = tile_range(weights[a][1], from_chip(d), lax.rem(y - e + replicas, replicas), k)
        return remote(piece, piece, cs_sem.at[a], cr_sem.at[a], mate)

    def share(full, r_of, q):
        return full.at[pl.ds((r_of * 2 + c) * per + q * part, part)]

    def core_copies(a):
        whole = weights[a][1].at[pl.ds(0, chips * per)]
        return remote(whole, whole, cs_sem.at[a], cr_sem.at[a], mate)

    def weights_sent(a):
        core_copies(a).wait_send()
        for d in range(1, chips):
            remote(
                weights[a][0].at[pl.ds(y * part, part)], share(weights[a][1], r, y),
                ws_sem.at[a, d - 1], wr_sem.at[a, d - 1, 0], {"fsdp": lax.rem(r + d, chips) * 2 + c},
            ).wait_send()
            for e in range(1, replicas):
                whole = share(weights[a][1], from_chip(d), y)
                remote(
                    whole, whole, ys_sem.at[a, d - 1, e - 1], yr_sem.at[a, d - 1, e - 1, 0],
                    {"dp": lax.rem(y + e, replicas)},
                ).wait_send()

    def own_core(a):
        return remote(
            weights[a][0], weights[a][1].at[pl.ds(f * per, per)], cs_sem.at[a], cr_sem.at[a], mate
        )

    def w_event(a, k):
        for d in range(1, chips):
            w_copy(a, d, k).wait_recv()
            for e in range(1, replicas):
                y_copy(a, d, e, k).start()
            core_copy(a, d, 0, k).start()

    def y_event(a, k):
        for d in range(1, chips):
            for e in range(1, replicas):
                y_copy(a, d, e, k).wait_recv()
                core_copy(a, d, e, k).start()

    def weights_in(a):
        weight_loads[a].wait()
        core_copies(a).wait_recv()

    def hidden_mate(g):
        at = pl.ds(g * hidden_span, hidden_span)
        return remote(ht_own.at[at], ht_mate.at[at], hs_sem.at[0], hr_sem.at[0], mate)

    def hidden_mates():
        return remote(ht_own, ht_mate, hs_sem.at[0], hr_sem.at[0], mate)

    def hidden_part(g):
        @pl.loop(g * hidden_span, (g + 1) * hidden_span)
        def _(h):
            spots = [h * COL_TILES + k for k in range(COL_TILES)]
            pre = mm(
                wide([x_all[tables[0, 1, i]] for i in spots], 1),
                wide([u_all[tables[0, 0, i]] for i in spots], 0), 1, 0,
            )
            value, tangent = gelu_parts(pre)
            value = value.astype(jnp.bfloat16)
            hidden[h] = value
            ht_own[h] = value.T
            slope[h] = tangent

        hidden_mate(g).start()

    def grad_mate(g):
        at = pl.ds(g * span, span)
        return remote(pg_own.at[at], pg_mate.at[at], gs_sem.at[0], gr_sem.at[0], mate)

    def grad_mates():
        at = pl.ds(0, hidden_blocks)
        return remote(pg_own.at[at], pg_mate, gs_sem.at[0], gr_sem.at[0], mate)

    def slope_part(g):
        @pl.loop(g * span, (g + 1) * span)
        def _(h):
            spots = [h * COL_TILES + k for k in range(COL_TILES)]
            value = mm(
                wide([cot_own[tables[1, 1, i]] for i in spots], 1),
                wide([d_all[tables[1, 0, i]] for i in spots], 1), 1, 1,
            )
            pg_own[h] = (value * slope[h]).astype(jnp.bfloat16)

        grad_mate(g).start()

    parts = (parts_o, parts_i)
    outs = ((flat_o, out), (flat_i, inp))

    def out_copy(a):
        return pltpu.make_async_copy(outs[a][0], outs[a][1], out_sem.at[a])
    held = (held_r, held_l)
    pair_width = 4

    run_parts = (HIDDEN_PARTS, PARTS)

    def run_part(a, g):
        t = 1 - a
        left, right, cut = (hidden, d_all, 0) if a == 0 else (pg_own, u_all, 1)
        steps = run.shape[0] // run_parts[a] // pair_width
        if g == 0:
            acc[...] = jnp.zeros_like(acc)

        @pl.loop(g * steps, (g + 1) * steps)
        def _(b):
            total = acc[...]
            for i in [b * pair_width + k for k in range(pair_width)]:
                product = mm(
                    wide([left[tables[t, 3, 2 * i]], left[tables[t, 3, 2 * i + 1]]], 1),
                    wide([right[tables[t, 2, 2 * i]], right[tables[t, 2, 2 * i + 1]]], cut), 1, cut,
                )
                total = jnp.where(tables[t, 4, 2 * i] == 1, 0.0, total) + product
                run[i] = total.astype(jnp.bfloat16)
            acc[...] = total

    def fold(a, i, way, source):
        s = n - 1 - i if way > 0 else i
        k = 0 if way > 0 else 1
        src = part_shard(parts[a], s) if source else held[k].at[a, i]
        return remote(
            src, held[k].at[a, i], ls_sem.at[a, k, i], lr_sem.at[a, k, i], {"tensor": z + way}
        )

    def edge(way):
        return z == 0 if way > 0 else z == n - 1

    def sends(i, way):
        return n - 1 - i > z if way > 0 else i < z

    def settle(a):
        target = parts[a]

        @pl.loop(0, target.shape[0])
        def _(b):
            spot = tables[1 - a, 5, b]
            found = run[jnp.maximum(spot, 0)]
            target[b] = jnp.where(spot >= 0, found, jnp.zeros_like(found))

        for i in range(n - 1):
            for way in (1, -1):

                @pl.when(edge(way))
                def _():
                    fold(a, i, way, True).start()

    def add_into(target, terms):
        @pl.loop(0, target.shape[0])
        def _(b):
            total = terms[0][b].astype(jnp.float32)
            for term_of in terms[1:]:
                total += term_of[b].astype(jnp.float32)
            target[b] = total.astype(target.dtype)

    def fold_event(a, t):
        for way in (1, -1):
            i = t - z if way > 0 else t - (n - 1 - z)
            s = n - 1 - i if way > 0 else i
            k = 0 if way > 0 else 1
            on_way = jnp.logical_and(i >= 0, sends(i, way))

            @pl.when(jnp.logical_and(on_way, jnp.logical_not(edge(way))))
            def _():
                fold(a, i, way, False).wait_recv()
                add_into(held[k].at[a, i], (held[k].at[a, i], part_shard(parts[a], s)))
                fold(a, i, way, False).start()

    def finish(a):
        mine = part_shard(parts[a], z)
        target = outs[a][0]

        def write(terms):
            for b in range(blocks):
                total = terms[0][b].astype(jnp.float32)
                for term_of in terms[1:]:
                    total += term_of[b].astype(jnp.float32)
                target[:, pl.ds(b * 128, 128)] = total.astype(target.dtype)

        @pl.when(z > 0)
        def _():
            fold(a, n - 1 - z, 1, False).wait_recv()

        @pl.when(z < n - 1)
        def _():
            fold(a, z, -1, False).wait_recv()

        @pl.when(z == 0)
        def _():
            write((mine, held_l.at[a, z]))

        @pl.when(z == n - 1)
        def _():
            write((mine, held_r.at[a, n - 1 - z]))

        @pl.when(jnp.logical_and(z > 0, z < n - 1))
        def _():
            write((mine, held_r.at[a, n - 1 - z], held_l.at[a, z]))

        out_copy(a).start()

    sums = (ga_d, ga_u)
    others = (gb_d, gb_u)

    def term(a, j):
        if a == 0:
            at, to = down_rows[j], down_cols[j]
            return mm(wide([ht_own[at], ht_mate[at]], 1), wide([cot_own[to], cot_mate[to]], 0), 1, 0)
        at, to = up_rows[j], up_cols[j]
        return mm(wide([xt_own[at], xt_mate[at]], 1), wide([pg_own[to], pg_mate[to]], 0), 1, 0)

    def first_tile(q, k):
        return (q * 2 + c) * per + k * size

    def x_copy(a, k, d):
        q = lax.rem(r + d, chips)
        at = pl.ds(k * size, size)
        return remote(
            stage.at[a, d - 1, at], x_in.at[a, d - 1, at], xs_sem.at[a, d - 1], xr_sem.at[a, k, d - 1],
            {"fsdp": q * 2 + c},
        )

    def hand_over(a, first_piece, end):
        @pl.loop(first_piece, end)
        def _(k):
            for d in range(1, chips):
                first = first_tile(lax.rem(r + d, chips), k)
                values = [term(a, first + i) for i in range(size)]
                for i in range(size):
                    stage[a, d - 1, k * size + i] = values[i].astype(jnp.bfloat16)
                x_copy(a, k, d).start()

    def done_piece(a, k):
        return x_in.at[a, 0, pl.ds(k * size, size)]

    def e_copy(a, k, e):
        return remote(
            done_piece(a, k), others[a].at[e - 1, pl.ds(k * size, size)],
            es_sem.at[a, e - 1], er_sem.at[a, e - 1], {"dp": lax.rem(y + e, replicas)},
        )

    def keep_copy(a, k):
        return pltpu.make_async_copy(
            done_piece(a, k), sums[a].at[pl.ds(k * size, size)], keep_sem.at[a]
        )

    def x_events(a, first_piece, end):
        pl.loop(first_piece, end)(functools.partial(x_event, a))

    def x_event(a, k):
        first = first_tile(r, k)
        values = [term(a, first + i) for i in range(size)]
        for d in range(1, chips):
            x_copy(a, k, d).wait_recv()
        for i in range(size):
            total = values[i]
            for d in range(1, chips):
                total += x_in[a, d - 1, k * size + i].astype(jnp.float32)
            x_in[a, 0, k * size + i] = total.astype(jnp.bfloat16)
        for e in range(1, replicas):
            e_copy(a, k, e).start()
        keep_copy(a, k).start()

    plan = []

    def at(time, work, *args):
        plan.append((time, functools.partial(work, *args)))

    def start_all():
        loads[0].wait()
        z_start(0)
        for a in range(2):
            for k in range(weight_chunks):
                for d in range(1, chips):
                    w_copy(a, d, k).start()
        for a in range(2):
            own_core(a).start()
        loads[1].wait()
        for k in range(CHUNKS):
            mate_chunk(0, k, 1).start()

    def table_copy(t):
        return pltpu.make_async_copy(made.at[t], tables.at[t], table_sem.at[t])

    def make_table(t):
        near, far = ((uc, ur), (dr, dc))[t]
        for row, values in enumerate(tables_of(near[...], far[...], n * blocks)):
            made[t, pl.ds(row, 1), pl.ds(0, values.shape[1])] = values
        table_copy(t).start()

    at(0.0, start_all)
    for t in range(2):
        at(10.2 + 5.65 * t, make_table, t)
        at(24.0, lambda t: table_copy(t).wait(), t)
    at(5.7, turn, 0, 1)
    chunk_time = SHARD_TIME / CHUNKS
    for s in range(1, n):
        for k in range(CHUNKS):
            when = 2.0 + ((s - 1) * CHUNKS + k + 1) * chunk_time
            at(when, z_event, 0, s, k)
        at(2.0 + s * SHARD_TIME + 0.1 + chunk_time, turn_event, s)
    act_in = 2.0 + (n - 1) * SHARD_TIME
    at(2.05 + max(n - 2, 0) * SHARD_TIME, z_start, 1)
    for a in range(2):
        for k in range(weight_chunks):
            when = 2.2 + (a * weight_chunks + k + 1) * WEIGHT_TIME
            at(when, w_event, a, k)
            at(when + 1.2 * WEIGHT_TIME, y_event, a, k)
    up_in = 2.3 + (weight_chunks + 1.2) * WEIGHT_TIME
    down_in = 2.3 + (2 * weight_chunks + 1.2) * WEIGHT_TIME
    at(up_in + 2.0, weights_in, 0)
    at(down_in + 2.0, weights_in, 1)
    hidden_from = max(act_in, up_in + 2.0) + 0.5
    for g in range(HIDDEN_PARTS):
        at(hidden_from + 3.0 * g, hidden_part, g)
    out_from = max(hidden_from + 3.0 * HIDDEN_PARTS, down_in + 2.0) + 0.5
    for g in range(HIDDEN_PARTS):
        at(out_from + 2.4 * g, run_part, 0, g)
    out_settle = out_from + 2.4 * HIDDEN_PARTS
    at(out_settle, settle, 0)
    for s in range(1, n):
        for k in range(CHUNKS):
            at(act_in + ((s - 1) * CHUNKS + k + 1) * chunk_time, z_event, 1, s, k)
    cot_in = max(act_in + (n - 1) * SHARD_TIME, out_settle) + 1.0

    def cot_ready():
        mate_chunks().wait_recv()
        hidden_mates().wait_recv()

    at(cot_in, cot_ready)
    piece_time = 2 * SHARD_TIME * PIECE_SHARE / pieces
    group = max(pieces // 8, 1)
    at(cot_in + 0.1, hand_over, 0, 0, group)
    for k in range(group, pieces, group):
        at(cot_in + 0.2 + 1.2 * (k // group), hand_over, 0, k, min(k + group, pieces))
    slope_from = cot_in + 9.0
    for g in range(PARTS):
        at(slope_from + 1.5 * g, slope_part, g)

    def grads_ready():
        mate_turns().wait_recv()
        grad_mates().wait_recv()

    up_from = slope_from + 1.5 * PARTS + 1.0
    at(up_from, grads_ready)
    for k in range(0, pieces, group):
        at(up_from + 0.1 + 1.4 * (k // group), hand_over, 1, k, min(k + group, pieces))
    inp_from = up_from + 0.1 + 1.4 * 8
    for g in range(PARTS):
        at(inp_from + 1.5 * g, run_part, 1, g)
    inp_settle = inp_from + 1.5 * PARTS
    at(inp_settle, settle, 1)
    for a, start in enumerate((out_settle, inp_settle)):
        for t in range(1, n - 1):
            at(start + 1.0 + t * SHARD_TIME, fold_event, a, t)
        at(start + 3.0 + (n - 1) * SHARD_TIME, finish, a)
    for a in range(2):
        for k in range(pieces):
            when = cot_in + 2.2 + piece_time * (a * pieces + k + 1)
            at(max(when, up_from + 0.2) if a else when, x_event, a, k)

    plan.sort(key=lambda item: item[0])
    steps = []
    for _, work in plan:
        if work.func is x_event:
            a, k = work.args
            if steps and steps[-1].func is x_events and steps[-1].args[::2] == (a, k):
                work = functools.partial(x_events, a, steps.pop().args[1], k + 1)
            else:
                work = functools.partial(x_events, a, k, k + 1)
        steps.append(work)
    for work in steps:
        work()

    mate_chunks().wait_send()
    mate_turns().wait_send()
    for a in range(2):
        out_copy(a).wait()
        weights_sent(a)
        for way in (1, -1):
            for s in range(n - 1):

                @pl.when(jnp.logical_and(can_send(way), has(s, way)))
                def _():
                    line_sent(a, s, way)

        for i in range(n - 1):
            for way in (1, -1):

                @pl.when(sends(i, way))
                def _():
                    fold(a, i, way, False).wait_send()

    hidden_mates().wait_send()
    grad_mates().wait_send()
    for a in range(2):
        for d in range(1, chips):
            remote(
                stage.at[a, d - 1], x_in.at[a, d - 1], xs_sem.at[a, d - 1], xr_sem.at[a, 0, d - 1],
                {"fsdp": lax.rem(r + d, chips) * 2 + c},
            ).wait_send()
        pltpu.make_async_copy(x_in.at[a, 0], sums[a], keep_sem.at[a]).wait()
        for e in range(1, replicas):
            remote(
                x_in.at[a, 0], others[a].at[e - 1], es_sem.at[a, e - 1], er_sem.at[a, e - 1],
                {"dp": lax.rem(y + e, replicas)},
            ).wait()


def run_block(sizes, lists, activations, cotangent, up_tiles, down_tiles):
    n, chips, replicas = sizes
    rows, features = activations.shape
    blocks = features // 128
    per = up_tiles.shape[0]
    total_tiles = 2 * chips * per
    hidden_blocks = total_tiles // COL_TILES
    model_blocks = n * blocks
    pairs = (total_tiles + model_blocks) // 2
    part = per // replicas
    weight_chunks = min(WEIGHT_CHUNKS, part)
    pieces = min(PIECES, per)
    kind = jnp.bfloat16
    dma = pltpu.SemaphoreType.DMA
    vmem = pl.BlockSpec(memory_space=pltpu.VMEM)
    smem = pl.BlockSpec(memory_space=pltpu.SMEM)
    anywhere = pl.BlockSpec(memory_space=pl.ANY)

    def held(*shape):
        return pltpu.VMEM(shape + (rows, 128), kind)

    def twice(*shape):
        return [dma(shape), dma(shape)]

    return pl.pallas_call(
        functools.partial(block_kernel, sizes),
        out_shape=(
            [jax.ShapeDtypeStruct((rows, features), kind)] * 2
            + [jax.ShapeDtypeStruct((per, 128, 128), kind)] * 2
            + [jax.ShapeDtypeStruct((replicas - 1, per, 128, 128), kind)] * 2
        ),
        in_specs=[smem] * 4 + [vmem] * 4 + [anywhere] * 4,
        out_specs=[anywhere] * 6,
        scratch_shapes=[
            held(model_blocks),
            pltpu.VMEM((rows, features), kind),
            pltpu.VMEM((rows, features), kind),
            pltpu.VMEM((model_blocks, 128, rows), kind),
            pltpu.VMEM((model_blocks, 128, rows), kind),
            held(model_blocks),
            held(model_blocks),
            pltpu.VMEM((total_tiles, 128, 128), kind),
            pltpu.VMEM((total_tiles, 128, 128), kind),
            held(hidden_blocks + 1),
            pltpu.VMEM((hidden_blocks, 128, rows), kind),
            pltpu.VMEM((hidden_blocks, 128, rows), kind),
            pltpu.VMEM((hidden_blocks, rows, 128), jnp.float32),
            held(hidden_blocks + 1),
            held(hidden_blocks),
            held(pairs),
            pltpu.VMEM((rows, 128), jnp.float32),
            held(model_blocks),
            held(model_blocks),
            held(2, n - 1, blocks),
            held(2, n - 1, blocks),
            pltpu.VMEM((2, chips - 1, per, 128, 128), kind),
            pltpu.VMEM((2, chips - 1, per, 128, 128), kind),
            pltpu.VMEM((2, 8, padded(total_tiles + model_blocks)), jnp.int32),
            pltpu.SMEM((2, 8, padded(total_tiles + model_blocks)), jnp.int32),
            dma((4,)),
            dma((2, 2, n - 1)),
            dma((2, 2, n - 1, CHUNKS)),
            *twice(1),
            *twice(1),
            dma((2, chips - 1)),
            dma((2, chips - 1, weight_chunks)),
            dma((2, chips - 1, replicas - 1)),
            dma((2, chips - 1, replicas - 1, weight_chunks)),
            *twice(2),
            *twice(1),
            *twice(1),
            *twice(2, 2, n - 1),
            dma((2, chips - 1)),
            dma((2, pieces, chips - 1)),
            *twice(2, replicas - 1),
            dma((2,)),
            dma((2,)),
            dma((2,)),
        ],
        compiler_params=pltpu.CompilerParams(
            collective_id=0, has_side_effects=True, vmem_limit_bytes=67043328
        ),
        name="block_all",
    )(*(v[:, 0] for v in lists), *(v.T for v in lists), activations, cotangent, up_tiles, down_tiles)


def total_kernel(ga_u, gb_u, ga_d, gb_d, out_in, inp_in, up_grad, down_grad, out, inp):
    for one, more, target in ((ga_u, gb_u, up_grad), (ga_d, gb_d, down_grad)):
        total = one[...].astype(jnp.float32)
        for e in range(more.shape[0]):
            total += more[e].astype(jnp.float32)
        target[...] = total
    out[...] = out_in[...]
    inp[...] = inp_in[...]


def totals(ga_u, gb_u, ga_d, gb_d, out, inp):
    per = ga_u.shape[0]
    step = max(per // 2, 1)
    rows, features = out.shape
    one = pl.BlockSpec((step, 128, 128), lambda i: (i, 0, 0))
    more = pl.BlockSpec((gb_u.shape[0], step, 128, 128), lambda i: (0, i, 0, 0))
    flat = pl.BlockSpec((rows * step // per, features), lambda i: (i, 0))
    return pl.pallas_call(
        total_kernel,
        grid=(per // step,),
        out_shape=(
            [jax.ShapeDtypeStruct(ga_u.shape, jnp.float32)] * 2 + [jax.ShapeDtypeStruct(out.shape, out.dtype)] * 2
        ),
        in_specs=[one, more, one, more, flat, flat],
        out_specs=[one, one, flat, flat],
        name="totals",
    )(ga_u, gb_u, ga_d, gb_d, out, inp)


def body(sizes, activations, cotangent, up_tiles, down_tiles, up_rows, up_cols, down_rows, down_cols):
    lists = (up_rows, up_cols, down_rows, down_cols)
    out, inp, ga_u, ga_d, gb_u, gb_d = run_block(
        sizes, lists, activations, cotangent, up_tiles, down_tiles
    )
    up_grad, down_grad, out, inp = totals(ga_u, gb_u, ga_d, gb_d, out, inp)
    return out, inp, up_grad, down_grad


def solution(mesh):
    sizes = (mesh.shape["tensor"], mesh.shape["fsdp"] // 2, mesh.shape["dp"])
    in_specs = (
        P(("dp", "fsdp"), "tensor"),
        P(("dp", "fsdp"), "tensor"),
        P(("fsdp", "tensor"), None, None),
        P(("fsdp", "tensor"), None, None),
        P(None, "tensor"),
        P(None, "tensor"),
        P(None, "tensor"),
        P(None, "tensor"),
    )
    out_specs = (
        P(("dp", "fsdp"), "tensor"),
        P(("dp", "fsdp"), "tensor"),
        P(("fsdp", "tensor"), None, None),
        P(("fsdp", "tensor"), None, None),
    )
    return jax.shard_map(
        functools.partial(body, sizes), mesh=mesh, in_specs=in_specs, out_specs=out_specs,
        check_vma=False,
    )
```

```python
import functools

import jax
import jax.numpy as jnp
from jax import lax
from jax.experimental import pallas as pl
from jax.experimental.pallas import tpu as pltpu
from jax.sharding import PartitionSpec as P

MESH = pl.DeviceIdType.MESH
COL_TILES = 8
PIECES = 16
CHUNKS = 2
WEIGHT_CHUNKS = 4
PARTS = 8
HIDDEN_PARTS = 4
RELAY = 2
INP_REST = 55.0
FINISH = 100.0
INP_LATE = 48.0
FOLD_LATE = 2.0
PASS_X = 24.0
RELAYED = 42.0
PASS_Y = 54.0
LANES = 128

SHARD_TIME = 11.3
WEIGHT_TIME = 5.6
PIECE_SHARE = 2

inv_root_two = 0.7071067811865476
inv_root_tau = 0.3989422804014327


def gelu_parts(values):
    normal_cdf = 0.5 * (1.0 + lax.erf(values * inv_root_two))
    density = inv_root_tau * jnp.exp(-0.5 * values * values)
    return (values * normal_cdf, normal_cdf + values * density)


def mm(a, b, ca, cb):
    return lax.dot_general(a, b, (((ca,), (cb,)), ((), ())), preferred_element_type=jnp.float32)


def wide(blocks, axis):
    return jnp.concatenate(blocks, axis=axis)


def remote(src, dst, send_sem, recv_sem, where):
    return pltpu.make_async_remote_copy(
        src_ref=src, dst_ref=dst, send_sem=send_sem, recv_sem=recv_sem,
        device_id=where, device_id_type=MESH,
    )


def place(sizes):
    n, chips, replicas = sizes
    z = lax.axis_index("tensor")
    f = lax.axis_index("fsdp")
    y = lax.axis_index("dp")
    return z, f // 2, f % 2, y


def relay_pieces(n, pieces):
    return min(RELAY, pieces // 4) if n >= 4 else 0


def enter(sizes, relays):
    n, chips, replicas = sizes
    z, r, c, y = place(sizes)
    barrier = pltpu.get_barrier_semaphore()

    def greet(where):
        pl.semaphore_signal(barrier, inc=1, device_id=where, device_id_type=MESH)

    @pl.when(z < n - 1)
    def _():
        greet({"tensor": z + 1})

    @pl.when(z > 0)
    def _():
        greet({"tensor": z - 1})

    greet({"fsdp": r * 2 + 1 - c})
    for d in range(1, chips):
        greet({"fsdp": lax.rem(r + d, chips) * 2 + c})
    for e in range(1, replicas):
        greet({"dp": lax.rem(y + e, replicas)})
    others = (chips - 1) + (replicas - 1)
    awaited = jnp.where(z < n - 1, 1, 0) + jnp.where(z > 0, 1, 0) + 1 + others
    if relays:

        @pl.when(jnp.logical_or(z == 1, z == n - 2))
        def _():
            outer = jnp.where(z == 1, 0, n - 1)
            for d in range(1, chips):
                greet({"fsdp": lax.rem(r + d, chips) * 2 + c, "tensor": outer})
            for e in range(1, replicas):
                greet({"dp": lax.rem(y + e, replicas), "tensor": outer})

        awaited += jnp.where(jnp.logical_or(z == 0, z == n - 1), others, 0)
    pl.semaphore_wait(barrier, awaited)


def padded(size):
    return -(-size // LANES) * LANES


def tables_of(near, far, model_blocks):
    count = near.shape[1]
    near_size = count // COL_TILES + 1
    spare = (near_size - 1) * 2
    wide_count = padded(count + model_blocks)

    def along(size, axis):
        return lax.broadcasted_iota(jnp.int32, (count, size), axis)

    def column(row, size):
        turned = jnp.broadcast_to(row, (LANES, count)).T
        return wide([turned] * (size // LANES), 1)

    def total(picked, values):
        return jnp.sum(jnp.where(picked, values, 0), axis=0, keepdims=True)

    at, over, over_wide = along(count, 0), along(count, 1), along(wide_count, 1)
    before = at < over
    near_c, far_c = column(near, wide_count), column(far, wide_count)
    near_n, far_n = near_c[:, :count], far_c[:, :count]
    spot = near * COL_TILES + total((near_n == near) & before, 1)
    packed = total(column(spot, count) == over, at * model_blocks + far_n)
    equal = far_n == far
    rank = total(equal & before, 1)
    often = total(equal, 1)
    takes = jnp.where((rank == often - 1) & (often % 2 == 1), 2, 1)
    takes_c = column(takes, count)
    place_of = rank + total(far_n < far, takes_c)
    place_c = column(place_of * 2 + jnp.where(rank == 0, 1, 0), wide_count)
    code = (along(wide_count, 0) * near_size + near_c) * 2 + place_c % 2 - spare
    pair_code = total(place_c // 2 == over_wide, code) + spare
    ends = padded(model_blocks)
    block = along(ends, 1)
    until = total(far_c[:, :ends] <= block, takes_c[:, :ends])
    last = jnp.where(total(far_c[:, :ends] == block, 1) > 0, until // 2 - 1, -1)
    pair_far = pair_code // 2
    return (
        packed // model_blocks, packed % model_blocks,
        pair_far // near_size, pair_far % near_size, pair_code % 2, last,
    )


def block_kernel(
    sizes, up_rows, up_cols, down_rows, down_cols, ur, uc, dr, dc,
    act, cot, up, down,
    out, inp, ga_u, ga_d, gb_u, gb_d,
    x_all, flat_o, flat_i, xt_own, xt_mate, cot_own, cot_mate, u_all, d_all, hidden, ht_own, ht_mate, slope,
    pg_own, pg_mate, run, acc, parts_o, parts_i, held_r, held_l, stage, x_in, relay_x, relay_y, made, tables,
    load_sem, zs_sem, zr_sem, ms_sem, mr_sem, ts_sem, tr_sem, ws_sem, wr_sem, ys_sem, yr_sem, cs_sem, cr_sem,
    hs_sem, hr_sem, gs_sem, gr_sem, ls_sem, lr_sem, xs_sem, xr_sem, es_sem, er_sem, keep_sem, table_sem, out_sem,
    rs_sem, rr_sem, fs_sem, ts2_sem, tr2_sem, fs2_sem,
):
    n, chips, replicas = sizes
    z, r, c, y = place(sizes)
    f = r * 2 + c
    blocks = act.shape[1] // 128
    per = up.shape[0]
    part = per // replicas
    total_tiles = u_all.shape[0]
    hidden_blocks = slope.shape[0]
    chunk = blocks // CHUNKS
    weight_chunks = min(WEIGHT_CHUNKS, part)
    weight_size = part // weight_chunks
    pieces = min(PIECES, per)
    size = per // pieces
    relays = relay_pieces(n, pieces)
    at_end = jnp.logical_or(z == 0, z == n - 1)
    helps = jnp.logical_or(z == 1, z == n - 2)
    inner = jnp.where(z == 0, 1, n - 2)
    outer = jnp.where(z == 1, 0, n - 1)
    span = hidden_blocks // PARTS
    hidden_span = hidden_blocks // HIDDEN_PARTS
    features = (x_all, cot_own)
    weights = ((up, u_all), (down, d_all))
    mate = {"fsdp": r * 2 + 1 - c}

    loads = []
    for a, (src, full) in enumerate(((act, x_all), (cot, cot_own))):
        for b in range(blocks):
            pltpu.make_async_copy(
                src.at[:, pl.ds(b * 128, 128)], full.at[z * blocks + b], load_sem.at[a]
            ).start()
        own = full.at[pl.ds(z * blocks, blocks)]
        loads.append(pltpu.make_async_copy(own, own, load_sem.at[a]))
    weight_loads = []
    for a, (src, full) in enumerate(weights):
        copy = pltpu.make_async_copy(src, full.at[pl.ds(f * per, per)], load_sem.at[2 + a])
        copy.start()
        weight_loads.append(copy)
    hidden[hidden_blocks] = jnp.zeros(hidden.shape[1:], hidden.dtype)
    pg_own[hidden_blocks] = jnp.zeros(pg_own.shape[1:], pg_own.dtype)
    enter(sizes, relays)

    def part_shard(ref, s):
        return ref.at[pl.ds(s * blocks, blocks)]

    def shard(full, s, k):
        return full.at[pl.ds(s * blocks + k * chunk, chunk)]

    def line(a, s, k, way):
        piece = shard(features[a], z - way * s, k)
        w = 0 if way > 0 else 1
        return remote(
            piece, piece, zs_sem.at[a, w, s], zr_sem.at[a, w, s, k], {"tensor": z + way}
        )

    def line_sent(a, s, way):
        whole = part_shard(features[a], z - way * s)
        w = 0 if way > 0 else 1
        remote(
            whole, whole, zs_sem.at[a, w, s], zr_sem.at[a, w, s, 0], {"tensor": z + way}
        ).wait_send()

    def can_send(way):
        return z < n - 1 if way > 0 else z > 0

    def has(s, way):
        return z - s >= 0 if way > 0 else z + s <= n - 1

    def z_start(a):
        for k in range(CHUNKS):
            for way in (1, -1):

                @pl.when(can_send(way))
                def _():
                    line(a, 0, k, way).start()

    def mate_chunk(s, k, way):
        return remote(
            shard(cot_own, z - way * s, k), shard(cot_mate, z - way * s, k),
            ms_sem.at[0], mr_sem.at[0], mate,
        )

    def mate_chunks():
        return remote(cot_own, cot_mate, ms_sem.at[0], mr_sem.at[0], mate)

    def mate_turned(s, way):
        at = pl.ds((z - way * s) * blocks, blocks)
        return remote(xt_own.at[at], xt_mate.at[at], ts_sem.at[0], tr_sem.at[0], mate)

    def mate_turns():
        return remote(xt_own, xt_mate, ts_sem.at[0], tr_sem.at[0], mate)

    def turn(s, way):
        first = (z - way * s) * blocks

        @pl.loop(0, blocks // 2)
        def _(b):
            for i in range(2):
                xt_own[first + 2 * b + i] = x_all[first + 2 * b + i].T

        mate_turned(s, way).start()

    def z_event(a, s, k):
        for way in (1, -1):

            @pl.when(has(s, way))
            def _():
                line(a, s - 1, k, way).wait_recv()
                if s < n - 1:

                    @pl.when(can_send(way))
                    def _():
                        line(a, s, k, way).start()

                if a == 1:
                    mate_chunk(s, k, way).start()

    def turn_event(s):
        for way in (1, -1):

            @pl.when(has(s, way))
            def _():
                turn(s, way)

    def tile_range(full, r_of, q, k):
        return full.at[pl.ds((r_of * 2 + c) * per + q * part + k * weight_size, weight_size)]

    def from_chip(d):
        return lax.rem(r - d + chips, chips)

    def w_copy(a, d, k):
        src = weights[a][0].at[pl.ds(y * part + k * weight_size, weight_size)]
        return remote(
            src, tile_range(weights[a][1], r, y, k), ws_sem.at[a, d - 1], wr_sem.at[a, d - 1, k],
            {"fsdp": lax.rem(r + d, chips) * 2 + c},
        )

    def y_copy(a, d, e, k):
        piece = tile_range(weights[a][1], from_chip(d), y, k)
        return remote(
            piece, piece, ys_sem.at[a, d - 1, e - 1], yr_sem.at[a, d - 1, e - 1, k],
            {"dp": lax.rem(y + e, replicas)},
        )

    def core_copy(a, d, e, k):
        piece = tile_range(weights[a][1], from_chip(d), lax.rem(y - e + replicas, replicas), k)
        return remote(piece, piece, cs_sem.at[a], cr_sem.at[a], mate)

    def share(full, r_of, q):
        return full.at[pl.ds((r_of * 2 + c) * per + q * part, part)]

    def core_copies(a):
        whole = weights[a][1].at[pl.ds(0, chips * per)]
        return remote(whole, whole, cs_sem.at[a], cr_sem.at[a], mate)

    def weights_sent(a):
        core_copies(a).wait_send()
        for d in range(1, chips):
            remote(
                weights[a][0].at[pl.ds(y * part, part)], share(weights[a][1], r, y),
                ws_sem.at[a, d - 1], wr_sem.at[a, d - 1, 0], {"fsdp": lax.rem(r + d, chips) * 2 + c},
            ).wait_send()
            for e in range(1, replicas):
                whole = share(weights[a][1], from_chip(d), y)
                remote(
                    whole, whole, ys_sem.at[a, d - 1, e - 1], yr_sem.at[a, d - 1, e - 1, 0],
                    {"dp": lax.rem(y + e, replicas)},
                ).wait_send()

    def own_core(a):
        return remote(
            weights[a][0], weights[a][1].at[pl.ds(f * per, per)], cs_sem.at[a], cr_sem.at[a], mate
        )

    def w_event(a, k):
        for d in range(1, chips):
            w_copy(a, d, k).wait_recv()
            for e in range(1, replicas):
                y_copy(a, d, e, k).start()
            core_copy(a, d, 0, k).start()

    def y_event(a, k):
        for d in range(1, chips):
            for e in range(1, replicas):
                y_copy(a, d, e, k).wait_recv()
                core_copy(a, d, e, k).start()

    def weights_in(a):
        weight_loads[a].wait()
        core_copies(a).wait_recv()

    def hidden_mate(g):
        at = pl.ds(g * hidden_span, hidden_span)
        return remote(ht_own.at[at], ht_mate.at[at], hs_sem.at[0], hr_sem.at[0], mate)

    def hidden_mates():
        return remote(ht_own, ht_mate, hs_sem.at[0], hr_sem.at[0], mate)

    def hidden_part(g):
        @pl.loop(g * hidden_span, (g + 1) * hidden_span)
        def _(h):
            spots = [h * COL_TILES + k for k in range(COL_TILES)]
            pre = mm(
                wide([x_all[tables[0, 1, i]] for i in spots], 1),
                wide([u_all[tables[0, 0, i]] for i in spots], 0), 1, 0,
            )
            value, tangent = gelu_parts(pre)
            value = value.astype(jnp.bfloat16)
            hidden[h] = value
            ht_own[h] = value.T
            slope[h] = tangent

        hidden_mate(g).start()

    def grad_mate(g):
        at = pl.ds(g * span, span)
        return remote(pg_own.at[at], pg_mate.at[at], gs_sem.at[0], gr_sem.at[0], mate)

    def grad_mates():
        at = pl.ds(0, hidden_blocks)
        return remote(pg_own.at[at], pg_mate, gs_sem.at[0], gr_sem.at[0], mate)

    def slope_part(g):
        @pl.loop(g * span, (g + 1) * span)
        def _(h):
            spots = [h * COL_TILES + k for k in range(COL_TILES)]
            value = mm(
                wide([cot_own[tables[1, 1, i]] for i in spots], 1),
                wide([d_all[tables[1, 0, i]] for i in spots], 1), 1, 1,
            )
            pg_own[h] = (value * slope[h]).astype(jnp.bfloat16)

        grad_mate(g).start()

    parts = (parts_o, parts_i)
    outs = ((flat_o, out), (flat_i, inp))

    def out_copy(a):
        return pltpu.make_async_copy(outs[a][0], outs[a][1], out_sem.at[a])
    held = (held_r, held_l)
    pair_width = 4

    run_parts = (HIDDEN_PARTS, PARTS)

    def run_part(a, g):
        t = 1 - a
        left, right, cut = (hidden, d_all, 0) if a == 0 else (pg_own, u_all, 1)
        steps = run.shape[0] // run_parts[a] // pair_width
        if g == 0:
            acc[...] = jnp.zeros_like(acc)

        @pl.loop(g * steps, (g + 1) * steps)
        def _(b):
            total = acc[...]
            for i in [b * pair_width + k for k in range(pair_width)]:
                product = mm(
                    wide([left[tables[t, 3, 2 * i]], left[tables[t, 3, 2 * i + 1]]], 1),
                    wide([right[tables[t, 2, 2 * i]], right[tables[t, 2, 2 * i + 1]]], cut), 1, cut,
                )
                total = jnp.where(tables[t, 4, 2 * i] == 1, 0.0, total) + product
                run[i] = total.astype(jnp.bfloat16)
            acc[...] = total

    def fold(a, i, way, source):
        s = n - 1 - i if way > 0 else i
        k = 0 if way > 0 else 1
        src = part_shard(parts[a], s) if source else held[k].at[a, i]
        return remote(
            src, held[k].at[a, i], ls_sem.at[a, k, i], lr_sem.at[a, k, i], {"tensor": z + way}
        )

    def edge(way):
        return z == 0 if way > 0 else z == n - 1

    def sends(i, way):
        return n - 1 - i > z if way > 0 else i < z

    def settle(a):
        target = parts[a]

        @pl.loop(0, target.shape[0])
        def _(b):
            spot = tables[1 - a, 5, b]
            found = run[jnp.maximum(spot, 0)]
            target[b] = jnp.where(spot >= 0, found, jnp.zeros_like(found))

    def fold_start(a, i):
        for way in (1, -1):

            @pl.when(edge(way))
            def _():
                fold(a, i, way, True).start()

    def add_into(target, terms):
        @pl.loop(0, target.shape[0])
        def _(b):
            total = terms[0][b].astype(jnp.float32)
            for term_of in terms[1:]:
                total += term_of[b].astype(jnp.float32)
            target[b] = total.astype(target.dtype)

    def fold_event(a, t):
        for way in (1, -1):
            i = t - z if way > 0 else t - (n - 1 - z)
            s = n - 1 - i if way > 0 else i
            k = 0 if way > 0 else 1
            on_way = jnp.logical_and(i >= 0, sends(i, way))

            @pl.when(jnp.logical_and(on_way, jnp.logical_not(edge(way))))
            def _():
                fold(a, i, way, False).wait_recv()
                add_into(held[k].at[a, i], (held[k].at[a, i], part_shard(parts[a], s)))
                fold(a, i, way, False).start()

    def finish(a):
        mine = part_shard(parts[a], z)
        target = outs[a][0]

        def write(terms):
            for b in range(blocks):
                total = terms[0][b].astype(jnp.float32)
                for term_of in terms[1:]:
                    total += term_of[b].astype(jnp.float32)
                target[:, pl.ds(b * 128, 128)] = total.astype(target.dtype)

        @pl.when(z > 0)
        def _():
            fold(a, n - 1 - z, 1, False).wait_recv()

        @pl.when(z < n - 1)
        def _():
            fold(a, z, -1, False).wait_recv()

        @pl.when(z == 0)
        def _():
            write((mine, held_l.at[a, z]))

        @pl.when(z == n - 1)
        def _():
            write((mine, held_r.at[a, n - 1 - z]))

        @pl.when(jnp.logical_and(z > 0, z < n - 1))
        def _():
            write((mine, held_r.at[a, n - 1 - z], held_l.at[a, z]))

        out_copy(a).start()

    sums = (ga_d, ga_u)
    others = (gb_d, gb_u)

    def term(a, j):
        if a == 0:
            at, to = down_rows[j], down_cols[j]
            return mm(wide([ht_own[at], ht_mate[at]], 1), wide([cot_own[to], cot_mate[to]], 0), 1, 0)
        at, to = up_rows[j], up_cols[j]
        return mm(wide([xt_own[at], xt_mate[at]], 1), wide([pg_own[to], pg_mate[to]], 0), 1, 0)

    def first_tile(q, k):
        return (q * 2 + c) * per + k * size

    def x_copy(a, k, d):
        q = lax.rem(r + d, chips)
        at = pl.ds(k * size, size)
        return remote(
            stage.at[a, d - 1, at], x_in.at[a, d - 1, at], xs_sem.at[a, d - 1], xr_sem.at[a, k, d - 1],
            {"fsdp": q * 2 + c},
        )

    def hand_over(a, first_piece, end):
        @pl.loop(first_piece, end)
        def _(k):
            for d in range(1, chips):
                first = first_tile(lax.rem(r + d, chips), k)
                values = [term(a, first + i) for i in range(size)]
                for i in range(size):
                    stage[a, d - 1, k * size + i] = values[i].astype(jnp.bfloat16)
                x_copy(a, k, d).start()

    def done_piece(a, k):
        return x_in.at[a, 0, pl.ds(k * size, size)]

    def e_copy(a, k, e):
        return remote(
            done_piece(a, k), others[a].at[e - 1, pl.ds(k * size, size)],
            es_sem.at[a, e - 1], er_sem.at[a, e - 1], {"dp": lax.rem(y + e, replicas)},
        )

    def keep_copy(a, k):
        return pltpu.make_async_copy(
            done_piece(a, k), sums[a].at[pl.ds(k * size, size)], keep_sem.at[a]
        )

    def piece(k):
        return pl.ds(k * size, size)

    def x_out(d, where):
        return remote(
            stage.at[0, d - 1, where], relay_x.at[d - 1, where], rs_sem.at[d - 1], rr_sem.at[0, d - 1],
            {"fsdp": lax.rem(r + d, chips) * 2 + c, "tensor": inner},
        )

    def x_out_piece(k, d):
        return remote(
            stage.at[0, d - 1, piece(k)], relay_x.at[d - 1, piece(k)], rs_sem.at[d - 1], rr_sem.at[k, d - 1],
            {"fsdp": lax.rem(r + d, chips) * 2 + c, "tensor": inner},
        )

    def x_on(d, where, recv_sem):
        return remote(
            relay_x.at[d - 1, where], x_in.at[0, d - 1, where], fs_sem.at[d - 1], recv_sem, {"tensor": outer}
        )

    def y_out(e, where, recv_sem):
        return remote(
            x_in.at[0, 0, where], relay_y.at[e - 1, where], ts2_sem.at[e - 1], recv_sem,
            {"dp": lax.rem(y + e, replicas), "tensor": inner},
        )

    def y_on(e, where):
        return remote(
            relay_y.at[e - 1, where], others[0].at[e - 1, where], fs2_sem.at[e - 1], er_sem.at[0, e - 1],
            {"tensor": outer},
        )

    def hand_relays():
        for k in range(relays):
            for d in range(1, chips):
                first = first_tile(lax.rem(r + d, chips), k)
                values = [term(0, first + i) for i in range(size)]
                for i in range(size):
                    stage[0, d - 1, k * size + i] = values[i].astype(jnp.bfloat16)
                x_out_piece(k, d).start()

    def pass_x(k):
        @pl.when(helps)
        def _():
            for d in range(1, chips):
                x_out_piece(k, d).wait_recv()
                x_on(d, piece(k), xr_sem.at[0, k, d - 1]).start()

    def pass_y(k):
        @pl.when(helps)
        def _():
            for e in range(1, replicas):
                y_out(e, piece(k), tr2_sem.at[k, e - 1]).wait_recv()
                y_on(e, piece(k)).start()

    def relayed_event(k):
        x_event(0, k, True)

    def x_events(a, first_piece, end):
        pl.loop(first_piece, end)(functools.partial(x_event, a))

    def x_event(a, k, relayed=False):
        first = first_tile(r, k)
        values = [term(a, first + i) for i in range(size)]
        for d in range(1, chips):
            x_copy(a, k, d).wait_recv()
        for i in range(size):
            total = values[i]
            for d in range(1, chips):
                total += x_in[a, d - 1, k * size + i].astype(jnp.float32)
            x_in[a, 0, k * size + i] = total.astype(jnp.bfloat16)
        for e in range(1, replicas):
            if relayed:
                y_out(e, piece(k), tr2_sem.at[k, e - 1]).start()
            else:
                e_copy(a, k, e).start()
        keep_copy(a, k).start()

    def start_all():
        loads[0].wait()
        z_start(0)
        for a in range(2):
            for k in range(weight_chunks):
                for d in range(1, chips):
                    w_copy(a, d, k).start()
        for a in range(2):
            own_core(a).start()
        loads[1].wait()
        for k in range(CHUNKS):
            mate_chunk(0, k, 1).start()

    def table_copy(t):
        return pltpu.make_async_copy(made.at[t], tables.at[t], table_sem.at[t])

    def make_table(t):
        near, far = ((uc, ur), (dr, dc))[t]
        for row, values in enumerate(tables_of(near[...], far[...], n * blocks)):
            made[t, pl.ds(row, 1), pl.ds(0, values.shape[1])] = values
        table_copy(t).start()

    def table_ready(t):
        table_copy(t).wait()

    def cot_ready():
        mate_chunks().wait_recv()
        hidden_mates().wait_recv()

    def grads_ready():
        mate_turns().wait_recv()
        grad_mates().wait_recv()

    chunk_time = SHARD_TIME / CHUNKS
    piece_time = 4 * SHARD_TIME / pieces
    up_in = 2.3 + (weight_chunks + 1.2) * WEIGHT_TIME
    down_in = 2.3 + (2 * weight_chunks + 1.2) * WEIGHT_TIME
    group = max(pieces // 8, 1)
    end_cot_in = 4.0 + 2 * (n - 1) * SHARD_TIME
    end_inp_settle = end_cot_in + INP_LATE

    def order(ends):
        plan = []

        def at(time, work, *args):
            plan.append((time, functools.partial(work, *args)))

        at(0.0, start_all)
        for t in range(2):
            at(10.2 + 5.65 * t, make_table, t)
            at(24.0, table_ready, t)
        at(5.7, turn, 0, 1)
        hops = n - 1 if ends else max(n - 2, 1)
        for s in range(1, n):
            for k in range(CHUNKS):
                at(2.0 + ((s - 1) * CHUNKS + k + 1) * chunk_time, z_event, 0, s, k)
                at(2.0 + hops * SHARD_TIME + ((s - 1) * CHUNKS + k + 1) * chunk_time, z_event, 1, s, k)
            at(2.0 + s * SHARD_TIME + 0.1 + chunk_time, turn_event, s)
        at(2.05 + max(n - 2, 0) * SHARD_TIME, z_start, 1)
        for a in range(2):
            for k in range(weight_chunks):
                when = 2.2 + (a * weight_chunks + k + 1) * WEIGHT_TIME
                at(when, w_event, a, k)
                at(when + 1.2 * WEIGHT_TIME, y_event, a, k)
        at(up_in + 2.0, weights_in, 0)
        at(down_in + 2.0, weights_in, 1)
        hidden_from = max(2.0 + hops * SHARD_TIME, up_in + 2.0) + 0.5
        hidden_in = hidden_from + 3.0 * HIDDEN_PARTS
        for g in range(HIDDEN_PARTS):
            at(hidden_from + 3.0 * g, hidden_part, g)
        out_from = max(hidden_in, down_in + 2.0) + 0.5
        out_settle = out_from + 2.4 * HIDDEN_PARTS
        for g in range(HIDDEN_PARTS):
            at(out_from + 2.4 * g, run_part, 0, g)
        at(out_settle, settle, 0)
        cot_in = 2.0 + 2 * hops * SHARD_TIME + 1.0
        cot_in = max(cot_in, out_settle if ends else hidden_in) + 1.0
        away = relays if ends else 0
        at(cot_in, cot_ready)
        if away:
            at(cot_in + 0.05, hand_relays)
        for j, k in enumerate(range(away, pieces, group)):
            at(cot_in + 0.1 + 1.2 * j, hand_over, 0, k, min(k + group, pieces))
        slope_from = max(cot_in + 9.0, out_settle + 0.5)
        for g in range(PARTS):
            at(slope_from + 1.5 * g, slope_part, g)
        up_from = slope_from + 1.5 * PARTS + 1.0
        at(up_from, grads_ready)
        first_groups = 3 if ends else 8
        inp_from = up_from + 0.1 + 1.4 * first_groups
        for j, k in enumerate(range(0, pieces, group)):
            late = 0.0 if j < first_groups else 0.7
            at(up_from + 0.1 + 1.4 * j + late, hand_over, 1, k, min(k + group, pieces))
        for g in range(PARTS):
            at(inp_from + 1.5 * g, run_part, 1, g)
        inp_settle = inp_from + 1.5 * PARTS + (3.0 if ends else 0.0)
        at(inp_settle, settle, 1)
        late = end_cot_in + FOLD_LATE
        for i in range(n - 1):
            at(max(out_settle, late if i and relays else 0.0) + 0.1, fold_start, 0, i)
            at(max(inp_settle, end_cot_in + INP_REST if i and relays else 0.0) + 0.1, fold_start, 1, i)
        for t in range(1, n - 1):
            begin = max(out_settle, late + 4.0 if t > 1 and relays else 0.0)
            at(begin + 1.0 + t * SHARD_TIME, fold_event, 0, t)
            at(end_inp_settle + 1.0 + t * SHARD_TIME + (8.0 if t > 1 else 0.0), fold_event, 1, t)
        at(late + 20.0 + (n - 1) * SHARD_TIME, finish, 0)
        at(FINISH + end_inp_settle + 3.0 + (n - 1) * SHARD_TIME, finish, 1)
        for k in range(relays):
            if ends:
                at(end_cot_in + RELAYED + piece_time * (k + 1), relayed_event, k)
            else:
                at(end_cot_in + PASS_X + piece_time * (k + 1), pass_x, k)
                at(end_cot_in + PASS_Y + piece_time * (k + 1), pass_y, k)
        for a in range(2):
            for k in range(0 if a else away, pieces):
                when = cot_in + 2.2 + piece_time * (a * pieces + k - away + 1)
                at(max(when, up_from + 0.2) if a else when, x_event, a, k)
        plan.sort(key=lambda item: item[0])
        steps = []
        for _, work in plan:
            if work.func is x_event:
                a, k = work.args
                if steps and steps[-1].func is x_events and steps[-1].args[::2] == (a, k):
                    work = functools.partial(x_events, a, steps.pop().args[1], k + 1)
                else:
                    work = functools.partial(x_events, a, k, k + 1)
            steps.append(work)
        return steps

    def run_all(steps):
        for work in steps:
            work()

    end_steps, mid_steps = order(True), order(False)
    if relays:
        shared = 0
        for one, other in zip(end_steps, mid_steps):
            if (one.func, one.args) != (other.func, other.args):
                break
            shared += 1
        run_all(end_steps[:shared])
        pl.when(at_end)(functools.partial(run_all, end_steps[shared:]))
        pl.when(jnp.logical_not(at_end))(functools.partial(run_all, mid_steps[shared:]))
    else:
        run_all(end_steps)

    mate_chunks().wait_send()
    mate_turns().wait_send()
    for a in range(2):
        out_copy(a).wait()
        weights_sent(a)
        for way in (1, -1):
            for s in range(n - 1):

                @pl.when(jnp.logical_and(can_send(way), has(s, way)))
                def _():
                    line_sent(a, s, way)

        for i in range(n - 1):
            for way in (1, -1):

                @pl.when(sends(i, way))
                def _():
                    fold(a, i, way, False).wait_send()

    hidden_mates().wait_send()
    grad_mates().wait_send()
    def sent(a, first):
        where = pl.ds(first * size, per - first * size)
        for d in range(1, chips):
            remote(
                stage.at[a, d - 1, where], x_in.at[a, d - 1, where], xs_sem.at[a, d - 1], xr_sem.at[a, 0, d - 1],
                {"fsdp": lax.rem(r + d, chips) * 2 + c},
            ).wait_send()
        for e in range(1, replicas):
            remote(
                x_in.at[a, 0, where], others[a].at[e - 1, where], es_sem.at[a, e - 1], er_sem.at[a, e - 1],
                {"dp": lax.rem(y + e, replicas)},
            ).wait_send()

    for a in range(2):
        pltpu.make_async_copy(x_in.at[a, 0], sums[a], keep_sem.at[a]).wait()
        for e in range(1, replicas):
            remote(
                x_in.at[a, 0], others[a].at[e - 1], es_sem.at[a, e - 1], er_sem.at[a, e - 1],
                {"dp": lax.rem(y + e, replicas)},
            ).wait_recv()
    sent(1, 0)
    if not relays:
        sent(0, 0)
    else:
        relayed = pl.ds(0, relays * size)

        @pl.when(at_end)
        def _():
            sent(0, relays)
            for d in range(1, chips):
                x_out(d, relayed).wait_send()
            for e in range(1, replicas):
                y_out(e, relayed, tr2_sem.at[0, e - 1]).wait_send()

        @pl.when(jnp.logical_not(at_end))
        def _():
            sent(0, 0)

        @pl.when(helps)
        def _():
            for d in range(1, chips):
                x_on(d, relayed, xr_sem.at[0, 0, d - 1]).wait_send()
            for e in range(1, replicas):
                y_on(e, relayed).wait_send()


def run_block(sizes, lists, activations, cotangent, up_tiles, down_tiles):
    n, chips, replicas = sizes
    rows, features = activations.shape
    blocks = features // 128
    per = up_tiles.shape[0]
    total_tiles = 2 * chips * per
    hidden_blocks = total_tiles // COL_TILES
    model_blocks = n * blocks
    pairs = (total_tiles + model_blocks) // 2
    part = per // replicas
    weight_chunks = min(WEIGHT_CHUNKS, part)
    pieces = min(PIECES, per)
    relays = max(relay_pieces(n, pieces), 1)
    relayed = relays * per // pieces
    kind = jnp.bfloat16
    dma = pltpu.SemaphoreType.DMA
    vmem = pl.BlockSpec(memory_space=pltpu.VMEM)
    smem = pl.BlockSpec(memory_space=pltpu.SMEM)
    anywhere = pl.BlockSpec(memory_space=pl.ANY)

    def held(*shape):
        return pltpu.VMEM(shape + (rows, 128), kind)

    def twice(*shape):
        return [dma(shape), dma(shape)]

    return pl.pallas_call(
        functools.partial(block_kernel, sizes),
        out_shape=(
            [jax.ShapeDtypeStruct((rows, features), kind)] * 2
            + [jax.ShapeDtypeStruct((per, 128, 128), kind)] * 2
            + [jax.ShapeDtypeStruct((replicas - 1, per, 128, 128), kind)] * 2
        ),
        in_specs=[smem] * 4 + [vmem] * 4 + [anywhere] * 4,
        out_specs=[anywhere] * 6,
        scratch_shapes=[
            held(model_blocks),
            pltpu.VMEM((rows, features), kind),
            pltpu.VMEM((rows, features), kind),
            pltpu.VMEM((model_blocks, 128, rows), kind),
            pltpu.VMEM((model_blocks, 128, rows), kind),
            held(model_blocks),
            held(model_blocks),
            pltpu.VMEM((total_tiles, 128, 128), kind),
            pltpu.VMEM((total_tiles, 128, 128), kind),
            held(hidden_blocks + 1),
            pltpu.VMEM((hidden_blocks, 128, rows), kind),
            pltpu.VMEM((hidden_blocks, 128, rows), kind),
            pltpu.VMEM((hidden_blocks, rows, 128), jnp.float32),
            held(hidden_blocks + 1),
            held(hidden_blocks),
            held(pairs),
            pltpu.VMEM((rows, 128), jnp.float32),
            held(model_blocks),
            held(model_blocks),
            held(2, n - 1, blocks),
            held(2, n - 1, blocks),
            pltpu.VMEM((2, chips - 1, per, 128, 128), kind),
            pltpu.VMEM((2, chips - 1, per, 128, 128), kind),
            pltpu.VMEM((chips - 1, relayed, 128, 128), kind),
            pltpu.VMEM((replicas - 1, relayed, 128, 128), kind),
            pltpu.VMEM((2, 8, padded(total_tiles + model_blocks)), jnp.int32),
            pltpu.SMEM((2, 8, padded(total_tiles + model_blocks)), jnp.int32),
            dma((4,)),
            dma((2, 2, n - 1)),
            dma((2, 2, n - 1, CHUNKS)),
            *twice(1),
            *twice(1),
            dma((2, chips - 1)),
            dma((2, chips - 1, weight_chunks)),
            dma((2, chips - 1, replicas - 1)),
            dma((2, chips - 1, replicas - 1, weight_chunks)),
            *twice(2),
            *twice(1),
            *twice(1),
            *twice(2, 2, n - 1),
            dma((2, chips - 1)),
            dma((2, pieces, chips - 1)),
            *twice(2, replicas - 1),
            dma((2,)),
            dma((2,)),
            dma((2,)),
            dma((chips - 1,)),
            dma((relays, chips - 1)),
            dma((chips - 1,)),
            dma((replicas - 1,)),
            dma((relays, replicas - 1)),
            dma((replicas - 1,)),
        ],
        compiler_params=pltpu.CompilerParams(
            collective_id=0, has_side_effects=True, vmem_limit_bytes=67043328
        ),
        name="block_all",
    )(*(v[:, 0] for v in lists), *(v.T for v in lists), activations, cotangent, up_tiles, down_tiles)


def total_kernel(ga_u, gb_u, ga_d, gb_d, out_in, inp_in, up_grad, down_grad, out, inp):
    for one, more, target in ((ga_u, gb_u, up_grad), (ga_d, gb_d, down_grad)):
        total = one[...].astype(jnp.float32)
        for e in range(more.shape[0]):
            total += more[e].astype(jnp.float32)
        target[...] = total
    out[...] = out_in[...]
    inp[...] = inp_in[...]


def totals(ga_u, gb_u, ga_d, gb_d, out, inp):
    per = ga_u.shape[0]
    step = max(per // 2, 1)
    rows, features = out.shape
    one = pl.BlockSpec((step, 128, 128), lambda i: (i, 0, 0))
    more = pl.BlockSpec((gb_u.shape[0], step, 128, 128), lambda i: (0, i, 0, 0))
    flat = pl.BlockSpec((rows * step // per, features), lambda i: (i, 0))
    return pl.pallas_call(
        total_kernel,
        grid=(per // step,),
        out_shape=(
            [jax.ShapeDtypeStruct(ga_u.shape, jnp.float32)] * 2 + [jax.ShapeDtypeStruct(out.shape, out.dtype)] * 2
        ),
        in_specs=[one, more, one, more, flat, flat],
        out_specs=[one, one, flat, flat],
        name="totals",
    )(ga_u, gb_u, ga_d, gb_d, out, inp)


def body(sizes, activations, cotangent, up_tiles, down_tiles, up_rows, up_cols, down_rows, down_cols):
    lists = (up_rows, up_cols, down_rows, down_cols)
    out, inp, ga_u, ga_d, gb_u, gb_d = run_block(
        sizes, lists, activations, cotangent, up_tiles, down_tiles
    )
    up_grad, down_grad, out, inp = totals(ga_u, gb_u, ga_d, gb_d, out, inp)
    return out, inp, up_grad, down_grad


def solution(mesh):
    sizes = (mesh.shape["tensor"], mesh.shape["fsdp"] // 2, mesh.shape["dp"])
    in_specs = (
        P(("dp", "fsdp"), "tensor"),
        P(("dp", "fsdp"), "tensor"),
        P(("fsdp", "tensor"), None, None),
        P(("fsdp", "tensor"), None, None),
        P(None, "tensor"),
        P(None, "tensor"),
        P(None, "tensor"),
        P(None, "tensor"),
    )
    out_specs = (
        P(("dp", "fsdp"), "tensor"),
        P(("dp", "fsdp"), "tensor"),
        P(("fsdp", "tensor"), None, None),
        P(("fsdp", "tensor"), None, None),
    )
    return jax.shard_map(
        functools.partial(body, sizes), mesh=mesh, in_specs=in_specs, out_specs=out_specs,
        check_vma=False,
    )
```

```python
import functools

import jax
import jax.numpy as jnp
from jax import lax
from jax.experimental import pallas as pl
from jax.experimental.pallas import tpu as pltpu
from jax.sharding import PartitionSpec as P

MESH = pl.DeviceIdType.MESH
COL_TILES = 8
PIECES = 16
CHUNKS = 2
WEIGHT_CHUNKS = 8
PARTS = 8
HIDDEN_PARTS = 4
RELAY = 2
INP_REST = 55.0
FINISH = 100.0
INP_LATE = 48.0
FOLD_LATE = 2.0
PASS_X = 24.0
RELAYED = 42.0
PASS_Y = 54.0
LANES = 128

SHARD_TIME = 11.3
WEIGHT_TIME = 2.8
PIECE_SHARE = 2

inv_root_two = 0.7071067811865476
inv_root_tau = 0.3989422804014327


def gelu_parts(values):
    normal_cdf = 0.5 * (1.0 + lax.erf(values * inv_root_two))
    density = inv_root_tau * jnp.exp(-0.5 * values * values)
    return (values * normal_cdf, normal_cdf + values * density)


def mm(a, b, ca, cb):
    return lax.dot_general(a, b, (((ca,), (cb,)), ((), ())), preferred_element_type=jnp.float32)


def wide(blocks, axis):
    return jnp.concatenate(blocks, axis=axis)


def remote(src, dst, send_sem, recv_sem, where):
    return pltpu.make_async_remote_copy(
        src_ref=src, dst_ref=dst, send_sem=send_sem, recv_sem=recv_sem,
        device_id=where, device_id_type=MESH,
    )


def place(sizes):
    n, chips, replicas = sizes
    z = lax.axis_index("tensor")
    f = lax.axis_index("fsdp")
    y = lax.axis_index("dp")
    return z, f // 2, f % 2, y


def relay_pieces(n, pieces):
    return min(RELAY, pieces // 4) if n >= 4 else 0


def enter(sizes, relays):
    n, chips, replicas = sizes
    z, r, c, y = place(sizes)
    barrier = pltpu.get_barrier_semaphore()

    def greet(where):
        pl.semaphore_signal(barrier, inc=1, device_id=where, device_id_type=MESH)

    @pl.when(z < n - 1)
    def _():
        greet({"tensor": z + 1})

    @pl.when(z > 0)
    def _():
        greet({"tensor": z - 1})

    greet({"fsdp": r * 2 + 1 - c})
    for d in range(1, chips):
        greet({"fsdp": lax.rem(r + d, chips) * 2 + c})
    for e in range(1, replicas):
        greet({"dp": lax.rem(y + e, replicas)})
    others = (chips - 1) + (replicas - 1)
    awaited = jnp.where(z < n - 1, 1, 0) + jnp.where(z > 0, 1, 0) + 1 + others
    if relays:

        @pl.when(jnp.logical_or(z == 1, z == n - 2))
        def _():
            outer = jnp.where(z == 1, 0, n - 1)
            for d in range(1, chips):
                greet({"fsdp": lax.rem(r + d, chips) * 2 + c, "tensor": outer})
            for e in range(1, replicas):
                greet({"dp": lax.rem(y + e, replicas), "tensor": outer})

        awaited += jnp.where(jnp.logical_or(z == 0, z == n - 1), others, 0)
    pl.semaphore_wait(barrier, awaited)


def padded(size):
    return -(-size // LANES) * LANES


def tables_of(near, far, model_blocks):
    count = near.shape[1]
    near_size = count // COL_TILES + 1
    spare = (near_size - 1) * 2
    wide_count = padded(count + model_blocks)

    def along(size, axis):
        return lax.broadcasted_iota(jnp.int32, (count, size), axis)

    def column(row, size):
        turned = jnp.broadcast_to(row, (LANES, count)).T
        return wide([turned] * (size // LANES), 1)

    def total(picked, values):
        return jnp.sum(jnp.where(picked, values, 0), axis=0, keepdims=True)

    at, over, over_wide = along(count, 0), along(count, 1), along(wide_count, 1)
    before = at < over
    near_c, far_c = column(near, wide_count), column(far, wide_count)
    near_n, far_n = near_c[:, :count], far_c[:, :count]
    spot = near * COL_TILES + total((near_n == near) & before, 1)
    packed = total(column(spot, count) == over, at * model_blocks + far_n)
    equal = far_n == far
    rank = total(equal & before, 1)
    often = total(equal, 1)
    takes = jnp.where((rank == often - 1) & (often % 2 == 1), 2, 1)
    takes_c = column(takes, count)
    place_of = rank + total(far_n < far, takes_c)
    place_c = column(place_of * 2 + jnp.where(rank == 0, 1, 0), wide_count)
    code = (along(wide_count, 0) * near_size + near_c) * 2 + place_c % 2 - spare
    pair_code = total(place_c // 2 == over_wide, code) + spare
    ends = padded(model_blocks)
    block = along(ends, 1)
    until = total(far_c[:, :ends] <= block, takes_c[:, :ends])
    last = jnp.where(total(far_c[:, :ends] == block, 1) > 0, until // 2 - 1, -1)
    pair_far = pair_code // 2
    return (
        packed // model_blocks, packed % model_blocks,
        pair_far // near_size, pair_far % near_size, pair_code % 2, last,
    )


def block_kernel(
    sizes, up_rows, up_cols, down_rows, down_cols, ur, uc, dr, dc,
    act, cot, up, down,
    out, inp, ga_u, ga_d, gb_u, gb_d,
    x_all, flat_o, flat_i, xt_own, xt_mate, cot_own, cot_mate, u_all, d_all, hidden, ht_own, ht_mate, slope,
    pg_own, pg_mate, run, acc, parts_o, parts_i, held_r, held_l, stage, x_in, relay_x, relay_y, made, tables,
    load_sem, zs_sem, zr_sem, ms_sem, mr_sem, ts_sem, tr_sem, ws_sem, wr_sem, ys_sem, yr_sem, cs_sem, cr_sem,
    hs_sem, hr_sem, gs_sem, gr_sem, ls_sem, lr_sem, xs_sem, xr_sem, es_sem, er_sem, keep_sem, table_sem, out_sem,
    rs_sem, rr_sem, fs_sem, ts2_sem, tr2_sem, fs2_sem,
):
    n, chips, replicas = sizes
    z, r, c, y = place(sizes)
    f = r * 2 + c
    blocks = act.shape[1] // 128
    per = up.shape[0]
    part = per // replicas
    total_tiles = u_all.shape[0]
    hidden_blocks = slope.shape[0]
    chunk = blocks // CHUNKS
    weight_chunks = min(WEIGHT_CHUNKS, part)
    weight_size = part // weight_chunks
    pieces = min(PIECES, per)
    size = per // pieces
    relays = relay_pieces(n, pieces)
    at_end = jnp.logical_or(z == 0, z == n - 1)
    helps = jnp.logical_or(z == 1, z == n - 2)
    inner = jnp.where(z == 0, 1, n - 2)
    outer = jnp.where(z == 1, 0, n - 1)
    span = hidden_blocks // PARTS
    hidden_span = hidden_blocks // HIDDEN_PARTS
    features = (x_all, cot_own)
    weights = ((up, u_all), (down, d_all))
    mate = {"fsdp": r * 2 + 1 - c}

    loads = []
    for a, (src, full) in enumerate(((act, x_all), (cot, cot_own))):
        for b in range(blocks):
            pltpu.make_async_copy(
                src.at[:, pl.ds(b * 128, 128)], full.at[z * blocks + b], load_sem.at[a]
            ).start()
        own = full.at[pl.ds(z * blocks, blocks)]
        loads.append(pltpu.make_async_copy(own, own, load_sem.at[a]))
    weight_loads = []
    for a, (src, full) in enumerate(weights):
        copy = pltpu.make_async_copy(src, full.at[pl.ds(f * per, per)], load_sem.at[2 + a])
        copy.start()
        weight_loads.append(copy)
    hidden[hidden_blocks] = jnp.zeros(hidden.shape[1:], hidden.dtype)
    pg_own[hidden_blocks] = jnp.zeros(pg_own.shape[1:], pg_own.dtype)
    enter(sizes, relays)

    def part_shard(ref, s):
        return ref.at[pl.ds(s * blocks, blocks)]

    def shard(full, s, k):
        return full.at[pl.ds(s * blocks + k * chunk, chunk)]

    def line(a, s, k, way):
        piece = shard(features[a], z - way * s, k)
        w = 0 if way > 0 else 1
        return remote(
            piece, piece, zs_sem.at[a, w, s], zr_sem.at[a, w, s, k], {"tensor": z + way}
        )

    def line_sent(a, s, way):
        whole = part_shard(features[a], z - way * s)
        w = 0 if way > 0 else 1
        remote(
            whole, whole, zs_sem.at[a, w, s], zr_sem.at[a, w, s, 0], {"tensor": z + way}
        ).wait_send()

    def can_send(way):
        return z < n - 1 if way > 0 else z > 0

    def has(s, way):
        return z - s >= 0 if way > 0 else z + s <= n - 1

    def z_start(a):
        for k in range(CHUNKS):
            for way in (1, -1):

                @pl.when(can_send(way))
                def _():
                    line(a, 0, k, way).start()

    def mate_chunk(s, k, way):
        return remote(
            shard(cot_own, z - way * s, k), shard(cot_mate, z - way * s, k),
            ms_sem.at[0], mr_sem.at[0], mate,
        )

    def mate_chunks():
        return remote(cot_own, cot_mate, ms_sem.at[0], mr_sem.at[0], mate)

    def mate_turned(s, way):
        at = pl.ds((z - way * s) * blocks, blocks)
        return remote(xt_own.at[at], xt_mate.at[at], ts_sem.at[0], tr_sem.at[0], mate)

    def mate_turns():
        return remote(xt_own, xt_mate, ts_sem.at[0], tr_sem.at[0], mate)

    def turn(s, way):
        first = (z - way * s) * blocks

        @pl.loop(0, blocks // 2)
        def _(b):
            for i in range(2):
                xt_own[first + 2 * b + i] = x_all[first + 2 * b + i].T

        mate_turned(s, way).start()

    def z_event(a, s, k):
        for way in (1, -1):

            @pl.when(has(s, way))
            def _():
                line(a, s - 1, k, way).wait_recv()
                if s < n - 1:

                    @pl.when(can_send(way))
                    def _():
                        line(a, s, k, way).start()

                if a == 1:
                    mate_chunk(s, k, way).start()

    def turn_event(s):
        for way in (1, -1):

            @pl.when(has(s, way))
            def _():
                turn(s, way)

    def tile_range(full, r_of, q, k):
        return full.at[pl.ds((r_of * 2 + c) * per + q * part + k * weight_size, weight_size)]

    def from_chip(d):
        return lax.rem(r - d + chips, chips)

    def w_copy(a, d, k):
        src = weights[a][0].at[pl.ds(y * part + k * weight_size, weight_size)]
        return remote(
            src, tile_range(weights[a][1], r, y, k), ws_sem.at[a, d - 1], wr_sem.at[a, d - 1, k],
            {"fsdp": lax.rem(r + d, chips) * 2 + c},
        )

    def y_copy(a, d, e, k):
        piece = tile_range(weights[a][1], from_chip(d), y, k)
        return remote(
            piece, piece, ys_sem.at[a, d - 1, e - 1], yr_sem.at[a, d - 1, e - 1, k],
            {"dp": lax.rem(y + e, replicas)},
        )

    def core_copy(a, d, e, k):
        piece = tile_range(weights[a][1], from_chip(d), lax.rem(y - e + replicas, replicas), k)
        return remote(piece, piece, cs_sem.at[a], cr_sem.at[a], mate)

    def share(full, r_of, q):
        return full.at[pl.ds((r_of * 2 + c) * per + q * part, part)]

    def core_copies(a):
        whole = weights[a][1].at[pl.ds(0, chips * per)]
        return remote(whole, whole, cs_sem.at[a], cr_sem.at[a], mate)

    def weights_sent(a):
        core_copies(a).wait_send()
        for d in range(1, chips):
            remote(
                weights[a][0].at[pl.ds(y * part, part)], share(weights[a][1], r, y),
                ws_sem.at[a, d - 1], wr_sem.at[a, d - 1, 0], {"fsdp": lax.rem(r + d, chips) * 2 + c},
            ).wait_send()
            for e in range(1, replicas):
                whole = share(weights[a][1], from_chip(d), y)
                remote(
                    whole, whole, ys_sem.at[a, d - 1, e - 1], yr_sem.at[a, d - 1, e - 1, 0],
                    {"dp": lax.rem(y + e, replicas)},
                ).wait_send()

    def own_core(a):
        return remote(
            weights[a][0], weights[a][1].at[pl.ds(f * per, per)], cs_sem.at[a], cr_sem.at[a], mate
        )

    def w_event(a, k):
        for d in range(1, chips):
            w_copy(a, d, k).wait_recv()
            for e in range(1, replicas):
                y_copy(a, d, e, k).start()
            core_copy(a, d, 0, k).start()

    def y_event(a, k):
        for d in range(1, chips):
            for e in range(1, replicas):
                y_copy(a, d, e, k).wait_recv()
                core_copy(a, d, e, k).start()

    def weights_in(a):
        weight_loads[a].wait()
        core_copies(a).wait_recv()

    def hidden_mate(g):
        at = pl.ds(g * hidden_span, hidden_span)
        return remote(ht_own.at[at], ht_mate.at[at], hs_sem.at[0], hr_sem.at[0], mate)

    def hidden_mates():
        return remote(ht_own, ht_mate, hs_sem.at[0], hr_sem.at[0], mate)

    def hidden_part(g):
        @pl.loop(g * hidden_span, (g + 1) * hidden_span)
        def _(h):
            spots = [h * COL_TILES + k for k in range(COL_TILES)]
            pre = mm(
                wide([x_all[tables[0, 1, i]] for i in spots], 1),
                wide([u_all[tables[0, 0, i]] for i in spots], 0), 1, 0,
            )
            value, tangent = gelu_parts(pre)
            value = value.astype(jnp.bfloat16)
            hidden[h] = value
            ht_own[h] = value.T
            slope[h] = tangent

        hidden_mate(g).start()

    def grad_mate(g):
        at = pl.ds(g * span, span)
        return remote(pg_own.at[at], pg_mate.at[at], gs_sem.at[0], gr_sem.at[0], mate)

    def grad_mates():
        at = pl.ds(0, hidden_blocks)
        return remote(pg_own.at[at], pg_mate, gs_sem.at[0], gr_sem.at[0], mate)

    def slope_part(g):
        @pl.loop(g * span, (g + 1) * span)
        def _(h):
            spots = [h * COL_TILES + k for k in range(COL_TILES)]
            value = mm(
                wide([cot_own[tables[1, 1, i]] for i in spots], 1),
                wide([d_all[tables[1, 0, i]] for i in spots], 1), 1, 1,
            )
            pg_own[h] = (value * slope[h]).astype(jnp.bfloat16)

        grad_mate(g).start()

    parts = (parts_o, parts_i)
    outs = ((flat_o, out), (flat_i, inp))

    def out_copy(a):
        return pltpu.make_async_copy(outs[a][0], outs[a][1], out_sem.at[a])
    held = (held_r, held_l)
    pair_width = 4

    run_parts = (HIDDEN_PARTS, PARTS)

    def run_part(a, g):
        t = 1 - a
        left, right, cut = (hidden, d_all, 0) if a == 0 else (pg_own, u_all, 1)
        steps = run.shape[0] // run_parts[a] // pair_width
        if g == 0:
            acc[...] = jnp.zeros_like(acc)

        @pl.loop(g * steps, (g + 1) * steps)
        def _(b):
            total = acc[...]
            for i in [b * pair_width + k for k in range(pair_width)]:
                product = mm(
                    wide([left[tables[t, 3, 2 * i]], left[tables[t, 3, 2 * i + 1]]], 1),
                    wide([right[tables[t, 2, 2 * i]], right[tables[t, 2, 2 * i + 1]]], cut), 1, cut,
                )
                total = jnp.where(tables[t, 4, 2 * i] == 1, 0.0, total) + product
                run[i] = total.astype(jnp.bfloat16)
            acc[...] = total

    def fold(a, i, way, source):
        s = n - 1 - i if way > 0 else i
        k = 0 if way > 0 else 1
        src = part_shard(parts[a], s) if source else held[k].at[a, i]
        return remote(
            src, held[k].at[a, i], ls_sem.at[a, k, i], lr_sem.at[a, k, i], {"tensor": z + way}
        )

    def edge(way):
        return z == 0 if way > 0 else z == n - 1

    def sends(i, way):
        return n - 1 - i > z if way > 0 else i < z

    def settle(a):
        target = parts[a]

        @pl.loop(0, target.shape[0])
        def _(b):
            spot = tables[1 - a, 5, b]
            found = run[jnp.maximum(spot, 0)]
            target[b] = jnp.where(spot >= 0, found, jnp.zeros_like(found))

    def fold_start(a, i):
        for way in (1, -1):

            @pl.when(edge(way))
            def _():
                fold(a, i, way, True).start()

    def add_into(target, terms):
        @pl.loop(0, target.shape[0])
        def _(b):
            total = terms[0][b].astype(jnp.float32)
            for term_of in terms[1:]:
                total += term_of[b].astype(jnp.float32)
            target[b] = total.astype(target.dtype)

    def fold_event(a, t):
        for way in (1, -1):
            i = t - z if way > 0 else t - (n - 1 - z)
            s = n - 1 - i if way > 0 else i
            k = 0 if way > 0 else 1
            on_way = jnp.logical_and(i >= 0, sends(i, way))

            @pl.when(jnp.logical_and(on_way, jnp.logical_not(edge(way))))
            def _():
                fold(a, i, way, False).wait_recv()
                add_into(held[k].at[a, i], (held[k].at[a, i], part_shard(parts[a], s)))
                fold(a, i, way, False).start()

    def finish(a):
        mine = part_shard(parts[a], z)
        target = outs[a][0]

        def write(terms):
            for b in range(blocks):
                total = terms[0][b].astype(jnp.float32)
                for term_of in terms[1:]:
                    total += term_of[b].astype(jnp.float32)
                target[:, pl.ds(b * 128, 128)] = total.astype(target.dtype)

        @pl.when(z > 0)
        def _():
            fold(a, n - 1 - z, 1, False).wait_recv()

        @pl.when(z < n - 1)
        def _():
            fold(a, z, -1, False).wait_recv()

        @pl.when(z == 0)
        def _():
            write((mine, held_l.at[a, z]))

        @pl.when(z == n - 1)
        def _():
            write((mine, held_r.at[a, n - 1 - z]))

        @pl.when(jnp.logical_and(z > 0, z < n - 1))
        def _():
            write((mine, held_r.at[a, n - 1 - z], held_l.at[a, z]))

        out_copy(a).start()

    sums = (ga_d, ga_u)
    others = (gb_d, gb_u)

    def term(a, j):
        if a == 0:
            at, to = down_rows[j], down_cols[j]
            return mm(wide([ht_own[at], ht_mate[at]], 1), wide([cot_own[to], cot_mate[to]], 0), 1, 0)
        at, to = up_rows[j], up_cols[j]
        return mm(wide([xt_own[at], xt_mate[at]], 1), wide([pg_own[to], pg_mate[to]], 0), 1, 0)

    def first_tile(q, k):
        return (q * 2 + c) * per + k * size

    def x_copy(a, k, d):
        q = lax.rem(r + d, chips)
        at = pl.ds(k * size, size)
        return remote(
            stage.at[a, d - 1, at], x_in.at[a, d - 1, at], xs_sem.at[a, d - 1], xr_sem.at[a, k, d - 1],
            {"fsdp": q * 2 + c},
        )

    def hand_over(a, first_piece, end):
        @pl.loop(first_piece, end)
        def _(k):
            for d in range(1, chips):
                first = first_tile(lax.rem(r + d, chips), k)
                values = [term(a, first + i) for i in range(size)]
                for i in range(size):
                    stage[a, d - 1, k * size + i] = values[i].astype(jnp.bfloat16)
                x_copy(a, k, d).start()

    def done_piece(a, k):
        return x_in.at[a, 0, pl.ds(k * size, size)]

    def e_copy(a, k, e):
        return remote(
            done_piece(a, k), others[a].at[e - 1, pl.ds(k * size, size)],
            es_sem.at[a, e - 1], er_sem.at[a, e - 1], {"dp": lax.rem(y + e, replicas)},
        )

    def keep_copy(a, k):
        return pltpu.make_async_copy(
            done_piece(a, k), sums[a].at[pl.ds(k * size, size)], keep_sem.at[a]
        )

    def piece(k):
        return pl.ds(k * size, size)

    def x_out(d, where):
        return remote(
            stage.at[0, d - 1, where], relay_x.at[d - 1, where], rs_sem.at[d - 1], rr_sem.at[0, d - 1],
            {"fsdp": lax.rem(r + d, chips) * 2 + c, "tensor": inner},
        )

    def x_out_piece(k, d):
        return remote(
            stage.at[0, d - 1, piece(k)], relay_x.at[d - 1, piece(k)], rs_sem.at[d - 1], rr_sem.at[k, d - 1],
            {"fsdp": lax.rem(r + d, chips) * 2 + c, "tensor": inner},
        )

    def x_on(d, where, recv_sem):
        return remote(
            relay_x.at[d - 1, where], x_in.at[0, d - 1, where], fs_sem.at[d - 1], recv_sem, {"tensor": outer}
        )

    def y_out(e, where, recv_sem):
        return remote(
            x_in.at[0, 0, where], relay_y.at[e - 1, where], ts2_sem.at[e - 1], recv_sem,
            {"dp": lax.rem(y + e, replicas), "tensor": inner},
        )

    def y_on(e, where):
        return remote(
            relay_y.at[e - 1, where], others[0].at[e - 1, where], fs2_sem.at[e - 1], er_sem.at[0, e - 1],
            {"tensor": outer},
        )

    def hand_relays():
        for k in range(relays):
            for d in range(1, chips):
                first = first_tile(lax.rem(r + d, chips), k)
                values = [term(0, first + i) for i in range(size)]
                for i in range(size):
                    stage[0, d - 1, k * size + i] = values[i].astype(jnp.bfloat16)
                x_out_piece(k, d).start()

    def pass_x(k):
        @pl.when(helps)
        def _():
            for d in range(1, chips):
                x_out_piece(k, d).wait_recv()
                x_on(d, piece(k), xr_sem.at[0, k, d - 1]).start()

    def pass_y(k):
        @pl.when(helps)
        def _():
            for e in range(1, replicas):
                y_out(e, piece(k), tr2_sem.at[k, e - 1]).wait_recv()
                y_on(e, piece(k)).start()

    def relayed_event(k):
        x_event(0, k, True)

    def x_events(a, first_piece, end):
        pl.loop(first_piece, end)(functools.partial(x_event, a))

    def x_event(a, k, relayed=False):
        first = first_tile(r, k)
        values = [term(a, first + i) for i in range(size)]
        for d in range(1, chips):
            x_copy(a, k, d).wait_recv()
        for i in range(size):
            total = values[i]
            for d in range(1, chips):
                total += x_in[a, d - 1, k * size + i].astype(jnp.float32)
            x_in[a, 0, k * size + i] = total.astype(jnp.bfloat16)
        for e in range(1, replicas):
            if relayed:
                y_out(e, piece(k), tr2_sem.at[k, e - 1]).start()
            else:
                e_copy(a, k, e).start()
        keep_copy(a, k).start()

    def start_all():
        loads[0].wait()
        z_start(0)
        for a in range(2):
            for k in range(weight_chunks):
                for d in range(1, chips):
                    w_copy(a, d, k).start()
        for a in range(2):
            own_core(a).start()
        loads[1].wait()
        for k in range(CHUNKS):
            mate_chunk(0, k, 1).start()

    def table_copy(t):
        return pltpu.make_async_copy(made.at[t], tables.at[t], table_sem.at[t])

    def make_table(t):
        near, far = ((uc, ur), (dr, dc))[t]
        for row, values in enumerate(tables_of(near[...], far[...], n * blocks)):
            made[t, pl.ds(row, 1), pl.ds(0, values.shape[1])] = values
        table_copy(t).start()

    def table_ready(t):
        table_copy(t).wait()

    def cot_ready():
        mate_chunks().wait_recv()
        hidden_mates().wait_recv()

    def grads_ready():
        mate_turns().wait_recv()
        grad_mates().wait_recv()

    chunk_time = SHARD_TIME / CHUNKS
    piece_time = 4 * SHARD_TIME / pieces
    up_in = 2.3 + (weight_chunks + 1.2) * WEIGHT_TIME
    down_in = 2.3 + (2 * weight_chunks + 1.2) * WEIGHT_TIME
    group = max(pieces // 8, 1)
    end_cot_in = 4.0 + 2 * (n - 1) * SHARD_TIME
    end_inp_settle = end_cot_in + INP_LATE

    def order(ends):
        plan = []

        def at(time, work, *args):
            plan.append((time, functools.partial(work, *args)))

        at(0.0, start_all)
        for t in range(2):
            at(10.2 + 5.65 * t, make_table, t)
            at(24.0, table_ready, t)
        at(5.7, turn, 0, 1)
        hops = n - 1 if ends else max(n - 2, 1)
        for s in range(1, n):
            for k in range(CHUNKS):
                at(2.0 + ((s - 1) * CHUNKS + k + 1) * chunk_time, z_event, 0, s, k)
                at(2.0 + hops * SHARD_TIME + ((s - 1) * CHUNKS + k + 1) * chunk_time, z_event, 1, s, k)
            at(2.0 + s * SHARD_TIME + 0.1 + chunk_time, turn_event, s)
        at(2.05 + max(n - 2, 0) * SHARD_TIME, z_start, 1)
        for a in range(2):
            for k in range(weight_chunks):
                when = 2.2 + (a * weight_chunks + k + 1) * WEIGHT_TIME
                at(when, w_event, a, k)
                at(when + 1.2 * WEIGHT_TIME, y_event, a, k)
        at(up_in + 2.0, weights_in, 0)
        at(down_in + 2.0, weights_in, 1)
        hidden_from = max(2.0 + hops * SHARD_TIME, up_in + 2.0) + 0.5
        hidden_in = hidden_from + 3.0 * HIDDEN_PARTS
        for g in range(HIDDEN_PARTS):
            at(hidden_from + 3.0 * g, hidden_part, g)
        out_from = max(hidden_in, down_in + 2.0) + 0.5
        out_settle = out_from + 2.4 * HIDDEN_PARTS
        for g in range(HIDDEN_PARTS):
            at(out_from + 2.4 * g, run_part, 0, g)
        at(out_settle, settle, 0)
        cot_in = 2.0 + 2 * hops * SHARD_TIME + 1.0
        cot_in = max(cot_in, out_settle if ends else hidden_in) + 1.0
        away = relays if ends else 0
        at(cot_in, cot_ready)
        if away:
            at(cot_in + 0.05, hand_relays)
        for j, k in enumerate(range(away, pieces, group)):
            at(cot_in + 0.1 + 1.2 * j, hand_over, 0, k, min(k + group, pieces))
        slope_from = max(cot_in + 9.0, out_settle + 0.5)
        for g in range(PARTS):
            at(slope_from + 1.5 * g, slope_part, g)
        up_from = slope_from + 1.5 * PARTS + 1.0
        at(up_from, grads_ready)
        first_groups = 3 if ends else 8
        inp_from = up_from + 0.1 + 1.4 * first_groups
        for j, k in enumerate(range(0, pieces, group)):
            late = 0.0 if j < first_groups else 0.7
            at(up_from + 0.1 + 1.4 * j + late, hand_over, 1, k, min(k + group, pieces))
        for g in range(PARTS):
            at(inp_from + 1.5 * g, run_part, 1, g)
        inp_settle = inp_from + 1.5 * PARTS + (3.0 if ends else 0.0)
        at(inp_settle, settle, 1)
        late = end_cot_in + FOLD_LATE
        for i in range(n - 1):
            at(max(out_settle, late if i and relays else 0.0) + 0.1, fold_start, 0, i)
            at(max(inp_settle, end_cot_in + INP_REST if i and relays else 0.0) + 0.1, fold_start, 1, i)
        for t in range(1, n - 1):
            begin = max(out_settle, late + 4.0 if t > 1 and relays else 0.0)
            at(begin + 1.0 + t * SHARD_TIME, fold_event, 0, t)
            at(end_inp_settle + 1.0 + t * SHARD_TIME + (8.0 if t > 1 else 0.0), fold_event, 1, t)
        at(late + 20.0 + (n - 1) * SHARD_TIME, finish, 0)
        at(FINISH + end_inp_settle + 3.0 + (n - 1) * SHARD_TIME, finish, 1)
        for k in range(relays):
            if ends:
                at(end_cot_in + RELAYED + piece_time * (k + 1), relayed_event, k)
            else:
                at(end_cot_in + PASS_X + piece_time * (k + 1), pass_x, k)
                at(end_cot_in + PASS_Y + piece_time * (k + 1), pass_y, k)
        for a in range(2):
            for k in range(0 if a else away, pieces):
                when = cot_in + 2.2 + piece_time * (a * pieces + k - away + 1)
                at(max(when, up_from + 0.2) if a else when, x_event, a, k)
        plan.sort(key=lambda item: item[0])
        steps = []
        for _, work in plan:
            if work.func is x_event:
                a, k = work.args
                if steps and steps[-1].func is x_events and steps[-1].args[::2] == (a, k):
                    work = functools.partial(x_events, a, steps.pop().args[1], k + 1)
                else:
                    work = functools.partial(x_events, a, k, k + 1)
            steps.append(work)
        return steps

    def run_all(steps):
        for work in steps:
            work()

    end_steps, mid_steps = order(True), order(False)
    if relays:
        shared = 0
        for one, other in zip(end_steps, mid_steps):
            if (one.func, one.args) != (other.func, other.args):
                break
            shared += 1
        run_all(end_steps[:shared])
        pl.when(at_end)(functools.partial(run_all, end_steps[shared:]))
        pl.when(jnp.logical_not(at_end))(functools.partial(run_all, mid_steps[shared:]))
    else:
        run_all(end_steps)

    mate_chunks().wait_send()
    mate_turns().wait_send()
    for a in range(2):
        out_copy(a).wait()
        weights_sent(a)
        for way in (1, -1):
            for s in range(n - 1):

                @pl.when(jnp.logical_and(can_send(way), has(s, way)))
                def _():
                    line_sent(a, s, way)

        for i in range(n - 1):
            for way in (1, -1):

                @pl.when(sends(i, way))
                def _():
                    fold(a, i, way, False).wait_send()

    hidden_mates().wait_send()
    grad_mates().wait_send()
    def sent(a, first):
        where = pl.ds(first * size, per - first * size)
        for d in range(1, chips):
            remote(
                stage.at[a, d - 1, where], x_in.at[a, d - 1, where], xs_sem.at[a, d - 1], xr_sem.at[a, 0, d - 1],
                {"fsdp": lax.rem(r + d, chips) * 2 + c},
            ).wait_send()
        for e in range(1, replicas):
            remote(
                x_in.at[a, 0, where], others[a].at[e - 1, where], es_sem.at[a, e - 1], er_sem.at[a, e - 1],
                {"dp": lax.rem(y + e, replicas)},
            ).wait_send()

    for a in range(2):
        pltpu.make_async_copy(x_in.at[a, 0], sums[a], keep_sem.at[a]).wait()
        for e in range(1, replicas):
            remote(
                x_in.at[a, 0], others[a].at[e - 1], es_sem.at[a, e - 1], er_sem.at[a, e - 1],
                {"dp": lax.rem(y + e, replicas)},
            ).wait_recv()
    sent(1, 0)
    if not relays:
        sent(0, 0)
    else:
        relayed = pl.ds(0, relays * size)

        @pl.when(at_end)
        def _():
            sent(0, relays)
            for d in range(1, chips):
                x_out(d, relayed).wait_send()
            for e in range(1, replicas):
                y_out(e, relayed, tr2_sem.at[0, e - 1]).wait_send()

        @pl.when(jnp.logical_not(at_end))
        def _():
            sent(0, 0)

        @pl.when(helps)
        def _():
            for d in range(1, chips):
                x_on(d, relayed, xr_sem.at[0, 0, d - 1]).wait_send()
            for e in range(1, replicas):
                y_on(e, relayed).wait_send()


def run_block(sizes, lists, activations, cotangent, up_tiles, down_tiles):
    n, chips, replicas = sizes
    rows, features = activations.shape
    blocks = features // 128
    per = up_tiles.shape[0]
    total_tiles = 2 * chips * per
    hidden_blocks = total_tiles // COL_TILES
    model_blocks = n * blocks
    pairs = (total_tiles + model_blocks) // 2
    part = per // replicas
    weight_chunks = min(WEIGHT_CHUNKS, part)
    pieces = min(PIECES, per)
    relays = max(relay_pieces(n, pieces), 1)
    relayed = relays * per // pieces
    kind = jnp.bfloat16
    dma = pltpu.SemaphoreType.DMA
    vmem = pl.BlockSpec(memory_space=pltpu.VMEM)
    smem = pl.BlockSpec(memory_space=pltpu.SMEM)
    anywhere = pl.BlockSpec(memory_space=pl.ANY)

    def held(*shape):
        return pltpu.VMEM(shape + (rows, 128), kind)

    def twice(*shape):
        return [dma(shape), dma(shape)]

    return pl.pallas_call(
        functools.partial(block_kernel, sizes),
        out_shape=(
            [jax.ShapeDtypeStruct((rows, features), kind)] * 2
            + [jax.ShapeDtypeStruct((per, 128, 128), kind)] * 2
            + [jax.ShapeDtypeStruct((replicas - 1, per, 128, 128), kind)] * 2
        ),
        in_specs=[smem] * 4 + [vmem] * 4 + [anywhere] * 4,
        out_specs=[anywhere] * 6,
        scratch_shapes=[
            held(model_blocks),
            pltpu.VMEM((rows, features), kind),
            pltpu.VMEM((rows, features), kind),
            pltpu.VMEM((model_blocks, 128, rows), kind),
            pltpu.VMEM((model_blocks, 128, rows), kind),
            held(model_blocks),
            held(model_blocks),
            pltpu.VMEM((total_tiles, 128, 128), kind),
            pltpu.VMEM((total_tiles, 128, 128), kind),
            held(hidden_blocks + 1),
            pltpu.VMEM((hidden_blocks, 128, rows), kind),
            pltpu.VMEM((hidden_blocks, 128, rows), kind),
            pltpu.VMEM((hidden_blocks, rows, 128), jnp.float32),
            held(hidden_blocks + 1),
            held(hidden_blocks),
            held(pairs),
            pltpu.VMEM((rows, 128), jnp.float32),
            held(model_blocks),
            held(model_blocks),
            held(2, n - 1, blocks),
            held(2, n - 1, blocks),
            pltpu.VMEM((2, chips - 1, per, 128, 128), kind),
            pltpu.VMEM((2, chips - 1, per, 128, 128), kind),
            pltpu.VMEM((chips - 1, relayed, 128, 128), kind),
            pltpu.VMEM((replicas - 1, relayed, 128, 128), kind),
            pltpu.VMEM((2, 8, padded(total_tiles + model_blocks)), jnp.int32),
            pltpu.SMEM((2, 8, padded(total_tiles + model_blocks)), jnp.int32),
            dma((4,)),
            dma((2, 2, n - 1)),
            dma((2, 2, n - 1, CHUNKS)),
            *twice(1),
            *twice(1),
            dma((2, chips - 1)),
            dma((2, chips - 1, weight_chunks)),
            dma((2, chips - 1, replicas - 1)),
            dma((2, chips - 1, replicas - 1, weight_chunks)),
            *twice(2),
            *twice(1),
            *twice(1),
            *twice(2, 2, n - 1),
            dma((2, chips - 1)),
            dma((2, pieces, chips - 1)),
            *twice(2, replicas - 1),
            dma((2,)),
            dma((2,)),
            dma((2,)),
            dma((chips - 1,)),
            dma((relays, chips - 1)),
            dma((chips - 1,)),
            dma((replicas - 1,)),
            dma((relays, replicas - 1)),
            dma((replicas - 1,)),
        ],
        compiler_params=pltpu.CompilerParams(
            collective_id=0, has_side_effects=True, vmem_limit_bytes=67043328
        ),
        name="block_all",
    )(*(v[:, 0] for v in lists), *(v.T for v in lists), activations, cotangent, up_tiles, down_tiles)


def total_kernel(ga_u, gb_u, ga_d, gb_d, out_in, inp_in, up_grad, down_grad, out, inp):
    for one, more, target in ((ga_u, gb_u, up_grad), (ga_d, gb_d, down_grad)):
        total = one[...].astype(jnp.float32)
        for e in range(more.shape[0]):
            total += more[e].astype(jnp.float32)
        target[...] = total
    out[...] = out_in[...]
    inp[...] = inp_in[...]


def totals(ga_u, gb_u, ga_d, gb_d, out, inp):
    per = ga_u.shape[0]
    step = max(per // 2, 1)
    rows, features = out.shape
    one = pl.BlockSpec((step, 128, 128), lambda i: (i, 0, 0))
    more = pl.BlockSpec((gb_u.shape[0], step, 128, 128), lambda i: (0, i, 0, 0))
    flat = pl.BlockSpec((rows * step // per, features), lambda i: (i, 0))
    return pl.pallas_call(
        total_kernel,
        grid=(per // step,),
        out_shape=(
            [jax.ShapeDtypeStruct(ga_u.shape, jnp.float32)] * 2 + [jax.ShapeDtypeStruct(out.shape, out.dtype)] * 2
        ),
        in_specs=[one, more, one, more, flat, flat],
        out_specs=[one, one, flat, flat],
        name="totals",
    )(ga_u, gb_u, ga_d, gb_d, out, inp)


def body(sizes, activations, cotangent, up_tiles, down_tiles, up_rows, up_cols, down_rows, down_cols):
    lists = (up_rows, up_cols, down_rows, down_cols)
    out, inp, ga_u, ga_d, gb_u, gb_d = run_block(
        sizes, lists, activations, cotangent, up_tiles, down_tiles
    )
    up_grad, down_grad, out, inp = totals(ga_u, gb_u, ga_d, gb_d, out, inp)
    return out, inp, up_grad, down_grad


def solution(mesh):
    sizes = (mesh.shape["tensor"], mesh.shape["fsdp"] // 2, mesh.shape["dp"])
    in_specs = (
        P(("dp", "fsdp"), "tensor"),
        P(("dp", "fsdp"), "tensor"),
        P(("fsdp", "tensor"), None, None),
        P(("fsdp", "tensor"), None, None),
        P(None, "tensor"),
        P(None, "tensor"),
        P(None, "tensor"),
        P(None, "tensor"),
    )
    out_specs = (
        P(("dp", "fsdp"), "tensor"),
        P(("dp", "fsdp"), "tensor"),
        P(("fsdp", "tensor"), None, None),
        P(("fsdp", "tensor"), None, None),
    )
    return jax.shard_map(
        functools.partial(body, sizes), mesh=mesh, in_specs=in_specs, out_specs=out_specs,
        check_vma=False,
    )
```
